128 devices in a mesh: gx: 8 (over x, core), gy: 16 (over z, y).
Axes of the slice: x: 4, y: 4, z: 4, core: 2. Of those that a mesh axis runs over, the one named last changes fastest.
Arguments:
- features: bfloat16 [32, 64, 64, 128], P('gx', 'gy'), may hold values from -6 to 6
- skip_grad: bfloat16 [32, 64, 64, 128], P('gx', 'gy'), may hold values from -1.5 to 1.5
- bottom_grad: bfloat16 [16, 32, 32, 256], P('gx', 'gy'), may hold values from -6 to 6
- conv_one: bfloat16 [3, 3, 3, 128, 128], replicated, may hold values from -0.109375 to 0.109375
- conv_two: bfloat16 [3, 3, 3, 128, 128], replicated, may hold values from -0.109375 to 0.109375
- conv_three: bfloat16 [3, 3, 3, 128, 256], P(None, None, None, None, 'gy'), may hold values from -0.109375 to 0.109375
Outputs:
- bottleneck: bfloat16 [16, 32, 32, 256], P('gx', 'gy')
- input_grad: bfloat16 [32, 64, 64, 128], P('gx', 'gy')
- grad_one: float32 [3, 3, 3, 128, 128], replicated
- grad_two: float32 [3, 3, 3, 128, 128], replicated
- grad_three: float32 [3, 3, 3, 128, 256], P(None, None, None, None, 'gy')
The draws below stay inside these ranges and needn't reach their ends.
All inputs are finite; a program needn't handle non-finite values.
Results may differ from the reference program's by a relative error of at most 0.018.
Values may be sent and summed in bfloat16 or wider, within the bound.
No kernel may reach another device: no remote copies, remote signals or barrier semaphores. Data moves between devices by JAX's collectives and lax.ppermute only.
A program may use at most 128 MiB of HBM per device.

```python
import math
import jax
import jax.numpy as jnp
from jax import lax

C1 = 128
C2 = 256
NX = 32
NY = 64
NZ = 64


def block_levels(rng, shape, shards, least, high):
    loudness, own = 1.0, jax.random.fold_in(rng, 6)
    for axis_at, shards_of in shards:
        draws = jnp.exp(jax.random.uniform(jax.random.fold_in(own, axis_at), (shards_of,), jnp.float32, least / len(shards), high / len(shards)))
        loudness = loudness * jnp.repeat(draws, shape[axis_at] // shards_of).reshape([-1 if axis == axis_at else 1 for axis in range(len(shape))])
    return loudness


def noise(own_key, extent, deviation, most, split=(), dtype=jnp.bfloat16):
    factor_of = block_levels(own_key, extent, split, -0.22, 0.18) if split else 1.0
    values = jax.random.normal(own_key, extent, jnp.float32) * deviation * factor_of
    return jnp.minimum(jnp.maximum(values, -most), most).astype(dtype)


def setup_inputs(seed: int = 0) -> dict:
    key_of = jax.random.split(jax.random.key(seed), 7)
    features = noise(key_of[0], (NX, NY, NZ, C1), 1.0, 6.0, ((0, 8), (1, 16)))
    skip_grad = noise(key_of[1], (NX, NY, NZ, C1), 0.25, 1.5, ((0, 8), (1, 16)))
    bottom_grad = noise(key_of[2], (NX // 2, NY // 2, NZ // 2, C2), 1.0, 6.0, ((0, 8), (1, 16)))
    conv_one = noise(key_of[3], (3, 3, 3, C1, C1), (27 * C1) ** -0.5, 0.109375)
    conv_two = noise(key_of[4], (3, 3, 3, C1, C1), (27 * C1) ** -0.5, 0.109375)
    conv_three = noise(key_of[5], (3, 3, 3, C1, C2), (27 * C1) ** -0.5, 0.109375, ((4, 16),))
    return dict(features=features, skip_grad=skip_grad, bottom_grad=bottom_grad, conv_one=conv_one, conv_two=conv_two, conv_three=conv_three)


def periodic_conv(field, taps):
    padded = jnp.pad(field, ((1, 1), (1, 1), (1, 1), (0, 0)), mode='wrap')
    result = lax.conv_general_dilated(padded[None], taps, (1, 1, 1), 'VALID', dimension_numbers=('NDHWC', 'DHWIO', 'NDHWC'), precision=lax.Precision.HIGHEST)
    return result[0]

def silu_slope(values):
    sigma = jax.nn.sigmoid(values)
    return sigma * (1.0 + values * (1.0 - sigma))

def pool_blocks(field):
    size_x, size_y, size_z, chans = field.shape
    blocks = field.astype(jnp.float32).reshape(size_x // 2, 2, size_y // 2, 2, size_z // 2, 2, chans)
    return lax.optimization_barrier(jnp.mean(blocks, axis=(1, 3, 5))).astype(jnp.bfloat16)

def spread_blocks(field):
    size_x, size_y, size_z, chans = field.shape
    wide = jnp.broadcast_to(field[:, None, :, None, :, None, :], (size_x, 2, size_y, 2, size_z, 2, chans))
    return wide.reshape(size_x * 2, size_y * 2, size_z * 2, chans)

def reference(features, skip_grad, bottom_grad, conv_one, conv_two, conv_three):
    pre_one, pull_one = jax.vjp(periodic_conv, features.astype(jnp.float32), conv_one.astype(jnp.float32))
    act_one = jax.nn.silu(pre_one).astype(jnp.bfloat16)
    pre_two, pull_two = jax.vjp(periodic_conv, act_one.astype(jnp.float32), conv_two.astype(jnp.float32))
    act_two = jax.nn.silu(pre_two).astype(jnp.bfloat16)
    pooled = pool_blocks(act_two)
    pre_three, pull_three = jax.vjp(periodic_conv, pooled.astype(jnp.float32), conv_three.astype(jnp.float32))
    bottleneck = jax.nn.silu(pre_three).astype(jnp.bfloat16)
    err_three = (bottom_grad.astype(jnp.float32) * silu_slope(pre_three)).astype(jnp.bfloat16)
    pooled_back, raw_three = pull_three(err_three.astype(jnp.float32))
    err_two = ((skip_grad.astype(jnp.float32) + spread_blocks(pooled_back) * 0.125) * silu_slope(pre_two)).astype(jnp.bfloat16)
    back_one, raw_two = pull_two(err_two.astype(jnp.float32))
    err_one = (back_one * silu_slope(pre_one)).astype(jnp.bfloat16)
    back_input, raw_one = pull_one(err_one.astype(jnp.float32))
    fine_cells = features.shape[0] * features.shape[1] * features.shape[2]
    fine_scale = 1.0 / math.sqrt(fine_cells)
    coarse_scale = 1.0 / math.sqrt(fine_cells // 8)
    return (bottleneck, back_input.astype(jnp.bfloat16), raw_one * fine_scale, raw_two * fine_scale, raw_three * coarse_scale)
```

```python
import math

import jax
import jax.numpy as jnp
from jax import lax
from jax.experimental import pallas as pl
from jax.experimental.pallas import tpu as pltpu
from jax.sharding import Mesh
from jax.sharding import PartitionSpec as P

GX = ("x", "c")
GY = ("z", "y")
FLAT = ("x", "z", "y")
F32 = jnp.float32
BF16 = jnp.bfloat16
UNITS = 7


def shifted(array, axes, step):
    count = lax.axis_size(axes)
    return lax.ppermute(array, axes, [(i, (i + step) % count) for i in range(count)])


def swap_cores(array):
    return lax.ppermute(array, "c", [(0, 1), (1, 0)])


def halo_pieces(own, width):
    before = shifted(own[:, -width:], GY, 1)
    after = shifted(own[:, :width], GY, -1)
    low = jnp.concatenate([before[:width], own[:width], after[:width]], axis=1)
    high = jnp.concatenate([before[-width:], own[-width:], after[-width:]], axis=1)
    left = shifted(high, GX, 1)
    right = shifted(low, GX, -1)
    return own, before, after, left, right


def fill_padded(padded, own, before, after, left, right):
    size_x, size_y = own.shape[0], own.shape[1]
    width = left.shape[0]
    padded[0:width] = left[...]
    padded[width + size_x : 2 * width + size_x] = right[...]
    middle = slice(width, width + size_x)
    padded[middle, 0:width] = before[...]
    padded[middle, width : width + size_y] = own[...]
    padded[middle, width + size_y : 2 * width + size_y] = after[...]


def slope_and_silu(values):
    sigma = 1.0 / (1.0 + jnp.exp(-values))
    return values * sigma, sigma * (1.0 + values * (1.0 - sigma))


def window_rows(source, row, count, skip=0):
    pieces = []
    for kx in range(3):
        for ky in range(3):
            block = source[row + kx + skip, ky + skip : ky + skip + count]
            pieces.append(block.reshape(block.shape[0] * block.shape[1], block.shape[2]))
    return jnp.concatenate(pieces, axis=1)


def roll_z(values, step):
    return pltpu.roll(values, step % values.shape[1], 1)


def join_taps(product, count, size_z, chans):
    parts = product.reshape(count, size_z, 3 * chans)
    return (
        roll_z(parts[:, :, 0:chans], 1)
        + parts[:, :, chans : 2 * chans]
        + roll_z(parts[:, :, 2 * chans : 3 * chans], -1)
    )


def spread_errors(errors):
    count, size_z, chans = errors.shape
    parts = [roll_z(errors, -1), errors, roll_z(errors, 1)]
    return jnp.concatenate([p.reshape(count * size_z, chans) for p in parts], axis=1).astype(BF16)


def fill_forward(packed, taps):
    for kx in range(3):
        for ky in range(3):
            for kz in range(3):
                at = kx * 3 + ky
                packed[at * 128 : at * 128 + 128, kz * 128 : kz * 128 + 128] = taps[at * 3 + kz]


def fill_backward(packed, taps):
    for kx in range(3):
        for ky in range(3):
            for kz in range(3):
                at = kx * 3 + ky
                packed[kz * 128 : kz * 128 + 128, at * 128 : at * 128 + 128] = taps[26 - at * 3 - kz]


def dot_nn(left, right):
    return lax.dot_general(left, right, (((1,), (0,)), ((), ())), preferred_element_type=F32)


def dot_nt(left, right):
    return lax.dot_general(left, right, (((1,), (1,)), ((), ())), preferred_element_type=F32)


def dot_tn(left, right):
    return lax.dot_general(left, right, (((0,), (0,)), ((), ())), preferred_element_type=F32)


def forward_kernel(own, before, after, left, right, taps_one, taps_two,
                   act_one, slope_one, slope_two, pooled, padded, packed, halves):
    fill_padded(padded, own, before, after, left, right)
    fill_forward(packed, taps_one)

    def first(row, _):
        product = dot_nn(window_rows(padded, row, 6), packed[...])
        act, slope = slope_and_silu(join_taps(product, 6, 64, 128))
        act_one[row] = act.astype(BF16)
        slope_one[row] = slope
        return 0

    lax.fori_loop(0, 6, first, 0)
    fill_forward(packed, taps_two)

    def second(row, _):
        product = dot_nn(window_rows(act_one, row, 4), packed[...])
        act, slope = slope_and_silu(join_taps(product, 4, 64, 128))
        slope_two[row] = slope
        act = act.astype(BF16).astype(F32)
        halves[row] = act.reshape(2, 2, 64, 128).sum(axis=1)
        return 0

    lax.fori_loop(0, 4, second, 0)
    for at_x in range(2):
        for at_y in range(2):
            total = 0.0
            for part in range(2):
                for start in range(2):
                    total = total + halves[2 * at_x + part, at_y, pl.ds(start, 32, stride=2), :]
            pooled[at_x, at_y] = (total * 0.125).astype(BF16)


def bottom_kernel(own, before, after, left, right, g_own, g_before, g_after, g_left, g_right,
                  taps_three, slope_two, skip, bottleneck, err_three, err_two,
                  padded, grads, packed, errors, wide):
    fill_padded(padded, own, before, after, left, right)
    fill_padded(grads, g_own, g_before, g_after, g_left, g_right)
    for at in range(9):
        for kz in range(3):
            packed[kz * 256 : kz * 256 + 256, at * 128 : at * 128 + 128] = taps_three[at * 3 + kz]
    for row in range(4):
        product = dot_nt(window_rows(padded, row, 4), packed[...])
        act, slope = slope_and_silu(join_taps(product, 4, 32, 256))
        if row in (1, 2):
            bottleneck[row - 1] = act[1:3].astype(BF16)
        errs = (grads[row].astype(F32) * slope).astype(BF16)
        errors[row] = errs
        if row in (1, 2):
            err_three[row - 1] = errs[1:3]
    for row in range(2):
        total = jnp.zeros((64, 384), F32)
        for kx in range(3):
            for ky in range(3):
                block = errors[row + kx, ky : ky + 2].reshape(64, 256)
                at = kx * 3 + ky
                back = jnp.concatenate(
                    [taps_three[26 - at * 3 - kz] for kz in range(3)], axis=1
                )
                total = total + dot_nn(block, back)
        upward = join_taps(total, 2, 32, 128) * 0.125
        for at_y in range(2):
            wide[pl.ds(0, 32, stride=2), :] = upward[at_y]
            wide[pl.ds(1, 32, stride=2), :] = upward[at_y]
            for dx in range(2):
                for dy in range(2):
                    at = (2 * row + dx, 2 * at_y + dy)
                    err_two[at] = (
                        (skip[at].astype(F32) + wide[...]) * slope_two[at]
                    ).astype(BF16)


def add_tap_grads(total, fields, skip, error_rows):
    total[...] = jnp.zeros_like(total)

    def step(row, _):
        total[...] += dot_tn(
            window_rows(fields, row, 4, skip), spread_errors(error_rows(row).astype(F32))
        )
        return 0

    lax.fori_loop(0, 4, step, 0)


def store_tap_grads(out, total):
    for at in range(9):
        for kz in range(3):
            rows = (at * 3 + kz) * 128
            out[rows : rows + 128] = total[
                at * 128 : at * 128 + 128, kz * 128 : kz * 128 + 128
            ].astype(BF16)
    out[3456:3584] = jnp.zeros((128, 128), BF16)


def middle_grads_kernel(act_one, err_two, out, total):
    add_tap_grads(total, act_one, 0, lambda row: err_two[row])
    store_tap_grads(out, total)


def bottom_grads_kernel(own, before, after, left, right, err_three, out, padded, total):
    fill_padded(padded, own, before, after, left, right)
    for row in range(2):
        term = dot_tn(
            spread_errors(err_three[row].astype(F32)), window_rows(padded, row, 2, 1)
        )
        if row == 0:
            total[...] = term
        else:
            total[...] += term
    for unit in range(28):
        at_x, at_t = unit // UNITS, unit % UNITS
        if unit == 27:
            out[:, at_x * 16 : at_x * 16 + 16, at_t] = jnp.zeros((2, 16, 8, 128), BF16)
            continue
        at, kz = unit // 3, unit % 3
        block = total[kz * 256 : kz * 256 + 256, at * 128 : at * 128 + 128]
        block = block.reshape(16, 2, 8, 128)
        for half in range(2):
            out[half, at_x * 16 : at_x * 16 + 16, at_t] = block[:, half].astype(BF16)


def first_errors_kernel(own, before, after, left, right, taps_two, slope_one,
                        f_own, f_before, f_after, f_left, f_right, err_one, out,
                        padded, packed, total):
    fill_padded(padded, own, before, after, left, right)
    fill_backward(packed, taps_two)

    def step(row, _):
        product = dot_nt(window_rows(padded, row, 6), packed[...])
        back = join_taps(product, 6, 64, 128)
        err_one[row] = (back * slope_one[row]).astype(BF16)
        return 0

    lax.fori_loop(0, 6, step, 0)
    fill_padded(padded, f_own, f_before, f_after, f_left, f_right)
    add_tap_grads(total, padded, 1, lambda row: err_one[row + 1, 1:5])
    store_tap_grads(out, total)


def input_kernel(err_one, taps_one, out, packed):
    fill_backward(packed, taps_one)

    def step(row, _):
        product = dot_nt(window_rows(err_one, row, 4), packed[...])
        out[row] = join_taps(product, 4, 64, 128).astype(BF16)
        return 0

    lax.fori_loop(0, 4, step, 0)


def call(kernel, out_shapes, scratch, flops, *operands):
    shapes = [jax.ShapeDtypeStruct(s, d) for s, d in out_shapes]
    moved = sum(o.size * o.dtype.itemsize for o in operands)
    return pl.pallas_call(
        kernel,
        out_shape=shapes,
        in_specs=[pl.BlockSpec(memory_space=pltpu.VMEM)] * len(operands),
        out_specs=[pl.BlockSpec(memory_space=pltpu.VMEM)] * len(shapes),
        scratch_shapes=[pltpu.VMEM(s, d) for s, d in scratch],
        compiler_params=pltpu.CompilerParams(vmem_limit_bytes=48 << 20),
        cost_estimate=pl.CostEstimate(flops=flops, bytes_accessed=moved, transcendentals=0),
        name=kernel.__name__,
    )(*operands)


def pick(stacked, index):
    return lax.dynamic_index_in_dim(stacked, index, 0, keepdims=False)


def summed_pieces(pieces):
    arrived = lax.all_to_all(pieces, FLAT, 0, 0)
    return jnp.sum(arrived.astype(F32), axis=0).astype(BF16)


def on_device(features, skip_grad, bottom_grad, conv_one, conv_two, conv_three):
    core = lax.axis_index("c")
    fine_cells = features.size // 128 * lax.axis_size(GX) * lax.axis_size(GY)
    fine_scale = 1.0 / math.sqrt(fine_cells)
    coarse_scale = 1.0 / math.sqrt(fine_cells // 8)
    taps_one = conv_one.reshape(27, 128, 128)
    taps_two = conv_two.reshape(27, 128, 128)

    f_pieces = halo_pieces(features, 2)

    own_taps = jnp.swapaxes(conv_three.reshape(27, 128, 16), 1, 2)
    half_taps = pick(jnp.swapaxes(own_taps.reshape(27, 2, 8, 128), 0, 1), core)
    mine = lax.all_gather(half_taps, GY)
    theirs = swap_cores(mine)
    both = jnp.where(core == 0, jnp.stack([mine, theirs]), jnp.stack([theirs, mine]))
    taps_three = jnp.transpose(both, (2, 1, 0, 3, 4)).reshape(27, 256, 128)

    g_pieces = halo_pieces(bottom_grad, 1)

    conv_flops = 2 * 1152 * 128 * 1024 * 3
    act_one, slope_one, slope_two, pooled = call(
        forward_kernel,
        [((6, 6, 64, 128), BF16), ((6, 6, 64, 128), F32), ((4, 4, 64, 128), F32), ((2, 2, 32, 128), BF16)],
        [((8, 8, 64, 128), BF16), ((1152, 384), BF16), ((4, 2, 64, 128), F32)],
        3 * conv_flops, *f_pieces, taps_one, taps_two,
    )
    p_pieces = halo_pieces(pooled, 2)
    bottleneck, err_three, err_two = call(
        bottom_kernel,
        [((2, 2, 32, 256), BF16), ((2, 2, 32, 256), BF16), ((4, 4, 64, 128), BF16)],
        [((6, 6, 32, 128), BF16), ((4, 4, 32, 256), BF16), ((768, 1152), BF16),
         ((4, 4, 32, 256), BF16), ((64, 128), F32)],
        conv_flops, *p_pieces, *g_pieces, taps_three, slope_two, skip_grad,
    )
    e_pieces = halo_pieces(err_two, 2)

    (three,) = call(
        bottom_grads_kernel, [((2, 64, UNITS, 8, 128), BF16)],
        [((6, 6, 32, 128), BF16), ((768, 1152), F32)],
        conv_flops // 4, *p_pieces, err_three,
    )
    (two,) = call(
        middle_grads_kernel, [((3584, 128), BF16)], [((1152, 384), F32)],
        conv_flops, act_one, err_two,
    )
    kept = pick(three, core).astype(F32) + swap_cores(pick(three, 1 - core)).astype(F32)
    three_part = summed_pieces(kept.astype(BF16))

    err_one, one = call(
        first_errors_kernel, [((6, 6, 64, 128), BF16), ((3584, 128), BF16)],
        [((8, 8, 64, 128), BF16), ((384, 1152), BF16), ((1152, 384), F32)],
        3 * conv_flops, *e_pieces, taps_two, slope_one, *f_pieces,
    )
    sent = jnp.where(core == 0, two, one)
    kept = jnp.where(core == 0, one, two).astype(F32) + swap_cores(sent).astype(F32)
    part = summed_pieces(kept.astype(BF16).reshape(64, UNITS, 8, 128))
    whole = lax.all_to_all(jnp.broadcast_to(part, (64, UNITS, 8, 128)), FLAT, 0, 0)
    (input_grad,) = call(
        input_kernel, [((4, 4, 64, 128), BF16)], [((384, 1152), BF16)],
        conv_flops, err_one, taps_one,
    )
    whole = whole.reshape(3584, 128)[:3456].reshape(3, 3, 3, 128, 128)
    other = swap_cores(whole)
    grad_one = jnp.where(core == 0, whole, other).astype(F32) * fine_scale
    grad_two = jnp.where(core == 0, other, whole).astype(F32) * fine_scale

    three_all = lax.all_to_all(jnp.broadcast_to(three_part, (8, UNITS, 8, 128)), GX, 0, 0)
    three_all = three_all.reshape(4, 2, UNITS, 8, 128).transpose(0, 2, 1, 3, 4)
    three_all = three_all.reshape(28, 16, 128)[:27].astype(F32) * coarse_scale
    grad_three = jnp.swapaxes(three_all, 1, 2).reshape(3, 3, 3, 128, 16)
    return (bottleneck, input_grad, grad_one, grad_two, grad_three)


def solution(mesh):
    fine = Mesh(mesh.devices.reshape(4, 2, 4, 4), ("x", "c", "z", "y"))
    cells = P(GX, GY, None, None)
    outs = P(None, None, None, None, GY)
    return jax.shard_map(
        on_device,
        mesh=fine,
        in_specs=(cells, cells, cells, P(), P(), outs),
        out_specs=(cells, cells, P(), P(), outs),
        check_vma=False,
    )
```

```python
import functools
import math

import jax
import jax.numpy as jnp
from jax import lax
from jax.experimental import pallas as pl
from jax.experimental.pallas import tpu as pltpu
from jax.sharding import Mesh
from jax.sharding import PartitionSpec as P

GX = ("x", "c")
GY = ("z", "y")
FLAT = ("x", "z", "y")
F32 = jnp.float32
BF16 = jnp.bfloat16
PIECE = 56


def shifted(array, axes, step):
    count = lax.axis_size(axes)
    return lax.ppermute(array, axes, [(i, (i + step) % count) for i in range(count)])


def swap_cores(array):
    return lax.ppermute(array, "c", [(0, 1), (1, 0)])


def halo_pieces(own, width):
    before = shifted(own[:, -width:], GY, 1)
    after = shifted(own[:, :width], GY, -1)
    low = jnp.concatenate([before[:width], own[:width], after[:width]], axis=1)
    high = jnp.concatenate([before[-width:], own[-width:], after[-width:]], axis=1)
    left = shifted(high, GX, 1)
    right = shifted(low, GX, -1)
    return (own, before, after, left, right)


def fill_padded(padded, own, before, after, left, right):
    size_x, size_y = own.shape[0], own.shape[1]
    width = left.shape[0]
    padded[0:width] = left[...]
    padded[width + size_x : 2 * width + size_x] = right[...]
    middle = slice(width, width + size_x)
    padded[middle, 0:width] = before[...]
    padded[middle, width : width + size_y] = own[...]
    padded[middle, width + size_y : 2 * width + size_y] = after[...]


def slope_and_silu(values):
    sigma = 1.0 / (1.0 + jnp.exp(-values))
    return values * sigma, sigma * (1.0 + values * (1.0 - sigma))


def window_rows(source, row, count, skip=0):
    pieces = []
    for kx in range(3):
        for ky in range(3):
            block = source[row + kx + skip, ky + skip : ky + skip + count]
            pieces.append(block.reshape(block.shape[0] * block.shape[1], block.shape[2]))
    return jnp.concatenate(pieces, axis=1)


def roll_z(values, step):
    return pltpu.roll(values, step % values.shape[1], 1)


def join_taps(product, count, size_z, chans):
    parts = product.reshape(count, size_z, 3 * chans)
    return (
        roll_z(parts[:, :, 0:chans], 1)
        + parts[:, :, chans : 2 * chans]
        + roll_z(parts[:, :, 2 * chans : 3 * chans], -1)
    )


def spread_errors(errors):
    count, size_z, chans = errors.shape
    parts = [roll_z(errors, -1), errors, roll_z(errors, 1)]
    return jnp.concatenate([p.reshape(count * size_z, chans) for p in parts], axis=1).astype(BF16)


def fill_forward(packed, taps):
    for kx in range(3):
        for ky in range(3):
            for kz in range(3):
                at = kx * 3 + ky
                packed[at * 128 : at * 128 + 128, kz * 128 : kz * 128 + 128] = taps[at * 3 + kz]


def fill_backward(packed, taps):
    for kx in range(3):
        for ky in range(3):
            for kz in range(3):
                at = kx * 3 + ky
                packed[kz * 128 : kz * 128 + 128, at * 128 : at * 128 + 128] = taps[26 - at * 3 - kz]


def dot_nn(left, right):
    return lax.dot_general(left, right, (((1,), (0,)), ((), ())), preferred_element_type=F32)


def dot_nt(left, right):
    return lax.dot_general(left, right, (((1,), (1,)), ((), ())), preferred_element_type=F32)


def dot_tn(left, right):
    return lax.dot_general(left, right, (((0,), (0,)), ((), ())), preferred_element_type=F32)


def forward_kernel(own, before, after, left, right, taps_one, taps_two,
                   act_one, slope_one, slope_two, pooled, padded, packed, halves):
    fill_padded(padded, own, before, after, left, right)
    fill_forward(packed, taps_one)

    def first(row, _):
        product = dot_nn(window_rows(padded, row, 6), packed[...])
        act, slope = slope_and_silu(join_taps(product, 6, 64, 128))
        act_one[row] = act.astype(BF16)
        slope_one[row] = slope
        return 0

    lax.fori_loop(0, 6, first, 0)
    fill_forward(packed, taps_two)

    def second(row, _):
        product = dot_nn(window_rows(act_one, row, 4), packed[...])
        act, slope = slope_and_silu(join_taps(product, 4, 64, 128))
        slope_two[row] = slope
        act = act.astype(BF16).astype(F32)
        halves[row] = act.reshape(2, 2, 64, 128).sum(axis=1)
        return 0

    lax.fori_loop(0, 4, second, 0)
    for at_x in range(2):
        for at_y in range(2):
            total = 0.0
            for part in range(2):
                for start in range(2):
                    total = total + halves[2 * at_x + part, at_y, pl.ds(start, 32, stride=2), :]
            pooled[at_x, at_y] = (total * 0.125).astype(BF16)


def bottom_kernel(own, before, after, left, right, g_own, g_before, g_after, g_left, g_right,
                  taps_three, slope_two, skip, bottleneck, err_three, err_two,
                  padded, grads, packed, errors, wide):
    fill_padded(padded, own, before, after, left, right)
    fill_padded(grads, g_own, g_before, g_after, g_left, g_right)
    for at in range(9):
        for kz in range(3):
            packed[kz * 256 : kz * 256 + 256, at * 128 : at * 128 + 128] = taps_three[at * 3 + kz]
    for row in range(4):
        product = dot_nt(window_rows(padded, row, 4), packed[...])
        act, slope = slope_and_silu(join_taps(product, 4, 32, 256))
        if row in (1, 2):
            bottleneck[row - 1] = act[1:3].astype(BF16)
        errs = (grads[row].astype(F32) * slope).astype(BF16)
        errors[row] = errs
        if row in (1, 2):
            err_three[row - 1] = errs[1:3]
    for row in range(2):
        total = jnp.zeros((64, 384), F32)
        for kx in range(3):
            for ky in range(3):
                block = errors[row + kx, ky : ky + 2].reshape(64, 256)
                at = kx * 3 + ky
                back = jnp.concatenate(
                    [taps_three[26 - at * 3 - kz] for kz in range(3)], axis=1
                )
                total = total + dot_nn(block, back)
        upward = join_taps(total, 2, 32, 128) * 0.125
        for at_y in range(2):
            wide[pl.ds(0, 32, stride=2), :] = upward[at_y]
            wide[pl.ds(1, 32, stride=2), :] = upward[at_y]
            for dx in range(2):
                for dy in range(2):
                    at = (2 * row + dx, 2 * at_y + dy)
                    err_two[at] = (
                        (skip[at].astype(F32) + wide[...]) * slope_two[at]
                    ).astype(BF16)


def add_tap_grads(total, fields, skip, error_rows):
    total[...] = jnp.zeros_like(total)

    def step(row, _):
        total[...] += dot_tn(
            window_rows(fields, row, 4, skip), spread_errors(error_rows(row).astype(F32))
        )
        return 0

    lax.fori_loop(0, 4, step, 0)


def store_tap_grads(out, total):
    for at in range(9):
        for kz in range(3):
            rows = (at * 3 + kz) * 128
            out[rows : rows + 128] = total[
                at * 128 : at * 128 + 128, kz * 128 : kz * 128 + 128
            ].astype(BF16)
    out[3456:3584] = jnp.zeros((128, 128), BF16)


def middle_grads_kernel(act_one, err_two, out, total):
    add_tap_grads(total, act_one, 0, lambda row: err_two[row])
    store_tap_grads(out, total)


def bottom_grads_kernel(own, before, after, left, right, err_three, out, padded, total):
    fill_padded(padded, own, before, after, left, right)
    for row in range(2):
        term = dot_tn(
            spread_errors(err_three[row].astype(F32)), window_rows(padded, row, 2, 1)
        )
        if row == 0:
            total[...] = term
        else:
            total[...] += term
    out[:, 48:64, 48:56] = jnp.zeros((2, 16, 8, 128), BF16)
    for unit in range(27):
        at_x, rows = unit // 7, unit % 7 * 8
        at, kz = unit // 3, unit % 3
        block = total[kz * 256 : kz * 256 + 256, at * 128 : at * 128 + 128]
        block = block.reshape(16, 2, 8, 128)
        for half in range(2):
            out[half, at_x * 16 : at_x * 16 + 16, rows : rows + 8] = block[:, half].astype(BF16)


def first_errors_kernel(own, before, after, left, right, taps_two, slope_one,
                        f_own, f_before, f_after, f_left, f_right, err_one, out,
                        padded, packed, total):
    fill_padded(padded, own, before, after, left, right)
    fill_backward(packed, taps_two)

    def step(row, _):
        product = dot_nt(window_rows(padded, row, 6), packed[...])
        back = join_taps(product, 6, 64, 128)
        err_one[row] = (back * slope_one[row]).astype(BF16)
        return 0

    lax.fori_loop(0, 6, step, 0)
    fill_padded(padded, f_own, f_before, f_after, f_left, f_right)
    add_tap_grads(total, padded, 1, lambda row: err_one[row + 1, 1:5])
    store_tap_grads(out, total)


def input_kernel(err_one, taps_one, out, packed):
    fill_backward(packed, taps_one)

    def step(row, _):
        product = dot_nt(window_rows(err_one, row, 4), packed[...])
        out[row] = join_taps(product, 4, 64, 128).astype(BF16)
        return 0

    lax.fori_loop(0, 4, step, 0)


def sum_kernel(pieces, out):
    total = pieces[0].astype(F32)
    for at in range(1, 64):
        total = total + pieces[at].astype(F32)
    total = total.astype(BF16)
    for at in range(64):
        out[at] = total


def place_kernel(chip, pair_0, pair_1, pair_2, pair_3, out, *, scale):
    for distance, pair in enumerate((pair_0, pair_1, pair_2, pair_3)):
        at = lax.rem(chip[0] + 4 - distance, 4)

        def put(rows, pair=pair, at=at):
            both = [pair[c, rows * 8 : rows * 8 + 8].astype(F32) * scale for c in range(2)]
            out[at * 7 + rows] = jnp.concatenate(both, axis=0)

        for rows in range(6):
            put(rows)
        pl.when(at < 3)(functools.partial(put, 6))


def finish_kernel(core, whole, other, grad_one, grad_two, *, scale):
    @pl.when(core[0] == 0)
    def _():
        grad_one[...] = whole[0:3456].astype(F32) * scale
        grad_two[...] = other[0:3456].astype(F32) * scale

    @pl.when(core[0] == 1)
    def _():
        grad_one[...] = other[0:3456].astype(F32) * scale
        grad_two[...] = whole[0:3456].astype(F32) * scale


def call(kernel, out_shapes, scratch, flops, *operands):
    shapes = [jax.ShapeDtypeStruct(s, d) for s, d in out_shapes]
    moved = sum(o.size * o.dtype.itemsize for o in operands)
    return pl.pallas_call(
        kernel,
        out_shape=shapes,
        in_specs=[pl.BlockSpec(memory_space=pltpu.VMEM)] * len(operands),
        out_specs=[pl.BlockSpec(memory_space=pltpu.VMEM)] * len(shapes),
        scratch_shapes=[pltpu.VMEM(s, d) for s, d in scratch],
        compiler_params=pltpu.CompilerParams(vmem_limit_bytes=48 << 20),
        cost_estimate=pl.CostEstimate(flops=flops // 20, bytes_accessed=moved // 20, transcendentals=0),
        name=kernel.__name__,
    )(*operands)


def pick(stacked, index):
    return lax.dynamic_index_in_dim(stacked, index, 0, keepdims=False)


def after(array, *others):
    return lax.optimization_barrier((array, *others))[0]


def on_device(features, skip_grad, bottom_grad, conv_one, conv_two, conv_three):
    core = lax.axis_index("c")
    fine_cells = features.size // 128 * lax.axis_size(GX) * lax.axis_size(GY)
    fine_scale = 1.0 / math.sqrt(fine_cells)
    coarse_scale = 1.0 / math.sqrt(fine_cells // 8)
    taps_one = conv_one.reshape(27, 128, 128)
    taps_two = conv_two.reshape(27, 128, 128)

    f_pieces = halo_pieces(features, 2)

    own_taps = jnp.swapaxes(conv_three.reshape(27, 128, 16), 1, 2)
    half_taps = pick(jnp.swapaxes(own_taps.reshape(27, 2, 8, 128), 0, 1), core)
    half_taps = jnp.broadcast_to(half_taps, (16, 27, 8, 128))
    mine = lax.all_to_all(half_taps, GY, 0, 0)
    g_pieces = halo_pieces(after(bottom_grad, f_pieces[1], f_pieces[2]), 1)

    conv_flops = 2 * 1152 * 128 * 1024 * 3
    act_one, slope_one, slope_two, pooled = call(
        forward_kernel,
        [((6, 6, 64, 128), BF16), ((6, 6, 64, 128), F32), ((4, 4, 64, 128), F32), ((2, 2, 32, 128), BF16)],
        [((8, 8, 64, 128), BF16), ((1152, 384), BF16), ((4, 2, 64, 128), F32)],
        3 * conv_flops, *f_pieces, taps_one, taps_two,
    )
    p_pieces = halo_pieces(pooled, 2)
    mine = after(mine, pooled)
    theirs = swap_cores(mine)
    both = jnp.where(core == 0, jnp.stack([mine, theirs]), jnp.stack([theirs, mine]))
    taps_three = jnp.transpose(both, (2, 1, 0, 3, 4)).reshape(27, 256, 128)
    bottleneck, err_three, err_two = call(
        bottom_kernel,
        [((2, 2, 32, 256), BF16), ((2, 2, 32, 256), BF16), ((4, 4, 64, 128), BF16)],
        [((6, 6, 32, 128), BF16), ((4, 4, 32, 256), BF16), ((768, 1152), BF16),
         ((4, 4, 32, 256), BF16), ((64, 128), F32)],
        conv_flops, *p_pieces, *g_pieces, taps_three, slope_two, skip_grad,
    )
    (three,) = call(
        bottom_grads_kernel, [((2, 64, PIECE, 128), BF16)],
        [((6, 6, 32, 128), BF16), ((768, 1152), F32)],
        conv_flops // 4, *p_pieces, err_three,
    )
    (two,) = call(
        middle_grads_kernel, [((3584, 128), BF16)], [((1152, 384), F32)],
        conv_flops, act_one, err_two,
    )
    kept = pick(three, core).astype(F32) + swap_cores(pick(three, 1 - core)).astype(F32)
    three_pieces = lax.all_to_all(kept.astype(BF16), FLAT, 0, 0)
    three_part = jnp.sum(three_pieces.astype(F32), axis=0).astype(BF16)
    e_pieces = halo_pieces(err_two, 2)

    err_one, one = call(
        first_errors_kernel, [((6, 6, 64, 128), BF16), ((3584, 128), BF16)],
        [((8, 8, 64, 128), BF16), ((384, 1152), BF16), ((1152, 384), F32)],
        3 * conv_flops, *e_pieces, taps_two, slope_one, *f_pieces,
    )
    one = after(one, three_pieces)
    sent = jnp.where(core == 0, two, one)
    kept = jnp.where(core == 0, one, two).astype(F32) + swap_cores(sent).astype(F32)
    kept = after(kept.astype(BF16).reshape(64, PIECE, 128), three_part)
    (part,) = call(
        sum_kernel, [((64, PIECE, 128), BF16)], [], 0, lax.all_to_all(kept, FLAT, 0, 0)
    )
    (input_grad,) = call(
        input_kernel, [((4, 4, 64, 128), BF16)], [((384, 1152), BF16)],
        conv_flops, err_one, taps_one,
    )
    both = swap_cores(three_part)
    both = jnp.where(core == 0, jnp.stack([three_part, both]), jnp.stack([both, three_part]))
    pairs = [both] + [lax.ppermute(both, "x", [(i, (i + d) % 4) for i in range(4)]) for d in (1, 2, 3)]
    grad_three = pl.pallas_call(
        functools.partial(place_kernel, scale=coarse_scale),
        out_shape=jax.ShapeDtypeStruct((27, 16, 128), F32),
        in_specs=[pl.BlockSpec(memory_space=pltpu.SMEM)] + [pl.BlockSpec(memory_space=pltpu.VMEM)] * 4,
        out_specs=pl.BlockSpec(memory_space=pltpu.VMEM),
        name="place_kernel",
    )(lax.axis_index("x").reshape(1), *pairs)
    grad_three = jnp.swapaxes(grad_three, 1, 2).reshape(3, 3, 3, 128, 16)
    part = after(part, input_grad, grad_three)
    whole = lax.all_to_all(part, FLAT, 0, 0).reshape(64 * PIECE, 128)
    grad_one, grad_two = pl.pallas_call(
        functools.partial(finish_kernel, scale=fine_scale),
        out_shape=[jax.ShapeDtypeStruct((3456, 128), F32)] * 2,
        in_specs=[pl.BlockSpec(memory_space=pltpu.SMEM)] + [pl.BlockSpec(memory_space=pltpu.VMEM)] * 2,
        out_specs=[pl.BlockSpec(memory_space=pltpu.VMEM)] * 2,
        compiler_params=pltpu.CompilerParams(vmem_limit_bytes=32 << 20),
        name="finish_kernel",
    )(core.reshape(1), whole, swap_cores(whole))
    grad_one = grad_one.reshape(3, 3, 3, 128, 128)
    grad_two = grad_two.reshape(3, 3, 3, 128, 128)

    return (bottleneck, input_grad, grad_one, grad_two, grad_three)


def solution(mesh):
    fine = Mesh(mesh.devices.reshape(4, 2, 4, 4), ("x", "c", "z", "y"))
    cells = P(GX, GY, None, None)
    outs = P(None, None, None, None, GY)
    return jax.shard_map(
        on_device,
        mesh=fine,
        in_specs=(cells, cells, cells, P(), P(), outs),
        out_specs=(cells, cells, P(), P(), outs),
        check_vma=False,
    )
```

```python
import functools
import math

import jax
import jax.numpy as jnp
from jax import lax
from jax.experimental import pallas as pl
from jax.experimental.pallas import tpu as pltpu
from jax.sharding import Mesh
from jax.sharding import PartitionSpec as P

GX = ("x", "c")
GY = ("z", "y")
FLAT = ("x", "z", "y")
F32 = jnp.float32
BF16 = jnp.bfloat16
PIECE = 56


def shifted(array, axes, step):
    count = lax.axis_size(axes)
    return lax.ppermute(array, axes, [(i, (i + step) % count) for i in range(count)])


def swap_cores(array):
    return lax.ppermute(array, "c", [(0, 1), (1, 0)])


def halo_pieces(own, width):
    before = shifted(own[:, -width:], GY, 1)
    after = shifted(own[:, :width], GY, -1)
    low = jnp.concatenate([before[:width], own[:width], after[:width]], axis=1)
    high = jnp.concatenate([before[-width:], own[-width:], after[-width:]], axis=1)
    left = shifted(high, GX, 1)
    right = shifted(low, GX, -1)
    return (own, before, after, left, right), high


def fill_padded(padded, own, before, after, left, right):
    size_x, size_y = own.shape[0], own.shape[1]
    width = left.shape[0]
    padded[0:width] = left[...]
    padded[width + size_x : 2 * width + size_x] = right[...]
    middle = slice(width, width + size_x)
    padded[middle, 0:width] = before[...]
    padded[middle, width : width + size_y] = own[...]
    padded[middle, width + size_y : 2 * width + size_y] = after[...]


def slope_and_silu(values):
    sigma = 1.0 / (1.0 + jnp.exp(-values))
    return values * sigma, sigma * (1.0 + values * (1.0 - sigma))


def window_rows(source, row, count, skip=0):
    pieces = []
    for kx in range(3):
        for ky in range(3):
            block = source[row + kx + skip, ky + skip : ky + skip + count]
            pieces.append(block.reshape(block.shape[0] * block.shape[1], block.shape[2]))
    return jnp.concatenate(pieces, axis=1)


def roll_z(values, step):
    return pltpu.roll(values, step % values.shape[1], 1)


def join_taps(product, count, size_z, chans):
    parts = product.reshape(count, size_z, 3 * chans)
    return (
        roll_z(parts[:, :, 0:chans], 1)
        + parts[:, :, chans : 2 * chans]
        + roll_z(parts[:, :, 2 * chans : 3 * chans], -1)
    )


def spread_errors(errors):
    count, size_z, chans = errors.shape
    parts = [roll_z(errors, -1), errors, roll_z(errors, 1)]
    return jnp.concatenate([p.reshape(count * size_z, chans) for p in parts], axis=1).astype(BF16)


def fill_forward(packed, taps):
    for kx in range(3):
        for ky in range(3):
            for kz in range(3):
                at = kx * 3 + ky
                packed[at * 128 : at * 128 + 128, kz * 128 : kz * 128 + 128] = taps[at * 3 + kz]


def fill_backward(packed, taps):
    for kx in range(3):
        for ky in range(3):
            for kz in range(3):
                at = kx * 3 + ky
                packed[kz * 128 : kz * 128 + 128, at * 128 : at * 128 + 128] = taps[26 - at * 3 - kz]


def dot_nn(left, right):
    return lax.dot_general(left, right, (((1,), (0,)), ((), ())), preferred_element_type=F32)


def dot_nt(left, right):
    return lax.dot_general(left, right, (((1,), (1,)), ((), ())), preferred_element_type=F32)


def dot_tn(left, right):
    return lax.dot_general(left, right, (((0,), (0,)), ((), ())), preferred_element_type=F32)


def forward_kernel(own, before, after, left, right, taps_one, taps_two,
                   act_one, slope_one, slope_two, pooled, padded, packed, halves):
    fill_padded(padded, own, before, after, left, right)
    fill_forward(packed, taps_one)

    def first(row, _):
        product = dot_nn(window_rows(padded, row, 6), packed[...])
        act, slope = slope_and_silu(join_taps(product, 6, 64, 128))
        act_one[row] = act.astype(BF16)
        slope_one[row] = slope
        return 0

    lax.fori_loop(0, 6, first, 0)
    fill_forward(packed, taps_two)

    def second(row, _):
        product = dot_nn(window_rows(act_one, row, 4), packed[...])
        act, slope = slope_and_silu(join_taps(product, 4, 64, 128))
        slope_two[row] = slope
        act = act.astype(BF16).astype(F32)
        halves[row] = act.reshape(2, 2, 64, 128).sum(axis=1)
        return 0

    lax.fori_loop(0, 4, second, 0)
    for at_x in range(2):
        for at_y in range(2):
            total = 0.0
            for part in range(2):
                for start in range(2):
                    total = total + halves[2 * at_x + part, at_y, pl.ds(start, 32, stride=2), :]
            pooled[at_x, at_y] = (total * 0.125).astype(BF16)


def bottom_kernel(own, before, after, left, right, g_own, g_before, g_after, g_left, g_right,
                  taps_three, slope_two, skip, bottleneck, err_three, err_two,
                  padded, grads, packed, errors, wide):
    fill_padded(padded, own, before, after, left, right)
    fill_padded(grads, g_own, g_before, g_after, g_left, g_right)
    for at in range(9):
        for kz in range(3):
            packed[kz * 256 : kz * 256 + 256, at * 128 : at * 128 + 128] = taps_three[at * 3 + kz]
    for row in range(4):
        product = dot_nt(window_rows(padded, row, 4), packed[...])
        act, slope = slope_and_silu(join_taps(product, 4, 32, 256))
        if row in (1, 2):
            bottleneck[row - 1] = act[1:3].astype(BF16)
        errs = (grads[row].astype(F32) * slope).astype(BF16)
        errors[row] = errs
        if row in (1, 2):
            err_three[row - 1] = errs[1:3]
    for row in range(2):
        total = jnp.zeros((64, 384), F32)
        for kx in range(3):
            for ky in range(3):
                block = errors[row + kx, ky : ky + 2].reshape(64, 256)
                at = kx * 3 + ky
                back = jnp.concatenate(
                    [taps_three[26 - at * 3 - kz] for kz in range(3)], axis=1
                )
                total = total + dot_nn(block, back)
        upward = join_taps(total, 2, 32, 128) * 0.125
        for at_y in range(2):
            wide[pl.ds(0, 32, stride=2), :] = upward[at_y]
            wide[pl.ds(1, 32, stride=2), :] = upward[at_y]
            for dx in range(2):
                for dy in range(2):
                    at = (2 * row + dx, 2 * at_y + dy)
                    err_two[at] = (
                        (skip[at].astype(F32) + wide[...]) * slope_two[at]
                    ).astype(BF16)


def add_tap_grads(total, fields, skip, error_rows):
    total[...] = jnp.zeros_like(total)

    def step(row, _):
        total[...] += dot_tn(
            window_rows(fields, row, 4, skip), spread_errors(error_rows(row).astype(F32))
        )
        return 0

    lax.fori_loop(0, 4, step, 0)


def store_tap_grads(total, put):
    for at in range(9):
        for kz in range(3):
            part = total[at * 128 : at * 128 + 128, kz * 128 : kz * 128 + 128].astype(BF16)
            put((at * 3 + kz) * 128, part)
    put(3456, jnp.zeros((128, 128), BF16))


def middle_grads_kernel(act_one, err_two, out, total):
    add_tap_grads(total, act_one, 0, lambda row: err_two[row])

    def put(rows, part):
        out[rows : rows + 128] = part

    store_tap_grads(total, put)


def bottom_grads_kernel(own, before, after, left, right, err_three, out, padded, total):
    fill_padded(padded, own, before, after, left, right)
    for row in range(2):
        term = dot_tn(
            spread_errors(err_three[row].astype(F32)), window_rows(padded, row, 2, 1)
        )
        if row == 0:
            total[...] = term
        else:
            total[...] += term
    out[:, 48:64, 48:56] = jnp.zeros((2, 16, 8, 128), BF16)
    for unit in range(27):
        at_x, rows = unit // 7, unit % 7 * 8
        at, kz = unit // 3, unit % 3
        block = total[kz * 256 : kz * 256 + 256, at * 128 : at * 128 + 128]
        block = block.reshape(16, 2, 8, 128)
        for half in range(2):
            out[half, at_x * 16 : at_x * 16 + 16, rows : rows + 8] = block[:, half].astype(BF16)


def first_errors_kernel(core, own, before, after, left, right, taps_two, slope_one,
                        f_own, f_before, f_after, f_left, f_right, two, token,
                        err_one, out, padded, packed, total):
    fill_padded(padded, own, before, after, left, right)
    fill_backward(packed, taps_two)

    def step(row, _):
        product = dot_nt(window_rows(padded, row, 6), packed[...])
        back = join_taps(product, 6, 64, 128)
        err_one[row] = (back * slope_one[row]).astype(BF16)
        return 0

    lax.fori_loop(0, 6, step, 0)
    fill_padded(padded, f_own, f_before, f_after, f_left, f_right)
    add_tap_grads(total, padded, 1, lambda row: err_one[row + 1, 1:5])

    def put(rows, part):
        out[core[0], rows : rows + 128] = part
        out[1 - core[0], rows : rows + 128] = two[rows : rows + 128]

    store_tap_grads(total, put)


def input_kernel(err_one, taps_one, out, packed):
    fill_backward(packed, taps_one)

    def step(row, _):
        product = dot_nt(window_rows(err_one, row, 4), packed[...])
        out[row] = join_taps(product, 4, 64, 128).astype(BF16)
        return 0

    lax.fori_loop(0, 4, step, 0)


def sum_kernel(pieces, out):
    total = pieces[0].astype(F32)
    for at in range(1, 64):
        total = total + pieces[at].astype(F32)
    total = total.astype(BF16)
    for at in range(out.shape[0]):
        out[at] = total


def place_kernel(chip, pair_0, pair_1, pair_2, pair_3, out, *, scale):
    for distance, pair in enumerate((pair_0, pair_1, pair_2, pair_3)):
        at = lax.rem(chip[0] + 4 - distance, 4)

        def put(rows, pair=pair, at=at):
            both = [pair[c, rows * 8 : rows * 8 + 8].astype(F32) * scale for c in range(2)]
            out[at * 7 + rows] = jnp.concatenate(both, axis=0)

        for rows in range(6):
            put(rows)
        pl.when(at < 3)(functools.partial(put, 6))


def finish_kernel(core, whole, other, grad_one, grad_two, *, scale):
    @pl.when(core[0] == 0)
    def _():
        grad_one[...] = whole[0:3456].astype(F32) * scale
        grad_two[...] = other[0:3456].astype(F32) * scale

    @pl.when(core[0] == 1)
    def _():
        grad_one[...] = other[0:3456].astype(F32) * scale
        grad_two[...] = whole[0:3456].astype(F32) * scale


def call(kernel, out_shapes, scratch, flops, *operands):
    shapes = [jax.ShapeDtypeStruct(s, d) for s, d in out_shapes]
    moved = sum(o.size * o.dtype.itemsize for o in operands)
    return pl.pallas_call(
        kernel,
        out_shape=shapes,
        in_specs=[
            pl.BlockSpec(memory_space=pltpu.SMEM if o.dtype == jnp.int32 else pltpu.VMEM) for o in operands
        ],
        out_specs=[pl.BlockSpec(memory_space=pltpu.VMEM)] * len(shapes),
        scratch_shapes=[pltpu.VMEM(s, d) for s, d in scratch],
        compiler_params=pltpu.CompilerParams(vmem_limit_bytes=14 << 20),
        cost_estimate=pl.CostEstimate(flops=flops // 20, bytes_accessed=moved // 20, transcendentals=0),
        name=kernel.__name__,
    )(*operands)


def pick(stacked, index):
    return lax.dynamic_index_in_dim(stacked, index, 0, keepdims=False)


def after(array, *others):
    return lax.optimization_barrier((array, *others))[0]


def on_device(features, skip_grad, bottom_grad, conv_one, conv_two, conv_three):
    core = lax.axis_index("c")
    fine_cells = features.size // 128 * lax.axis_size(GX) * lax.axis_size(GY)
    fine_scale = 1.0 / math.sqrt(fine_cells)
    coarse_scale = 1.0 / math.sqrt(fine_cells // 8)
    taps_one = conv_one.reshape(27, 128, 128)
    taps_two = conv_two.reshape(27, 128, 128)

    f_pieces, _ = halo_pieces(features, 2)

    own_taps = jnp.swapaxes(conv_three.reshape(27, 128, 16), 1, 2)
    half_taps = pick(jnp.swapaxes(own_taps.reshape(27, 2, 8, 128), 0, 1), core)
    half_taps = jnp.broadcast_to(half_taps, (16, 27, 8, 128))
    mine = lax.all_to_all(half_taps, GY, 0, 0)
    g_pieces, _ = halo_pieces(after(bottom_grad, f_pieces[1], f_pieces[2]), 1)

    conv_flops = 2 * 1152 * 128 * 1024 * 3
    act_one, slope_one, slope_two, pooled = call(
        forward_kernel,
        [((6, 6, 64, 128), BF16), ((6, 6, 64, 128), F32), ((4, 4, 64, 128), F32), ((2, 2, 32, 128), BF16)],
        [((8, 8, 64, 128), BF16), ((1152, 384), BF16), ((4, 2, 64, 128), F32)],
        3 * conv_flops, *f_pieces, taps_one, taps_two,
    )
    p_pieces, _ = halo_pieces(pooled, 2)
    mine = after(mine, pooled)
    theirs = swap_cores(mine)
    both = jnp.where(core == 0, jnp.stack([mine, theirs]), jnp.stack([theirs, mine]))
    taps_three = jnp.transpose(both, (2, 1, 0, 3, 4)).reshape(27, 256, 128)
    bottleneck, err_three, err_two = call(
        bottom_kernel,
        [((2, 2, 32, 256), BF16), ((2, 2, 32, 256), BF16), ((4, 4, 64, 128), BF16)],
        [((6, 6, 32, 128), BF16), ((4, 4, 32, 256), BF16), ((768, 1152), BF16),
         ((4, 4, 32, 256), BF16), ((64, 128), F32)],
        conv_flops, *p_pieces, *g_pieces, taps_three, slope_two, skip_grad,
    )
    (three,) = call(
        bottom_grads_kernel, [((2, 64, PIECE, 128), BF16)],
        [((6, 6, 32, 128), BF16), ((768, 1152), F32)],
        conv_flops // 4, *p_pieces, err_three,
    )
    (two,) = call(
        middle_grads_kernel, [((3584, 128), BF16)], [((1152, 384), F32)],
        conv_flops, act_one, err_two,
    )
    e_pieces, e_high = halo_pieces(err_two, 2)
    token = swap_cores(e_high[0, 0, :8])
    kept = pick(three, core).astype(F32) + swap_cores(pick(three, 1 - core)).astype(F32)
    kept, token = lax.optimization_barrier((kept.astype(BF16), token))
    three_pieces = lax.all_to_all(kept, FLAT, 0, 0)

    err_one, one = call(
        first_errors_kernel, [((6, 6, 64, 128), BF16), ((2, 3584, 128), BF16)],
        [((8, 8, 64, 128), BF16), ((384, 1152), BF16), ((1152, 384), F32)],
        3 * conv_flops, core.reshape(1), *e_pieces, taps_two, slope_one, *f_pieces, two, token,
    )
    sent = after(one[1], three_pieces)
    kept = one[0].astype(F32) + swap_cores(sent).astype(F32)
    kept = kept.astype(BF16).reshape(64, PIECE, 128)
    (part,) = call(
        sum_kernel, [((64, PIECE, 128), BF16)], [], 0, lax.all_to_all(kept, FLAT, 0, 0)
    )
    (input_grad,) = call(
        input_kernel, [((4, 4, 64, 128), BF16)], [((384, 1152), BF16)],
        conv_flops, err_one, taps_one,
    )
    (three_part,) = call(sum_kernel, [((1, PIECE, 128), BF16)], [], 0, three_pieces)
    three_part = three_part[0]
    both = swap_cores(three_part)
    both = jnp.where(core == 0, jnp.stack([three_part, both]), jnp.stack([both, three_part]))
    pairs = [both] + [lax.ppermute(both, "x", [(i, (i + d) % 4) for i in range(4)]) for d in (1, 2, 3)]
    grad_three = pl.pallas_call(
        functools.partial(place_kernel, scale=coarse_scale),
        out_shape=jax.ShapeDtypeStruct((27, 16, 128), F32),
        in_specs=[pl.BlockSpec(memory_space=pltpu.SMEM)] + [pl.BlockSpec(memory_space=pltpu.VMEM)] * 4,
        out_specs=pl.BlockSpec(memory_space=pltpu.VMEM),
        name="place_kernel",
    )(lax.axis_index("x").reshape(1), *pairs)
    grad_three = jnp.swapaxes(grad_three, 1, 2).reshape(3, 3, 3, 128, 16)
    part = after(part, input_grad, grad_three)
    whole = lax.all_to_all(part, FLAT, 0, 0).reshape(64 * PIECE, 128)
    grad_one, grad_two = pl.pallas_call(
        functools.partial(finish_kernel, scale=fine_scale),
        out_shape=[jax.ShapeDtypeStruct((3456, 128), F32)] * 2,
        in_specs=[pl.BlockSpec(memory_space=pltpu.SMEM)] + [pl.BlockSpec(memory_space=pltpu.VMEM)] * 2,
        out_specs=[pl.BlockSpec(memory_space=pltpu.VMEM)] * 2,
        compiler_params=pltpu.CompilerParams(vmem_limit_bytes=8 << 20),
        name="finish_kernel",
    )(core.reshape(1), whole, swap_cores(whole))
    grad_one = grad_one.reshape(3, 3, 3, 128, 128)
    grad_two = grad_two.reshape(3, 3, 3, 128, 128)

    return (bottleneck, input_grad, grad_one, grad_two, grad_three)


def solution(mesh):
    fine = Mesh(mesh.devices.reshape(4, 2, 4, 4), ("x", "c", "z", "y"))
    cells = P(GX, GY, None, None)
    outs = P(None, None, None, None, GY)
    return jax.shard_map(
        on_device,
        mesh=fine,
        in_specs=(cells, cells, cells, P(), P(), outs),
        out_specs=(cells, cells, P(), P(), outs),
        check_vma=False,
    )
```

```python
import functools
import math

import jax
import jax.numpy as jnp
from jax import lax
from jax.experimental import pallas as pl
from jax.experimental.pallas import tpu as pltpu
from jax.sharding import Mesh
from jax.sharding import PartitionSpec as P

GX = ("x", "c")
GY = ("z", "y")
FLAT = ("x", "z", "y")
F32 = jnp.float32
BF16 = jnp.bfloat16
PIECE = 56


def shifted(array, axes, step):
    count = lax.axis_size(axes)
    return lax.ppermute(array, axes, [(i, (i + step) % count) for i in range(count)])


def swap_cores(array):
    return lax.ppermute(array, "c", [(0, 1), (1, 0)])


def halo_pieces(own, width, first=None, last=None):
    before = shifted(own[:, -width:] if last is None else last, GY, 1)
    after = shifted(own[:, :width] if first is None else first, GY, -1)
    low = jnp.concatenate([before[:width], own[:width], after[:width]], axis=1)
    high = jnp.concatenate([before[-width:], own[-width:], after[-width:]], axis=1)
    low, high = lax.optimization_barrier((low, high))
    left = shifted(high, GX, 1)
    right = shifted(low, GX, -1)
    return (own, before, after, left, right), high


def fill_padded(padded, own, before, after, left, right):
    size_x, size_y = own.shape[0], own.shape[1]
    width = left.shape[0]
    padded[0:width] = left[...]
    padded[width + size_x : 2 * width + size_x] = right[...]
    middle = slice(width, width + size_x)
    padded[middle, 0:width] = before[...]
    padded[middle, width : width + size_y] = own[...]
    padded[middle, width + size_y : 2 * width + size_y] = after[...]


def slope_and_silu(values):
    sigma = 1.0 / (1.0 + jnp.exp(-values))
    return values * sigma, sigma * (1.0 + values * (1.0 - sigma))


def window_rows(source, row, count, skip=0):
    pieces = []
    for kx in range(3):
        for ky in range(3):
            block = source[row + kx + skip, ky + skip : ky + skip + count]
            pieces.append(block.reshape(block.shape[0] * block.shape[1], block.shape[2]))
    return jnp.concatenate(pieces, axis=1)


def roll_z(values, step):
    return pltpu.roll(values, step % values.shape[1], 1)


def join_taps(product, count, size_z, chans):
    parts = product.reshape(count, size_z, 3 * chans)
    return (
        roll_z(parts[:, :, 0:chans], 1)
        + parts[:, :, chans : 2 * chans]
        + roll_z(parts[:, :, 2 * chans : 3 * chans], -1)
    )


def spread_errors(errors):
    count, size_z, chans = errors.shape
    parts = [roll_z(errors, -1), errors, roll_z(errors, 1)]
    return jnp.concatenate([p.reshape(count * size_z, chans) for p in parts], axis=1).astype(BF16)


def fill_forward(packed, taps):
    for kx in range(3):
        for ky in range(3):
            for kz in range(3):
                at = kx * 3 + ky
                packed[at * 128 : at * 128 + 128, kz * 128 : kz * 128 + 128] = taps[at * 3 + kz]


def fill_backward(packed, taps):
    for kx in range(3):
        for ky in range(3):
            for kz in range(3):
                at = kx * 3 + ky
                packed[kz * 128 : kz * 128 + 128, at * 128 : at * 128 + 128] = taps[26 - at * 3 - kz]


def dot_nn(left, right):
    return lax.dot_general(left, right, (((1,), (0,)), ((), ())), preferred_element_type=F32)


def dot_nt(left, right):
    return lax.dot_general(left, right, (((1,), (1,)), ((), ())), preferred_element_type=F32)


def dot_tn(left, right):
    return lax.dot_general(left, right, (((0,), (0,)), ((), ())), preferred_element_type=F32)


def forward_kernel(core, own, before, after, left, right, taps_one, taps_two,
                   field_keep, field_send, slope_one, slope_two, pooled,
                   padded, packed, act_one, halves):
    fill_padded(padded, own, before, after, left, right)
    fill_forward(packed, taps_one)
    first_core = core[0] == 0

    def first(row, _):
        product = dot_nn(window_rows(padded, row, 6), packed[...])
        act, slope = slope_and_silu(join_taps(product, 6, 64, 128))
        act = act.astype(BF16)
        field = padded[row + 1, 1:7]
        act_one[row] = act
        field_keep[row] = jnp.where(first_core, field, act)
        field_send[row] = jnp.where(first_core, act, field)
        slope_one[row] = slope
        return 0

    lax.fori_loop(0, 6, first, 0)
    fill_forward(packed, taps_two)

    def second(row, _):
        product = dot_nn(window_rows(act_one, row, 4), packed[...])
        act, slope = slope_and_silu(join_taps(product, 4, 64, 128))
        slope_two[row] = slope
        act = act.astype(BF16).astype(F32)
        halves[row] = act.reshape(2, 2, 64, 128).sum(axis=1)
        return 0

    lax.fori_loop(0, 4, second, 0)
    for at_x in range(2):
        for at_y in range(2):
            total = 0.0
            for part in range(2):
                for start in range(2):
                    total = total + halves[2 * at_x + part, at_y, pl.ds(start, 32, stride=2), :]
            pooled[at_x, at_y] = (total * 0.125).astype(BF16)


def bottom_kernel(own, before, after, left, right, g_own, g_before, g_after, g_left, g_right,
                  taps_three, slope_two, skip, bottleneck, bundle, err_two, err_first, err_last,
                  padded, grads, packed, errors, wide):
    fill_padded(padded, own, before, after, left, right)
    fill_padded(grads, g_own, g_before, g_after, g_left, g_right)
    for at in range(9):
        for kz in range(3):
            packed[kz * 256 : kz * 256 + 256, at * 128 : at * 128 + 128] = taps_three[at * 3 + kz]
    for row in range(4):
        product = dot_nt(window_rows(padded, row, 4), packed[...])
        act, slope = slope_and_silu(join_taps(product, 4, 32, 256))
        if row in (1, 2):
            bottleneck[row - 1] = act[1:3].astype(BF16)
        errs = (grads[row].astype(F32) * slope).astype(BF16)
        errors[row] = errs
        bundle[row * 4 : row * 4 + 4] = padded[row + 1, 1:5]
        if row in (1, 2):
            for at_y in range(2):
                for half in range(2):
                    at = 16 + ((row - 1) * 2 + at_y) * 2 + half
                    bundle[at] = errs[1 + at_y, :, half * 128 : half * 128 + 128]
    for row in range(2):
        total = jnp.zeros((64, 384), F32)
        for kx in range(3):
            for ky in range(3):
                block = errors[row + kx, ky : ky + 2].reshape(64, 256)
                at = kx * 3 + ky
                back = jnp.concatenate(
                    [taps_three[26 - at * 3 - kz] for kz in range(3)], axis=1
                )
                total = total + dot_nn(block, back)
        upward = join_taps(total, 2, 32, 128) * 0.125
        for at_y in range(2):
            wide[pl.ds(0, 32, stride=2), :] = upward[at_y]
            wide[pl.ds(1, 32, stride=2), :] = upward[at_y]
            for dx in range(2):
                for dy in range(2):
                    at = (2 * row + dx, 2 * at_y + dy)
                    err = ((skip[at].astype(F32) + wide[...]) * slope_two[at]).astype(BF16)
                    err_two[at] = err
                    edge = err_first if at_y == 0 else err_last
                    edge[2 * row + dx, dy] = err


def add_tap_grads(total, fields, errors):
    def step(row, _):
        total[...] += dot_tn(window_rows(fields, row, 4), spread_errors(errors[row].astype(F32)))
        return 0

    lax.fori_loop(0, 4, step, 0)


def own_grads_kernel(fields, errors, total):
    total[...] = jnp.zeros_like(total)
    add_tap_grads(total, fields, errors)


def pair_grads_kernel(fields, errors, own_total, out, total):
    total[...] = own_total[...]
    add_tap_grads(total, fields, errors)
    for at in range(9):
        for kz in range(3):
            rows = (at * 3 + kz) * 128
            out[rows : rows + 128] = total[
                at * 128 : at * 128 + 128, kz * 128 : kz * 128 + 128
            ].astype(BF16)
    out[3456:3584] = jnp.zeros((128, 128), BF16)


def bottom_grads_kernel(core, own, other, out, total):
    for step, bundle in ((0, own), (1, other)):
        for row in range(2):
            fields = []
            for kx in range(3):
                for ky in range(3):
                    at = (row + kx) * 4 + ky
                    fields.append(bundle[at : at + 2].reshape(64, 128))
            at = 16 + row * 4
            errors = [
                jnp.concatenate([bundle[at + 2 * y], bundle[at + 2 * y + 1]], axis=1).reshape(1, 32, 256)
                for y in range(2)
            ]
            errors = jnp.concatenate(errors, axis=0).astype(F32)
            term = dot_tn(spread_errors(errors), jnp.concatenate(fields, axis=1))
            if step == 0 and row == 0:
                total[...] = term
            else:
                total[...] += term
    first_core = core[0] == 0
    out[48:64, 48:56] = jnp.zeros((16, 8, 128), BF16)
    for unit in range(27):
        at_x, rows = unit // 7, unit % 7 * 8
        at, kz = unit // 3, unit % 3
        block = total[kz * 256 : kz * 256 + 256, at * 128 : at * 128 + 128]
        block = block.reshape(16, 2, 8, 128)
        block = jnp.where(first_core, block[:, 0], block[:, 1]).astype(BF16)
        out[at_x * 16 : at_x * 16 + 16, rows : rows + 8] = block


def first_errors_kernel(core, own, before, after, left, right, taps_two, slope_one, token,
                        err_one, err_keep, err_send, padded, packed):
    fill_padded(padded, own, before, after, left, right)
    fill_backward(packed, taps_two)

    def step(row, _):
        product = dot_nt(window_rows(padded, row, 6), packed[...])
        back = join_taps(product, 6, 64, 128)
        err_one[row] = (back * slope_one[row]).astype(BF16)
        return 0

    lax.fori_loop(0, 6, step, 0)
    first_core = core[0] == 0
    for row in range(4):
        first, second = err_one[row + 1, 1:5], own[row]
        err_keep[row] = jnp.where(first_core, first, second)
        err_send[row] = jnp.where(first_core, second, first)


def input_kernel(err_one, taps_one, out, packed):
    fill_backward(packed, taps_one)

    def step(row, _):
        product = dot_nt(window_rows(err_one, row, 4), packed[...])
        out[row] = join_taps(product, 4, 64, 128).astype(BF16)
        return 0

    lax.fori_loop(0, 4, step, 0)


def sum_kernel(pieces, out):
    total = pieces[0].astype(F32)
    for at in range(1, 64):
        total = total + pieces[at].astype(F32)
    total = total.astype(BF16)
    for at in range(out.shape[0]):
        out[at] = total


def place_kernel(chip, pair_0, pair_1, pair_2, pair_3, out, *, scale):
    for distance, pair in enumerate((pair_0, pair_1, pair_2, pair_3)):
        at = lax.rem(chip[0] + 4 - distance, 4)

        def put(rows, pair=pair, at=at):
            both = [pair[c, rows * 8 : rows * 8 + 8].astype(F32) * scale for c in range(2)]
            out[at * 7 + rows] = jnp.concatenate(both, axis=0)

        for rows in range(6):
            put(rows)
        pl.when(at < 3)(functools.partial(put, 6))


def finish_kernel(core, whole, other, grad_one, grad_two, *, scale):
    @pl.when(core[0] == 0)
    def _():
        grad_one[...] = whole[0:3456].astype(F32) * scale
        grad_two[...] = other[0:3456].astype(F32) * scale

    @pl.when(core[0] == 1)
    def _():
        grad_one[...] = other[0:3456].astype(F32) * scale
        grad_two[...] = whole[0:3456].astype(F32) * scale


def in_hbm(array):
    return pltpu.with_memory_space_constraint(array, pltpu.HBM)


def call(kernel, out_shapes, scratch, flops, *operands):
    shapes = [pltpu.HBM(*s[:2]) if s[2:] else jax.ShapeDtypeStruct(*s) for s in out_shapes]
    moved = sum(o.size * o.dtype.itemsize for o in operands)
    return pl.pallas_call(
        kernel,
        out_shape=shapes,
        in_specs=[
            pl.BlockSpec(memory_space=pltpu.SMEM if o.dtype == jnp.int32 else pltpu.VMEM) for o in operands
        ],
        out_specs=[pl.BlockSpec(memory_space=pltpu.VMEM)] * len(shapes),
        scratch_shapes=[pltpu.VMEM(s, d) for s, d in scratch],
        compiler_params=pltpu.CompilerParams(vmem_limit_bytes=18 << 20),
        cost_estimate=pl.CostEstimate(flops=flops // 20, bytes_accessed=moved // 20, transcendentals=0),
        name=kernel.__name__,
    )(*operands)


def pick(stacked, index):
    return lax.dynamic_index_in_dim(stacked, index, 0, keepdims=False)


def after(array, *others):
    return lax.optimization_barrier((array, *others))[0]


def on_device(features, skip_grad, bottom_grad, conv_one, conv_two, conv_three):
    core = lax.axis_index("c")
    fine_cells = features.size // 128 * lax.axis_size(GX) * lax.axis_size(GY)
    fine_scale = 1.0 / math.sqrt(fine_cells)
    coarse_scale = 1.0 / math.sqrt(fine_cells // 8)
    taps_one = conv_one.reshape(27, 128, 128)
    taps_two = conv_two.reshape(27, 128, 128)

    f_pieces, _ = halo_pieces(features, 2)

    own_taps = jnp.swapaxes(conv_three.reshape(27, 128, 16), 1, 2)
    half_taps = pick(jnp.swapaxes(own_taps.reshape(27, 2, 8, 128), 0, 1), core)
    half_taps = jnp.broadcast_to(half_taps, (16, 27, 8, 128))
    mine = lax.all_to_all(half_taps, GY, 0, 0)
    g_pieces, _ = halo_pieces(after(bottom_grad, f_pieces[1], f_pieces[2]), 1)

    conv_flops = 2 * 1152 * 128 * 1024 * 3
    core_ref = core.reshape(1)
    field = (6, 6, 64, 128)
    block = (4, 4, 64, 128)
    field_keep, field_send, slope_one, slope_two, pooled = call(
        forward_kernel,
        [(field, BF16, True), (field, BF16, True), (field, F32, True), (block, F32, True), ((2, 2, 32, 128), BF16)],
        [((8, 8, 64, 128), BF16), ((1152, 384), BF16), (field, BF16), ((4, 2, 64, 128), F32)],
        3 * conv_flops, core_ref, *f_pieces, taps_one, taps_two,
    )
    field_other = swap_cores(field_send)
    p_pieces, _ = halo_pieces(pooled, 2)
    mine = after(mine, pooled)
    theirs = swap_cores(mine)
    both = jnp.where(core == 0, jnp.stack([mine, theirs]), jnp.stack([theirs, mine]))
    taps_three = jnp.transpose(both, (2, 1, 0, 3, 4)).reshape(27, 256, 128)
    edge = (4, 2, 64, 128)
    bottleneck, bundle, err_two, err_first, err_last = call(
        bottom_kernel,
        [((2, 2, 32, 256), BF16, True), ((24, 32, 128), BF16), (block, BF16, True), (edge, BF16), (edge, BF16)],
        [((6, 6, 32, 128), BF16), ((4, 4, 32, 256), BF16), ((768, 1152), BF16),
         ((4, 4, 32, 256), BF16), ((64, 128), F32)],
        conv_flops, *p_pieces, *g_pieces, taps_three, slope_two, skip_grad,
    )
    e_pieces, e_high = halo_pieces(err_two, 2, err_first, err_last)
    token = swap_cores(e_high[0, 0, :8])

    (three,) = call(
        bottom_grads_kernel, [((64, PIECE, 128), BF16, True)], [((768, 1152), F32)],
        conv_flops // 2, core_ref, bundle, swap_cores(bundle),
    )
    three, token = lax.optimization_barrier((three, token))
    three_pieces = lax.all_to_all(three, FLAT, 0, 0)

    err_one, err_keep, err_send = call(
        first_errors_kernel, [(field, BF16, True), (block, BF16), (block, BF16)],
        [((8, 8, 64, 128), BF16), ((384, 1152), BF16)],
        2 * conv_flops, core_ref, *[in_hbm(e) for e in e_pieces[:3]], *e_pieces[3:],
        in_hbm(taps_two), in_hbm(slope_one), token,
    )
    err_other = swap_cores(err_send)
    (total,) = call(own_grads_kernel, [((1152, 384), F32)], [], conv_flops, in_hbm(field_keep), err_keep)
    (kept,) = call(
        pair_grads_kernel, [((3584, 128), BF16, True)], [((1152, 384), F32)],
        conv_flops, field_other, err_other, total,
    )
    kept = after(kept, three_pieces).reshape(64, PIECE, 128)
    (part,) = call(
        sum_kernel, [((64, PIECE, 128), BF16, True)], [], 0, lax.all_to_all(kept, FLAT, 0, 0)
    )
    (three_part,) = call(sum_kernel, [((1, PIECE, 128), BF16)], [], 0, three_pieces)
    three_part = three_part[0]
    both = swap_cores(three_part)
    both = jnp.where(core == 0, jnp.stack([three_part, both]), jnp.stack([both, three_part]))
    pairs = [both] + [lax.ppermute(both, "x", [(i, (i + d) % 4) for i in range(4)]) for d in (1, 2, 3)]
    grad_three = pl.pallas_call(
        functools.partial(place_kernel, scale=coarse_scale),
        out_shape=jax.ShapeDtypeStruct((27, 16, 128), F32),
        in_specs=[pl.BlockSpec(memory_space=pltpu.SMEM)] + [pl.BlockSpec(memory_space=pltpu.VMEM)] * 4,
        out_specs=pl.BlockSpec(memory_space=pltpu.VMEM),
        name="place_kernel",
    )(lax.axis_index("x").reshape(1), *pairs)
    grad_three = jnp.swapaxes(grad_three, 1, 2).reshape(3, 3, 3, 128, 16)
    (input_grad,) = call(
        input_kernel, [(block, BF16, True)], [((384, 1152), BF16)],
        conv_flops, in_hbm(err_one), in_hbm(taps_one),
    )
    part = after(part, input_grad, grad_three)
    whole = lax.all_to_all(part, FLAT, 0, 0).reshape(64 * PIECE, 128)
    grad_one, grad_two = pl.pallas_call(
        functools.partial(finish_kernel, scale=fine_scale),
        out_shape=[jax.ShapeDtypeStruct((3456, 128), F32)] * 2,
        in_specs=[pl.BlockSpec(memory_space=pltpu.SMEM)] + [pl.BlockSpec(memory_space=pltpu.VMEM)] * 2,
        out_specs=[pl.BlockSpec(memory_space=pltpu.VMEM)] * 2,
        compiler_params=pltpu.CompilerParams(vmem_limit_bytes=8 << 20),
        name="finish_kernel",
    )(core.reshape(1), whole, swap_cores(whole))
    grad_one = grad_one.reshape(3, 3, 3, 128, 128)
    grad_two = grad_two.reshape(3, 3, 3, 128, 128)

    return (bottleneck, input_grad, grad_one, grad_two, grad_three)


def solution(mesh):
    fine = Mesh(mesh.devices.reshape(4, 2, 4, 4), ("x", "c", "z", "y"))
    cells = P(GX, GY, None, None)
    outs = P(None, None, None, None, GY)
    return jax.shard_map(
        on_device,
        mesh=fine,
        in_specs=(cells, cells, cells, P(), P(), outs),
        out_specs=(cells, cells, P(), P(), outs),
        check_vma=False,
    )
```

```python
import functools
import math

import jax
import jax.numpy as jnp
from jax import lax
from jax.experimental import pallas as pl
from jax.experimental.pallas import tpu as pltpu
from jax.sharding import Mesh
from jax.sharding import PartitionSpec as P

GX = ("x", "c")
GY = ("z", "y")
FLAT = ("x", "z", "y")
F32 = jnp.float32
BF16 = jnp.bfloat16
PIECE = 56


def shifted(array, axes, step):
    count = lax.axis_size(axes)
    return lax.ppermute(array, axes, [(i, (i + step) % count) for i in range(count)])


def swap_cores(array):
    return lax.ppermute(array, "c", [(0, 1), (1, 0)])


def ring_pieces(pieces, axis):
    sent = [lax.ppermute(pieces[d], axis, [(i, (i + d) % 4) for i in range(4)]) for d in (1, 2, 3)]
    return [pieces[0]] + sent


def halo_pieces(own, width, first=None, last=None):
    before = shifted(own[:, -width:] if last is None else last, GY, 1)
    after = shifted(own[:, :width] if first is None else first, GY, -1)
    low = jnp.concatenate([before[:width], own[:width], after[:width]], axis=1)
    high = jnp.concatenate([before[-width:], own[-width:], after[-width:]], axis=1)
    low, high = lax.optimization_barrier((low, high))
    left = shifted(high, GX, 1)
    right = shifted(low, GX, -1)
    return (own, before, after, left, right), high


def fill_padded(padded, own, before, after, left, right):
    size_x, size_y = own.shape[0], own.shape[1]
    width = left.shape[0]
    padded[0:width] = left[...]
    padded[width + size_x : 2 * width + size_x] = right[...]
    middle = slice(width, width + size_x)
    padded[middle, 0:width] = before[...]
    padded[middle, width : width + size_y] = own[...]
    padded[middle, width + size_y : 2 * width + size_y] = after[...]


def slope_and_silu(values):
    sigma = 1.0 / (1.0 + jnp.exp(-values))
    return values * sigma, sigma * (1.0 + values * (1.0 - sigma))


def window_rows(source, row, count, skip=0):
    pieces = []
    for kx in range(3):
        for ky in range(3):
            block = source[row + kx + skip, ky + skip : ky + skip + count]
            pieces.append(block.reshape(block.shape[0] * block.shape[1], block.shape[2]))
    return jnp.concatenate(pieces, axis=1)


def roll_z(values, step):
    return pltpu.roll(values, step % values.shape[1], 1)


def join_taps(product, count, size_z, chans):
    parts = product.reshape(count, size_z, 3 * chans)
    return (
        roll_z(parts[:, :, 0:chans], 1)
        + parts[:, :, chans : 2 * chans]
        + roll_z(parts[:, :, 2 * chans : 3 * chans], -1)
    )


def spread_errors(errors):
    count, size_z, chans = errors.shape
    parts = [roll_z(errors, -1), errors, roll_z(errors, 1)]
    return jnp.concatenate([p.reshape(count * size_z, chans) for p in parts], axis=1).astype(BF16)


def fill_forward(packed, taps):
    for kx in range(3):
        for ky in range(3):
            for kz in range(3):
                at = kx * 3 + ky
                packed[at * 128 : at * 128 + 128, kz * 128 : kz * 128 + 128] = taps[at * 3 + kz]


def fill_backward(packed, taps):
    for kx in range(3):
        for ky in range(3):
            for kz in range(3):
                at = kx * 3 + ky
                packed[kz * 128 : kz * 128 + 128, at * 128 : at * 128 + 128] = taps[26 - at * 3 - kz]


def dot_nn(left, right):
    return lax.dot_general(left, right, (((1,), (0,)), ((), ())), preferred_element_type=F32)


def dot_nt(left, right):
    return lax.dot_general(left, right, (((1,), (1,)), ((), ())), preferred_element_type=F32)


def dot_tn(left, right):
    return lax.dot_general(left, right, (((0,), (0,)), ((), ())), preferred_element_type=F32)


def forward_kernel(core, own, before, after, left, right, taps_one, taps_two,
                   field_keep, field_send, slope_one, slope_two, pooled,
                   padded, packed, act_one, halves):
    fill_padded(padded, own, before, after, left, right)
    fill_forward(packed, taps_one)
    first_core = core[0] == 0

    def first(row, _):
        product = dot_nn(window_rows(padded, row, 6), packed[...])
        act, slope = slope_and_silu(join_taps(product, 6, 64, 128))
        act = act.astype(BF16)
        field = padded[row + 1, 1:7]
        act_one[row] = act
        field_keep[row] = jnp.where(first_core, field, act)
        field_send[row] = jnp.where(first_core, act, field)
        slope_one[row] = slope
        return 0

    lax.fori_loop(0, 6, first, 0)
    fill_forward(packed, taps_two)

    def second(row, _):
        product = dot_nn(window_rows(act_one, row, 4), packed[...])
        act, slope = slope_and_silu(join_taps(product, 4, 64, 128))
        slope_two[row] = slope
        act = act.astype(BF16).astype(F32)
        halves[row] = act.reshape(2, 2, 64, 128).sum(axis=1)
        return 0

    lax.fori_loop(0, 4, second, 0)
    for at_x in range(2):
        for at_y in range(2):
            total = 0.0
            for part in range(2):
                for start in range(2):
                    total = total + halves[2 * at_x + part, at_y, pl.ds(start, 32, stride=2), :]
            pooled[at_x, at_y] = (total * 0.125).astype(BF16)


def bottom_kernel(own, before, after, left, right, g_own, g_before, g_after, g_left, g_right,
                  taps_three, slope_two, skip, bottleneck, bundle, err_two, err_first, err_last,
                  padded, grads, packed, errors, wide):
    fill_padded(padded, own, before, after, left, right)
    fill_padded(grads, g_own, g_before, g_after, g_left, g_right)
    for at in range(9):
        for kz in range(3):
            packed[kz * 256 : kz * 256 + 256, at * 128 : at * 128 + 128] = taps_three[at * 3 + kz]
    for row in range(4):
        product = dot_nt(window_rows(padded, row, 4), packed[...])
        act, slope = slope_and_silu(join_taps(product, 4, 32, 256))
        if row in (1, 2):
            bottleneck[row - 1] = act[1:3].astype(BF16)
        errs = (grads[row].astype(F32) * slope).astype(BF16)
        errors[row] = errs
        bundle[row * 4 : row * 4 + 4] = padded[row + 1, 1:5]
        if row in (1, 2):
            for at_y in range(2):
                for half in range(2):
                    at = 16 + ((row - 1) * 2 + at_y) * 2 + half
                    bundle[at] = errs[1 + at_y, :, half * 128 : half * 128 + 128]
    for row in range(2):
        total = jnp.zeros((64, 384), F32)
        for kx in range(3):
            for ky in range(3):
                block = errors[row + kx, ky : ky + 2].reshape(64, 256)
                at = kx * 3 + ky
                back = jnp.concatenate(
                    [taps_three[26 - at * 3 - kz] for kz in range(3)], axis=1
                )
                total = total + dot_nn(block, back)
        upward = join_taps(total, 2, 32, 128) * 0.125
        for at_y in range(2):
            wide[pl.ds(0, 32, stride=2), :] = upward[at_y]
            wide[pl.ds(1, 32, stride=2), :] = upward[at_y]
            for dx in range(2):
                for dy in range(2):
                    at = (2 * row + dx, 2 * at_y + dy)
                    err = ((skip[at].astype(F32) + wide[...]) * slope_two[at]).astype(BF16)
                    err_two[at] = err
                    edge = err_first if at_y == 0 else err_last
                    edge[2 * row + dx, dy] = err


def add_tap_grads(total, fields, errors):
    def step(row, _):
        total[...] += dot_tn(window_rows(fields, row, 4), spread_errors(errors[row].astype(F32)))
        return 0

    lax.fori_loop(0, 4, step, 0)


def own_grads_kernel(fields, errors, total):
    total[...] = jnp.zeros_like(total)
    add_tap_grads(total, fields, errors)


def pair_grads_kernel(fields, errors, own_total, out, total):
    total[...] = own_total[...]
    add_tap_grads(total, fields, errors)
    for at in range(9):
        for kz in range(3):
            rows = (at * 3 + kz) * 128
            out[rows : rows + 128] = total[
                at * 128 : at * 128 + 128, kz * 128 : kz * 128 + 128
            ].astype(BF16)
    out[3456:3584] = jnp.zeros((128, 128), BF16)


def bottom_grads_kernel(core, chip, own, other, out, total):
    for step, bundle in ((0, own), (1, other)):
        for row in range(2):
            fields = []
            for kx in range(3):
                for ky in range(3):
                    at = (row + kx) * 4 + ky
                    fields.append(bundle[at : at + 2].reshape(64, 128))
            at = 16 + row * 4
            errors = [
                jnp.concatenate([bundle[at + 2 * y], bundle[at + 2 * y + 1]], axis=1).reshape(1, 32, 256)
                for y in range(2)
            ]
            errors = jnp.concatenate(errors, axis=0).astype(F32)
            term = dot_tn(spread_errors(errors), jnp.concatenate(fields, axis=1))
            if step == 0 and row == 0:
                total[...] = term
            else:
                total[...] += term
    first_core = core[0] == 0
    out[lax.rem(7 - chip[0], 4), :, 48:56] = jnp.zeros((16, 8, 128), BF16)
    for unit in range(27):
        at_x, rows = lax.rem(unit // 7 + 4 - chip[0], 4), unit % 7 * 8
        at, kz = unit // 3, unit % 3
        block = total[kz * 256 : kz * 256 + 256, at * 128 : at * 128 + 128]
        block = block.reshape(16, 2, 8, 128)
        block = jnp.where(first_core, block[:, 0], block[:, 1]).astype(BF16)
        out[at_x, :, rows : rows + 8] = block


def first_errors_kernel(core, own, before, after, left, right, taps_two, slope_one,
                        err_one, err_keep, err_send, padded, packed):
    fill_padded(padded, own, before, after, left, right)
    fill_backward(packed, taps_two)

    def step(row, _):
        product = dot_nt(window_rows(padded, row, 6), packed[...])
        back = join_taps(product, 6, 64, 128)
        err_one[row] = (back * slope_one[row]).astype(BF16)
        return 0

    lax.fori_loop(0, 6, step, 0)
    first_core = core[0] == 0
    for row in range(4):
        first, second = err_one[row + 1, 1:5], own[row]
        err_keep[row] = jnp.where(first_core, first, second)
        err_send[row] = jnp.where(first_core, second, first)


def input_kernel(err_one, taps_one, out, packed):
    fill_backward(packed, taps_one)

    def step(row, _):
        product = dot_nt(window_rows(err_one, row, 4), packed[...])
        out[row] = join_taps(product, 4, 64, 128).astype(BF16)
        return 0

    lax.fori_loop(0, 4, step, 0)


def sum_kernel(pieces, out):
    total = pieces[0].astype(F32)
    for at in range(1, 64):
        total = total + pieces[at].astype(F32)
    total = total.astype(BF16)
    for at in range(out.shape[0]):
        out[at] = total


def stage_kernel(chip, own, piece_1, piece_2, piece_3, *outs):
    pieces = (own, piece_1, piece_2, piece_3)
    if len(outs) == 1:
        total = sum(p[0].astype(F32) for p in pieces)
        outs[0][...] = total.astype(BF16)
        return
    quarter = own.shape[0] // 4
    for distance, out in enumerate(outs):
        at = lax.rem(chip[0] + distance, 4) * quarter
        for row in range(quarter):
            total = sum(p[at + row].astype(F32) for p in pieces)
            out[row] = total.astype(BF16)


def gather_kernel(chip, piece_0, piece_1, piece_2, piece_3, out):
    for distance, piece in enumerate((piece_0, piece_1, piece_2, piece_3)):
        at = lax.rem(chip[0] + 4 - distance, 4)
        if len(out.shape) == 4:
            out[at] = piece[...]
        else:
            for row in range(4):
                out[:, row, at] = piece[row]


def place_kernel(chip, pair_0, pair_1, pair_2, pair_3, out, *, scale):
    for distance, pair in enumerate((pair_0, pair_1, pair_2, pair_3)):
        at = lax.rem(chip[0] + 4 - distance, 4)

        def put(rows, pair=pair, at=at):
            both = [pair[c, rows * 8 : rows * 8 + 8].astype(F32) * scale for c in range(2)]
            out[at * 7 + rows] = jnp.concatenate(both, axis=0)

        for rows in range(6):
            put(rows)
        pl.when(at < 3)(functools.partial(put, 6))


def finish_kernel(core, whole, other, grad_one, grad_two, *, scale):
    @pl.when(core[0] == 0)
    def _():
        grad_one[...] = whole[0:3456].astype(F32) * scale
        grad_two[...] = other[0:3456].astype(F32) * scale

    @pl.when(core[0] == 1)
    def _():
        grad_one[...] = other[0:3456].astype(F32) * scale
        grad_two[...] = whole[0:3456].astype(F32) * scale


def in_hbm(array):
    return pltpu.with_memory_space_constraint(array, pltpu.HBM)


def call(kernel, out_shapes, scratch, flops, *operands):
    shapes = [pltpu.HBM(*s[:2]) if s[2:] else jax.ShapeDtypeStruct(*s) for s in out_shapes]
    moved = sum(o.size * o.dtype.itemsize for o in operands)
    return pl.pallas_call(
        kernel,
        out_shape=shapes,
        in_specs=[
            pl.BlockSpec(memory_space=pltpu.SMEM if o.dtype == jnp.int32 else pltpu.VMEM) for o in operands
        ],
        out_specs=[pl.BlockSpec(memory_space=pltpu.VMEM)] * len(shapes),
        scratch_shapes=[pltpu.VMEM(s, d) for s, d in scratch],
        compiler_params=pltpu.CompilerParams(vmem_limit_bytes=18 << 20),
        cost_estimate=pl.CostEstimate(flops=flops // 20, bytes_accessed=moved // 20, transcendentals=0),
        name=kernel.__name__,
    )(*operands)


def pick(stacked, index):
    return lax.dynamic_index_in_dim(stacked, index, 0, keepdims=False)


def after(array, *others):
    return lax.optimization_barrier((array, *others))[0]


def on_device(features, skip_grad, bottom_grad, conv_one, conv_two, conv_three):
    core = lax.axis_index("c")
    f_sent, first_core, core, core_ref, *chip = lax.optimization_barrier((
        features[:, -2:], core == 0, core, core.reshape(1),
        *[lax.axis_index(axis).reshape(1) for axis in ("x", "z", "y")],
    ))
    fine_cells = features.size // 128 * lax.axis_size(GX) * lax.axis_size(GY)
    fine_scale = 1.0 / math.sqrt(fine_cells)
    coarse_scale = 1.0 / math.sqrt(fine_cells // 8)
    taps_one = conv_one.reshape(27, 128, 128)
    taps_two = conv_two.reshape(27, 128, 128)

    f_pieces, f_high = halo_pieces(features, 2, last=f_sent)

    own_taps = jnp.swapaxes(conv_three.reshape(27, 128, 16), 1, 2)
    half_taps = pick(jnp.swapaxes(own_taps.reshape(27, 2, 8, 128), 0, 1), core)
    half_taps = after(half_taps, f_high)
    piece = (4, 27, 8, 128)
    (mine,) = call(
        gather_kernel, [(piece, BF16)], [], 0, chip[1], *ring_pieces([half_taps] * 4, "z")
    )
    taps_pieces = ring_pieces([after(mine, *f_pieces[3:])] * 4, "y")
    g_pieces, _ = halo_pieces(after(bottom_grad, f_pieces[1], f_pieces[2]), 1)

    conv_flops = 2 * 1152 * 128 * 1024 * 3
    field = (6, 6, 64, 128)
    block = (4, 4, 64, 128)
    field_keep, field_send, slope_one, slope_two, pooled = call(
        forward_kernel,
        [(field, BF16), (field, BF16), (field, F32), (block, F32), ((2, 2, 32, 128), BF16)],
        [((8, 8, 64, 128), BF16), ((1152, 384), BF16), (field, BF16), ((4, 2, 64, 128), F32)],
        3 * conv_flops, core_ref, *f_pieces, taps_one, taps_two,
    )
    field_other = swap_cores(field_send)
    p_pieces, p_high = halo_pieces(pooled, 2)
    *taps_pieces, p_high = lax.optimization_barrier((*taps_pieces, p_high))
    (mine,) = call(gather_kernel, [((27, 4, 4, 8, 128), BF16)], [], 0, chip[2], *taps_pieces)
    mine = mine.reshape(27, 16, 8, 128)
    theirs = swap_cores(mine)
    both = jnp.where(first_core, jnp.stack([mine, theirs], 2), jnp.stack([theirs, mine], 2))
    taps_three = both.reshape(27, 256, 128)
    edge = (4, 2, 64, 128)
    bottleneck, bundle, err_two, err_first, err_last = call(
        bottom_kernel,
        [((2, 2, 32, 256), BF16, True), ((24, 32, 128), BF16), (block, BF16), (edge, BF16), (edge, BF16)],
        [((6, 6, 32, 128), BF16), ((4, 4, 32, 256), BF16), ((768, 1152), BF16),
         ((4, 4, 32, 256), BF16), ((64, 128), F32)],
        conv_flops, *p_pieces, *g_pieces, taps_three, slope_two, skip_grad,
    )
    e_pieces, e_high = halo_pieces(err_two, 2, err_first, err_last)
    bundle = after(bundle, e_high)
    (three,) = call(
        bottom_grads_kernel, [((4, 16, PIECE, 128), BF16)], [((768, 1152), F32)],
        conv_flops // 2, core_ref, chip[0], bundle, swap_cores(bundle),
    )
    three = after(three, e_pieces[3], e_pieces[4])
    pieces = ring_pieces([three[d] for d in range(4)], "x")
    pieces = call(stage_kernel, [((4, PIECE, 128), BF16)] * 4, [], 0, chip[1], *pieces)
    err_one, err_keep, err_send = call(
        first_errors_kernel, [(field, BF16, True), (block, BF16), (block, BF16)],
        [((8, 8, 64, 128), BF16), ((384, 1152), BF16)],
        2 * conv_flops, core_ref, *e_pieces, taps_two, slope_one,
    )
    err_other = swap_cores(err_send)
    (total,) = call(own_grads_kernel, [((1152, 384), F32)], [], conv_flops, field_keep, err_keep)
    (kept,) = call(
        pair_grads_kernel, [((3584, 128), BF16, True)], [((1152, 384), F32)],
        conv_flops, field_other, err_other, total,
    )
    kept, *pieces = lax.optimization_barrier((kept, *pieces))
    kept = kept.reshape(64, PIECE, 128)
    (part,) = call(
        sum_kernel, [((64, PIECE, 128), BF16, True)], [], 0, lax.all_to_all(kept, FLAT, 0, 0)
    )
    pieces = ring_pieces(pieces, "z")
    pieces = call(stage_kernel, [((1, PIECE, 128), BF16)] * 4, [], 0, chip[2], *pieces)
    (three_part,) = call(stage_kernel, [((PIECE, 128), BF16)], [], 0, chip[2], *ring_pieces(pieces, "y"))
    (input_grad,) = call(
        input_kernel, [(block, BF16, True)], [((384, 1152), BF16)],
        conv_flops, err_one, taps_one,
    )
    part, three_part = lax.optimization_barrier((after(part, input_grad), three_part))
    whole = lax.all_to_all(part, FLAT, 0, 0).reshape(64 * PIECE, 128)
    both = swap_cores(three_part)
    both = jnp.where(first_core, jnp.stack([three_part, both]), jnp.stack([both, three_part]))
    pairs = ring_pieces([both] * 4, "x")
    grad_three = pl.pallas_call(
        functools.partial(place_kernel, scale=coarse_scale),
        out_shape=jax.ShapeDtypeStruct((27, 16, 128), F32),
        in_specs=[pl.BlockSpec(memory_space=pltpu.SMEM)] + [pl.BlockSpec(memory_space=pltpu.VMEM)] * 4,
        out_specs=pl.BlockSpec(memory_space=pltpu.VMEM),
        name="place_kernel",
    )(chip[0], *pairs)
    whole, grad_three = lax.optimization_barrier((whole, grad_three))
    grad_three = jnp.swapaxes(grad_three, 1, 2).reshape(3, 3, 3, 128, 16)
    grad_one, grad_two = pl.pallas_call(
        functools.partial(finish_kernel, scale=fine_scale),
        out_shape=[jax.ShapeDtypeStruct((3456, 128), F32)] * 2,
        in_specs=[pl.BlockSpec(memory_space=pltpu.SMEM)] + [pl.BlockSpec(memory_space=pltpu.VMEM)] * 2,
        out_specs=[pl.BlockSpec(memory_space=pltpu.VMEM)] * 2,
        compiler_params=pltpu.CompilerParams(vmem_limit_bytes=8 << 20),
        name="finish_kernel",
    )(core_ref, whole, swap_cores(whole))
    grad_one = grad_one.reshape(3, 3, 3, 128, 128)
    grad_two = grad_two.reshape(3, 3, 3, 128, 128)

    return (bottleneck, input_grad, grad_one, grad_two, grad_three)


def solution(mesh):
    fine = Mesh(mesh.devices.reshape(4, 2, 4, 4), ("x", "c", "z", "y"))
    cells = P(GX, GY, None, None)
    outs = P(None, None, None, None, GY)
    return jax.shard_map(
        on_device,
        mesh=fine,
        in_specs=(cells, cells, cells, P(), P(), outs),
        out_specs=(cells, cells, P(), P(), outs),
        check_vma=False,
    )
```

```python
import functools
import math

import jax
import jax.numpy as jnp
from jax import lax
from jax.experimental import pallas as pl
from jax.experimental.pallas import tpu as pltpu
from jax.sharding import Mesh
from jax.sharding import PartitionSpec as P

GX = ("x", "c")
GY = ("z", "y")
FLAT = ("x", "z", "y")
F32 = jnp.float32
BF16 = jnp.bfloat16
PIECE = 56


def shifted(array, axes, step):
    count = lax.axis_size(axes)
    return lax.ppermute(array, axes, [(i, (i + step) % count) for i in range(count)])


def swap_cores(array):
    return lax.ppermute(array, "c", [(0, 1), (1, 0)])


def ring_pieces(pieces, axis):
    sent = [lax.ppermute(pieces[d], axis, [(i, (i + d) % 4) for i in range(4)]) for d in (1, 2, 3)]
    return [pieces[0]] + sent


def slab_kernel(own, before, after, low, high):
    width, size_x = low.shape[0], own.shape[0]
    for slab, start in ((low, 0), (high, size_x - width)):
        rows = slice(start, start + width)
        columns = 0
        for part in (before, own, after):
            slab[:, columns : columns + part.shape[1]] = part[rows]
            columns += part.shape[1]


def first_slab_kernel(own, before, after, grads, low, high):
    for slab, start, row in ((low, 0, 0), (high, 2, 1)):
        for at in range(2):
            slab[at * 8 : at * 8 + 2] = before[start + at]
            slab[at * 8 + 2 : at * 8 + 6] = own[start + at]
            slab[at * 8 + 6 : at * 8 + 8] = after[start + at]
        slab[16] = before[4, row]
        slab[19] = after[4, row]
        for at_y in range(2):
            for half in range(2):
                part = grads[row, at_y, :, half * 128 : half * 128 + 128]
                slab[17 + at_y, half * 32 : half * 32 + 32] = part


def exchange_x(low, high):
    return shifted(high, GX, 1), shifted(low, GX, -1)


def halo_pieces(own, width, first, last):
    before, after = shifted(last, GY, 1), shifted(first, GY, -1)
    size_x, size_y, size_z, chans = own.shape
    slab = (width, size_y + 2 * width, size_z, chans)
    low, high = call(slab_kernel, [(slab, BF16)] * 2, [], 0, own, before, after)
    return (own, before, after, *exchange_x(low, high)), high


def fill_padded(padded, own, before, after, left, right):
    size_x, size_y = own.shape[0], own.shape[1]
    width = left.shape[0]
    padded[0:width] = left[...]
    padded[width + size_x : 2 * width + size_x] = right[...]
    middle = slice(width, width + size_x)
    padded[middle, 0:width] = before[...]
    padded[middle, width : width + size_y] = own[...]
    padded[middle, width + size_y : 2 * width + size_y] = after[...]


def slope_and_silu(values):
    sigma = 1.0 / (1.0 + jnp.exp(-values))
    return values * sigma, sigma * (1.0 + values * (1.0 - sigma))


def window_rows(source, row, count, skip=0):
    pieces = []
    for kx in range(3):
        for ky in range(3):
            block = source[row + kx + skip, ky + skip : ky + skip + count]
            pieces.append(block.reshape(block.shape[0] * block.shape[1], block.shape[2]))
    return jnp.concatenate(pieces, axis=1)


def roll_z(values, step):
    return pltpu.roll(values, step % values.shape[1], 1)


def join_taps(product, count, size_z, chans):
    parts = product.reshape(count, size_z, 3 * chans)
    return (
        roll_z(parts[:, :, 0:chans], 1)
        + parts[:, :, chans : 2 * chans]
        + roll_z(parts[:, :, 2 * chans : 3 * chans], -1)
    )


def spread_errors(errors):
    count, size_z, chans = errors.shape
    parts = [roll_z(errors, -1), errors, roll_z(errors, 1)]
    return jnp.concatenate([p.reshape(count * size_z, chans) for p in parts], axis=1).astype(BF16)


def fill_forward(packed, taps):
    for kx in range(3):
        for ky in range(3):
            for kz in range(3):
                at = kx * 3 + ky
                packed[at * 128 : at * 128 + 128, kz * 128 : kz * 128 + 128] = taps[at * 3 + kz]


def fill_backward(packed, taps):
    for kx in range(3):
        for ky in range(3):
            for kz in range(3):
                at = kx * 3 + ky
                packed[kz * 128 : kz * 128 + 128, at * 128 : at * 128 + 128] = taps[26 - at * 3 - kz]


def dot_nn(left, right):
    return lax.dot_general(left, right, (((1,), (0,)), ((), ())), preferred_element_type=F32)


def dot_nt(left, right):
    return lax.dot_general(left, right, (((1,), (1,)), ((), ())), preferred_element_type=F32)


def dot_tn(left, right):
    return lax.dot_general(left, right, (((0,), (0,)), ((), ())), preferred_element_type=F32)


def forward_kernel(core, own, before, after, left, right, taps_one, taps_two,
                   field_keep, field_send, slope_one, slope_two, pooled,
                   padded, packed, act_one, halves):
    for at in range(2):
        padded[at] = left[at * 8 : at * 8 + 8]
        padded[6 + at] = right[at * 8 : at * 8 + 8]
    padded[2:6, 0:2] = before[0:4]
    padded[2:6, 2:6] = own[...]
    padded[2:6, 6:8] = after[0:4]
    fill_forward(packed, taps_one)
    first_core = core[0] == 0

    def first(row, _):
        product = dot_nn(window_rows(padded, row, 6), packed[...])
        act, slope = slope_and_silu(join_taps(product, 6, 64, 128))
        act = act.astype(BF16)
        field = padded[row + 1, 1:7]
        act_one[row] = act
        field_keep[row] = jnp.where(first_core, field, act)
        field_send[row] = jnp.where(first_core, act, field)
        slope_one[row] = slope.astype(BF16)
        return 0

    lax.fori_loop(0, 6, first, 0)
    fill_forward(packed, taps_two)

    def second(row, _):
        product = dot_nn(window_rows(act_one, row, 4), packed[...])
        act, slope = slope_and_silu(join_taps(product, 4, 64, 128))
        slope_two[row] = slope.astype(BF16)
        act = act.astype(BF16).astype(F32)
        halves[row] = act.reshape(2, 2, 64, 128).sum(axis=1)
        return 0

    lax.fori_loop(0, 4, second, 0)
    for at_x in range(2):
        for at_y in range(2):
            total = 0.0
            for part in range(2):
                for start in range(2):
                    total = total + halves[2 * at_x + part, at_y, pl.ds(start, 32, stride=2), :]
            pooled[at_x, at_y] = (total * 0.125).astype(BF16)


def bottom_kernel(own, before, after, left, right, g_own, f_before, f_after, f_left, f_right,
                  taps_three, slope_two, skip, bottleneck, bundle, err_two, err_first, err_last,
                  padded, grads, packed, errors, wide):
    fill_padded(padded, own, before, after, left, right)
    for half in range(2):
        rows, lanes = slice(half * 32, half * 32 + 32), slice(half * 128, half * 128 + 128)
        grads[0, :, :, lanes] = f_left[16:20, rows]
        grads[3, :, :, lanes] = f_right[16:20, rows]
        for at in range(2):
            grads[1 + at, 0, :, lanes] = f_before[4, at, rows]
            grads[1 + at, 3, :, lanes] = f_after[4, at, rows]
    grads[1:3, 1:3] = g_own[...]
    for at in range(9):
        for kz in range(3):
            packed[kz * 256 : kz * 256 + 256, at * 128 : at * 128 + 128] = taps_three[at * 3 + kz]
    for row in range(4):
        product = dot_nt(window_rows(padded, row, 4), packed[...])
        act, slope = slope_and_silu(join_taps(product, 4, 32, 256))
        if row in (1, 2):
            bottleneck[row - 1] = act[1:3].astype(BF16)
        errs = (grads[row].astype(F32) * slope).astype(BF16)
        errors[row] = errs
        bundle[row * 4 : row * 4 + 4] = padded[row + 1, 1:5]
        if row in (1, 2):
            for at_y in range(2):
                for half in range(2):
                    at = 16 + ((row - 1) * 2 + at_y) * 2 + half
                    bundle[at] = errs[1 + at_y, :, half * 128 : half * 128 + 128]
    for row in range(2):
        total = jnp.zeros((64, 384), F32)
        for kx in range(3):
            for ky in range(3):
                block = errors[row + kx, ky : ky + 2].reshape(64, 256)
                at = kx * 3 + ky
                back = jnp.concatenate(
                    [taps_three[26 - at * 3 - kz] for kz in range(3)], axis=1
                )
                total = total + dot_nn(block, back)
        upward = join_taps(total, 2, 32, 128) * 0.125
        for at_y in range(2):
            wide[pl.ds(0, 32, stride=2), :] = upward[at_y]
            wide[pl.ds(1, 32, stride=2), :] = upward[at_y]
            for dx in range(2):
                for dy in range(2):
                    at = (2 * row + dx, 2 * at_y + dy)
                    err = skip[at].astype(F32) + wide[...]
                    err = (err * slope_two[at].astype(F32)).astype(BF16)
                    err_two[at] = err
                    edge = err_first if at_y == 0 else err_last
                    edge[2 * row + dx, dy] = err


def add_tap_grads(total, fields, errors):
    def step(row, _):
        total[...] += dot_tn(window_rows(fields, row, 4), spread_errors(errors[row].astype(F32)))
        return 0

    lax.fori_loop(0, 4, step, 0)


def own_grads_kernel(fields, errors, total):
    total[...] = jnp.zeros_like(total)
    add_tap_grads(total, fields, errors)


def pair_grads_kernel(fields, errors, own_total, three, out, total):
    total[...] = own_total[...]
    add_tap_grads(total, fields, errors)
    for at in range(9):
        for kz in range(3):
            start = (at * 3 + kz) * 128
            done = 0
            while done < 128:
                piece, row = divmod(start + done, PIECE)
                size = min(PIECE - row, 128 - done)
                rows = slice(at * 128 + done, at * 128 + done + size)
                out[piece, row : row + size] = total[rows, kz * 128 : kz * 128 + 128].astype(BF16)
                done += size
    out[61, 40:PIECE] = jnp.zeros((PIECE - 40, 128), BF16)
    out[62:64, 0:PIECE] = jnp.zeros((2, PIECE, 128), BF16)
    out[:, PIECE : 2 * PIECE] = three[...]


def bottom_grads_kernel(core, own, other, out, total):
    for step, bundle in ((0, own), (1, other)):
        for row in range(2):
            fields = []
            for kx in range(3):
                for ky in range(3):
                    at = (row + kx) * 4 + ky
                    fields.append(bundle[at : at + 2].reshape(64, 128))
            at = 16 + row * 4
            errors = [
                jnp.concatenate([bundle[at + 2 * y], bundle[at + 2 * y + 1]], axis=1).reshape(1, 32, 256)
                for y in range(2)
            ]
            errors = jnp.concatenate(errors, axis=0).astype(F32)
            term = dot_tn(spread_errors(errors), jnp.concatenate(fields, axis=1))
            if step == 0 and row == 0:
                total[...] = term
            else:
                total[...] += term
    first_core = core[0] == 0
    out[48:64, 48:56] = jnp.zeros((16, 8, 128), BF16)
    for unit in range(27):
        at_x, rows = unit // 7, unit % 7 * 8
        at, kz = unit // 3, unit % 3
        block = total[kz * 256 : kz * 256 + 256, at * 128 : at * 128 + 128]
        block = block.reshape(16, 2, 8, 128)
        block = jnp.where(first_core, block[:, 0], block[:, 1]).astype(BF16)
        out[at_x * 16 : at_x * 16 + 16, rows : rows + 8] = block


def first_errors_kernel(core, own, before, after, left, right, taps_two, slope_one,
                        err_one, err_keep, err_send, padded, packed):
    fill_padded(padded, own, before, after, left, right)
    fill_backward(packed, taps_two)

    def step(row, _):
        product = dot_nt(window_rows(padded, row, 6), packed[...])
        back = join_taps(product, 6, 64, 128)
        err_one[row] = (back * slope_one[row].astype(F32)).astype(BF16)
        return 0

    lax.fori_loop(0, 6, step, 0)
    first_core = core[0] == 0
    for row in range(4):
        first, second = err_one[row + 1, 1:5], own[row]
        err_keep[row] = jnp.where(first_core, first, second)
        err_send[row] = jnp.where(first_core, second, first)


def input_kernel(err_one, taps_one, out, packed):
    fill_backward(packed, taps_one)

    def step(row, _):
        product = dot_nt(window_rows(err_one, row, 4), packed[...])
        out[row] = join_taps(product, 4, 64, 128).astype(BF16)
        return 0

    lax.fori_loop(0, 4, step, 0)


def sum_kernel(pieces, out, three):
    total = pieces[0].astype(F32)
    for at in range(1, 64):
        total = total + pieces[at].astype(F32)
    total = total.astype(BF16)
    three[...] = total[PIECE : 2 * PIECE]
    for at in range(64):
        out[at] = total[0:PIECE]


def place_kernel(chip, pair_0, pair_1, pair_2, pair_3, out, *, scale):
    for distance, pair in enumerate((pair_0, pair_1, pair_2, pair_3)):
        at = lax.rem(chip[0] + 4 - distance, 4)

        def put(rows, pair=pair, at=at):
            both = [pair[c, rows * 8 : rows * 8 + 8].astype(F32) * scale for c in range(2)]
            out[at * 7 + rows] = jnp.concatenate(both, axis=0)

        for rows in range(6):
            put(rows)
        pl.when(at < 3)(functools.partial(put, 6))


def finish_kernel(core, whole, other, grad_one, grad_two, *, scale):
    @pl.when(core[0] == 0)
    def _():
        grad_one[...] = whole[0:3456].astype(F32) * scale
        grad_two[...] = other[0:3456].astype(F32) * scale

    @pl.when(core[0] == 1)
    def _():
        grad_one[...] = other[0:3456].astype(F32) * scale
        grad_two[...] = whole[0:3456].astype(F32) * scale


def in_hbm(array):
    return pltpu.with_memory_space_constraint(array, pltpu.HBM)


def call(kernel, out_shapes, scratch, flops, *operands):
    shapes = [pltpu.HBM(*s[:2]) if s[2:] else jax.ShapeDtypeStruct(*s) for s in out_shapes]
    moved = sum(o.size * o.dtype.itemsize for o in operands)
    return pl.pallas_call(
        kernel,
        out_shape=shapes,
        in_specs=[
            pl.BlockSpec(memory_space=pltpu.SMEM if o.dtype == jnp.int32 else pltpu.VMEM) for o in operands
        ],
        out_specs=[pl.BlockSpec(memory_space=pltpu.VMEM)] * len(shapes),
        scratch_shapes=[pltpu.VMEM(s, d) for s, d in scratch],
        compiler_params=pltpu.CompilerParams(vmem_limit_bytes=18 << 20),
        cost_estimate=pl.CostEstimate(flops=flops // 20, bytes_accessed=moved // 20, transcendentals=0),
        name=kernel.__name__,
    )(*operands)


def on_device(features, skip_grad, bottom_grad, conv_one, conv_two, conv_three):
    core = lax.axis_index("c")
    first = jnp.concatenate([bottom_grad[:, :1, :, :128], bottom_grad[:, :1, :, 128:]], axis=2)
    last = jnp.concatenate([bottom_grad[:, 1:, :, :128], bottom_grad[:, 1:, :, 128:]], axis=2)
    first = jnp.concatenate([features[:, :2], first.reshape(1, 2, 64, 128)], axis=0)
    last = jnp.concatenate([features[:, -2:], last.reshape(1, 2, 64, 128)], axis=0)
    first, last, first_core, core_ref, chip = lax.optimization_barrier(
        (first, last, core == 0, core.reshape(1), lax.axis_index("x").reshape(1))
    )
    fine_cells = features.size // 128 * lax.axis_size(GX) * lax.axis_size(GY)
    fine_scale = 1.0 / math.sqrt(fine_cells)
    coarse_scale = 1.0 / math.sqrt(fine_cells // 8)
    taps_one = conv_one.reshape(27, 128, 128)
    taps_two = conv_two.reshape(27, 128, 128)
    taps_three = jnp.swapaxes(conv_three.reshape(27, 128, 16), 1, 2)
    taps_three = lax.all_gather(taps_three, GY, axis=1, tiled=True)

    f_before, f_after = shifted(last, GY, 1), shifted(first, GY, -1)
    low, high = call(
        first_slab_kernel, [((20, 64, 128), BF16)] * 2, [], 0, features, f_before, f_after, bottom_grad
    )
    f_left, f_right = exchange_x(low, high)

    conv_flops = 2 * 1152 * 128 * 1024 * 3
    field = (6, 6, 64, 128)
    block = (4, 4, 64, 128)
    edge = (4, 2, 64, 128)
    field_keep, field_send, slope_one, slope_two, pooled = call(
        forward_kernel,
        [(field, BF16, True), (field, BF16, True), (field, BF16, True), (block, BF16, True), ((2, 2, 32, 128), BF16)],
        [((8, 8, 64, 128), BF16), ((1152, 384), BF16), (field, BF16), ((4, 2, 64, 128), F32)],
        3 * conv_flops, core_ref, features, f_before, f_after, f_left, f_right, taps_one, taps_two,
    )
    field_other = swap_cores(field_send)
    p_pieces, _ = halo_pieces(pooled, 2, pooled, pooled)
    bottleneck, bundle, err_two, err_first, err_last = call(
        bottom_kernel,
        [((2, 2, 32, 256), BF16, True), ((24, 32, 128), BF16), (block, BF16), (edge, BF16), (edge, BF16)],
        [((6, 6, 32, 128), BF16), ((4, 4, 32, 256), BF16), ((768, 1152), BF16),
         ((4, 4, 32, 256), BF16), ((64, 128), F32)],
        conv_flops, *p_pieces, bottom_grad, f_before, f_after, f_left, f_right,
        in_hbm(taps_three), in_hbm(slope_two), in_hbm(skip_grad),
    )
    e_pieces, e_high = halo_pieces(err_two, 2, err_first, err_last)
    bundle, e_high = lax.optimization_barrier((bundle, e_high))
    (three,) = call(
        bottom_grads_kernel, [((64, PIECE, 128), BF16)], [((768, 1152), F32)],
        conv_flops // 2, core_ref, bundle, swap_cores(bundle),
    )
    three, *e_ends = lax.optimization_barrier((three, *e_pieces[3:]))
    err_one, err_keep, err_send = call(
        first_errors_kernel, [(field, BF16, True), (block, BF16), (block, BF16)],
        [((8, 8, 64, 128), BF16), ((384, 1152), BF16)],
        2 * conv_flops, core_ref, *e_pieces[:3], *e_ends, taps_two, slope_one,
    )
    err_other = swap_cores(err_send)
    (total,) = call(own_grads_kernel, [((1152, 384), F32)], [], conv_flops, field_keep, err_keep)
    (kept,) = call(
        pair_grads_kernel, [((64, 2 * PIECE, 128), BF16, True)], [((1152, 384), F32)],
        conv_flops, field_other, err_other, total, three,
    )
    part, three_part = call(
        sum_kernel, [((64, PIECE, 128), BF16, True), ((PIECE, 128), BF16)], [], 0,
        lax.all_to_all(kept, FLAT, 0, 0),
    )
    (input_grad,) = call(
        input_kernel, [(block, BF16, True)], [((384, 1152), BF16)],
        conv_flops, err_one, taps_one,
    )
    part, input_grad = lax.optimization_barrier((part, input_grad))
    whole = lax.all_to_all(part, FLAT, 0, 0).reshape(64 * PIECE, 128)
    both = swap_cores(three_part)
    both = jnp.where(first_core, jnp.stack([three_part, both]), jnp.stack([both, three_part]))
    grad_three = pl.pallas_call(
        functools.partial(place_kernel, scale=coarse_scale),
        out_shape=jax.ShapeDtypeStruct((27, 16, 128), F32),
        in_specs=[pl.BlockSpec(memory_space=pltpu.SMEM)] + [pl.BlockSpec(memory_space=pltpu.VMEM)] * 4,
        out_specs=pl.BlockSpec(memory_space=pltpu.VMEM),
        compiler_params=pltpu.CompilerParams(vmem_limit_bytes=8 << 20),
        name="place_kernel",
    )(chip, *ring_pieces([both] * 4, "x"))
    whole, grad_three = lax.optimization_barrier((whole, grad_three))
    grad_three = jnp.swapaxes(grad_three, 1, 2).reshape(3, 3, 3, 128, 16)
    grad_one, grad_two = pl.pallas_call(
        functools.partial(finish_kernel, scale=fine_scale),
        out_shape=[jax.ShapeDtypeStruct((3456, 128), F32)] * 2,
        in_specs=[pl.BlockSpec(memory_space=pltpu.SMEM)] + [pl.BlockSpec(memory_space=pltpu.VMEM)] * 2,
        out_specs=[pl.BlockSpec(memory_space=pltpu.VMEM)] * 2,
        compiler_params=pltpu.CompilerParams(vmem_limit_bytes=8 << 20),
        name="finish_kernel",
    )(core_ref, whole, swap_cores(whole))
    grad_one = grad_one.reshape(3, 3, 3, 128, 128)
    grad_two = grad_two.reshape(3, 3, 3, 128, 128)
    return (bottleneck, input_grad, grad_one, grad_two, grad_three)


def solution(mesh):
    fine = Mesh(mesh.devices.reshape(4, 2, 4, 4), ("x", "c", "z", "y"))
    cells = P(GX, GY, None, None)
    outs = P(None, None, None, None, GY)
    return jax.shard_map(
        on_device,
        mesh=fine,
        in_specs=(cells, cells, cells, P(), P(), outs),
        out_specs=(cells, cells, P(), P(), outs),
        check_vma=False,
    )
```

```python
import functools
import math

import jax
import jax.numpy as jnp
from jax import lax
from jax.experimental import pallas as pl
from jax.experimental.pallas import tpu as pltpu
from jax.sharding import Mesh
from jax.sharding import PartitionSpec as P

GX = ("x", "c")
GY = ("z", "y")
FLAT = ("x", "z", "y")
F32 = jnp.float32
BF16 = jnp.bfloat16
PIECE = 56


def shifted(array, axes, step):
    count = lax.axis_size(axes)
    return lax.ppermute(array, axes, [(i, (i + step) % count) for i in range(count)])


def swap_cores(array):
    return lax.ppermute(array, "c", [(0, 1), (1, 0)])


def ring_pieces(pieces, axis):
    sent = [lax.ppermute(pieces[d], axis, [(i, (i + d) % 4) for i in range(4)]) for d in (1, 2, 3)]
    return [pieces[0]] + sent


def slab_kernel(own, before, after, low, high):
    width, size_x = low.shape[0], own.shape[0]
    for slab, start in ((low, 0), (high, size_x - width)):
        rows = slice(start, start + width)
        columns = 0
        for part in (before, own, after):
            slab[:, columns : columns + part.shape[1]] = part[rows]
            columns += part.shape[1]


def first_slab_kernel(own, before, after, grads, low, high):
    for slab, start, row in ((low, 0, 0), (high, 2, 1)):
        for at in range(2):
            slab[at * 8 : at * 8 + 2] = before[start + at]
            slab[at * 8 + 2 : at * 8 + 6] = own[start + at]
            slab[at * 8 + 6 : at * 8 + 8] = after[start + at]
        slab[16] = before[4, row]
        slab[19] = after[4, row]
        for at_y in range(2):
            for half in range(2):
                part = grads[row, at_y, :, half * 128 : half * 128 + 128]
                slab[17 + at_y, half * 32 : half * 32 + 32] = part


def exchange_x(low, high):
    return shifted(high, GX, 1), shifted(low, GX, -1)


def halo_pieces(own, width, first, last):
    before, after = shifted(last, GY, 1), shifted(first, GY, -1)
    size_x, size_y, size_z, chans = own.shape
    slab = (width, size_y + 2 * width, size_z, chans)
    low, high = call(slab_kernel, [(slab, BF16)] * 2, [], 0, own, before, after)
    return (own, before, after, *exchange_x(low, high)), high


def fill_padded(padded, own, before, after, left, right):
    size_x, size_y = own.shape[0], own.shape[1]
    width = left.shape[0]
    padded[0:width] = left[...]
    padded[width + size_x : 2 * width + size_x] = right[...]
    middle = slice(width, width + size_x)
    padded[middle, 0:width] = before[...]
    padded[middle, width : width + size_y] = own[...]
    padded[middle, width + size_y : 2 * width + size_y] = after[...]


def slope_and_silu(values):
    sigma = 1.0 / (1.0 + jnp.exp(-values))
    return values * sigma, sigma * (1.0 + values * (1.0 - sigma))


def window_rows(source, row, count, skip=0):
    pieces = []
    for kx in range(3):
        for ky in range(3):
            block = source[row + kx + skip, ky + skip : ky + skip + count]
            pieces.append(block.reshape(block.shape[0] * block.shape[1], block.shape[2]))
    return jnp.concatenate(pieces, axis=1)


def roll_z(values, step):
    return pltpu.roll(values, step % values.shape[1], 1)


def join_taps(product, count, size_z, chans):
    parts = product.reshape(count, size_z, 3 * chans)
    return (
        roll_z(parts[:, :, 0:chans], 1)
        + parts[:, :, chans : 2 * chans]
        + roll_z(parts[:, :, 2 * chans : 3 * chans], -1)
    )


def spread_errors(errors):
    count, size_z, chans = errors.shape
    parts = [roll_z(errors, -1), errors, roll_z(errors, 1)]
    return jnp.concatenate([p.reshape(count * size_z, chans) for p in parts], axis=1).astype(BF16)


def fill_forward(packed, taps):
    for kx in range(3):
        for ky in range(3):
            for kz in range(3):
                at = kx * 3 + ky
                packed[at * 128 : at * 128 + 128, kz * 128 : kz * 128 + 128] = taps[at * 3 + kz]


def fill_backward(packed, taps):
    for kx in range(3):
        for ky in range(3):
            for kz in range(3):
                at = kx * 3 + ky
                packed[kz * 128 : kz * 128 + 128, at * 128 : at * 128 + 128] = taps[26 - at * 3 - kz]


def dot_nn(left, right):
    return lax.dot_general(left, right, (((1,), (0,)), ((), ())), preferred_element_type=F32)


def dot_nt(left, right):
    return lax.dot_general(left, right, (((1,), (1,)), ((), ())), preferred_element_type=F32)


def dot_tn(left, right):
    return lax.dot_general(left, right, (((0,), (0,)), ((), ())), preferred_element_type=F32)


def forward_kernel(core, own, before, after, left, right, taps_one, taps_two,
                   field_keep, field_send, slope_one, slope_two, pooled,
                   padded, packed, act_one, halves):
    for at in range(2):
        padded[at] = left[at * 8 : at * 8 + 8]
        padded[6 + at] = right[at * 8 : at * 8 + 8]
    padded[2:6, 0:2] = before[0:4]
    padded[2:6, 2:6] = own[...]
    padded[2:6, 6:8] = after[0:4]
    fill_forward(packed, taps_one)
    first_core = core[0] == 0

    def first(row, _):
        product = dot_nn(window_rows(padded, row, 6), packed[...])
        act, slope = slope_and_silu(join_taps(product, 6, 64, 128))
        act = act.astype(BF16)
        field = padded[row + 1, 1:7]
        act_one[row] = act
        field_keep[row] = jnp.where(first_core, field, act)
        field_send[row] = jnp.where(first_core, act, field)
        slope_one[row] = slope.astype(BF16)
        return 0

    lax.fori_loop(0, 6, first, 0)
    fill_forward(packed, taps_two)

    def second(row, _):
        product = dot_nn(window_rows(act_one, row, 4), packed[...])
        act, slope = slope_and_silu(join_taps(product, 4, 64, 128))
        slope_two[row] = slope.astype(BF16)
        act = act.astype(BF16).astype(F32)
        halves[row] = act.reshape(2, 2, 64, 128).sum(axis=1)
        return 0

    lax.fori_loop(0, 4, second, 0)
    for at_x in range(2):
        for at_y in range(2):
            total = 0.0
            for part in range(2):
                for start in range(2):
                    total = total + halves[2 * at_x + part, at_y, pl.ds(start, 32, stride=2), :]
            pooled[at_x, at_y] = (total * 0.125).astype(BF16)


def bottom_kernel(own, before, after, left, right, g_own, f_before, f_after, f_left, f_right,
                  taps_three, slope_two, skip, bottleneck, bundle, err_two, err_first, err_last,
                  padded, grads, packed, errors, wide):
    fill_padded(padded, own, before, after, left, right)
    for half in range(2):
        rows, lanes = slice(half * 32, half * 32 + 32), slice(half * 128, half * 128 + 128)
        grads[0, :, :, lanes] = f_left[16:20, rows]
        grads[3, :, :, lanes] = f_right[16:20, rows]
        for at in range(2):
            grads[1 + at, 0, :, lanes] = f_before[4, at, rows]
            grads[1 + at, 3, :, lanes] = f_after[4, at, rows]
    grads[1:3, 1:3] = g_own[...]
    for at in range(9):
        for kz in range(3):
            packed[kz * 256 : kz * 256 + 256, at * 128 : at * 128 + 128] = taps_three[at * 3 + kz]
    for row in range(4):
        product = dot_nt(window_rows(padded, row, 4), packed[...])
        act, slope = slope_and_silu(join_taps(product, 4, 32, 256))
        if row in (1, 2):
            bottleneck[row - 1] = act[1:3].astype(BF16)
        errs = (grads[row].astype(F32) * slope).astype(BF16)
        errors[row] = errs
        bundle[row * 4 : row * 4 + 4] = padded[row + 1, 1:5]
        if row in (1, 2):
            for at_y in range(2):
                for half in range(2):
                    at = 16 + ((row - 1) * 2 + at_y) * 2 + half
                    bundle[at] = errs[1 + at_y, :, half * 128 : half * 128 + 128]
    for row in range(2):
        total = jnp.zeros((64, 384), F32)
        for kx in range(3):
            for ky in range(3):
                block = errors[row + kx, ky : ky + 2].reshape(64, 256)
                at = kx * 3 + ky
                back = jnp.concatenate(
                    [taps_three[26 - at * 3 - kz] for kz in range(3)], axis=1
                )
                total = total + dot_nn(block, back)
        upward = join_taps(total, 2, 32, 128) * 0.125
        for at_y in range(2):
            wide[pl.ds(0, 32, stride=2), :] = upward[at_y]
            wide[pl.ds(1, 32, stride=2), :] = upward[at_y]
            for dx in range(2):
                for dy in range(2):
                    at = (2 * row + dx, 2 * at_y + dy)
                    err = skip[at].astype(F32) + wide[...]
                    err = (err * slope_two[at].astype(F32)).astype(BF16)
                    err_two[at] = err
                    edge = err_first if at_y == 0 else err_last
                    edge[2 * row + dx, dy] = err


def add_tap_grads(total, fields, errors):
    def step(row, _):
        total[...] += dot_tn(window_rows(fields, row, 4), spread_errors(errors[row].astype(F32)))
        return 0

    lax.fori_loop(0, 4, step, 0)


def own_grads_kernel(fields, errors, total):
    total[...] = jnp.zeros_like(total)
    add_tap_grads(total, fields, errors)


def pair_grads_kernel(fields, errors, own_total, three, out, total):
    total[...] = own_total[...]
    add_tap_grads(total, fields, errors)
    for at in range(9):
        for kz in range(3):
            start = (at * 3 + kz) * 128
            done = 0
            while done < 128:
                piece, row = divmod(start + done, PIECE)
                size = min(PIECE - row, 128 - done)
                rows = slice(at * 128 + done, at * 128 + done + size)
                out[piece, row : row + size] = total[rows, kz * 128 : kz * 128 + 128].astype(BF16)
                done += size
    out[61, 40:PIECE] = jnp.zeros((PIECE - 40, 128), BF16)
    out[62:64, 0:PIECE] = jnp.zeros((2, PIECE, 128), BF16)
    out[:, PIECE : 2 * PIECE] = three[...]


def bottom_grads_kernel(core, own, other, out, total):
    for step, bundle in ((0, own), (1, other)):
        for row in range(2):
            fields = []
            for kx in range(3):
                for ky in range(3):
                    at = (row + kx) * 4 + ky
                    fields.append(bundle[at : at + 2].reshape(64, 128))
            at = 16 + row * 4
            errors = [
                jnp.concatenate([bundle[at + 2 * y], bundle[at + 2 * y + 1]], axis=1).reshape(1, 32, 256)
                for y in range(2)
            ]
            errors = jnp.concatenate(errors, axis=0).astype(F32)
            term = dot_tn(spread_errors(errors), jnp.concatenate(fields, axis=1))
            if step == 0 and row == 0:
                total[...] = term
            else:
                total[...] += term
    first_core = core[0] == 0
    out[48:64, 48:56] = jnp.zeros((16, 8, 128), BF16)
    for unit in range(27):
        at_x, rows = unit // 7, unit % 7 * 8
        at, kz = unit // 3, unit % 3
        block = total[kz * 256 : kz * 256 + 256, at * 128 : at * 128 + 128]
        block = block.reshape(16, 2, 8, 128)
        block = jnp.where(first_core, block[:, 0], block[:, 1]).astype(BF16)
        out[at_x * 16 : at_x * 16 + 16, rows : rows + 8] = block


def first_errors_kernel(core, own, before, after, left, right, taps_two, slope_one,
                        err_one, err_keep, err_send, padded, packed):
    fill_padded(padded, own, before, after, left, right)
    fill_backward(packed, taps_two)

    def step(row, _):
        product = dot_nt(window_rows(padded, row, 6), packed[...])
        back = join_taps(product, 6, 64, 128)
        err_one[row] = (back * slope_one[row].astype(F32)).astype(BF16)
        return 0

    lax.fori_loop(0, 6, step, 0)
    first_core = core[0] == 0
    for row in range(4):
        first, second = err_one[row + 1, 1:5], own[row]
        err_keep[row] = jnp.where(first_core, first, second)
        err_send[row] = jnp.where(first_core, second, first)


def input_kernel(err_one, taps_one, out, packed):
    fill_backward(packed, taps_one)

    def step(row, _):
        product = dot_nt(window_rows(err_one, row, 4), packed[...])
        out[row] = join_taps(product, 4, 64, 128).astype(BF16)
        return 0

    lax.fori_loop(0, 4, step, 0)


def sum_kernel(pieces, out, three):
    total = pieces[0].astype(F32)
    for at in range(1, 64):
        total = total + pieces[at].astype(F32)
    total = total.astype(BF16)
    three[...] = total[PIECE : 2 * PIECE]
    for at in range(64):
        out[at] = total[0:PIECE]


def place_kernel(chip, pair_0, pair_1, pair_2, pair_3, out, *, scale):
    for distance, pair in enumerate((pair_0, pair_1, pair_2, pair_3)):
        at = lax.rem(chip[0] + 4 - distance, 4)

        def put(rows, pair=pair, at=at):
            both = [pair[c, rows * 8 : rows * 8 + 8].astype(F32) * scale for c in range(2)]
            out[at * 7 + rows] = jnp.concatenate(both, axis=0)

        for rows in range(6):
            put(rows)
        pl.when(at < 3)(functools.partial(put, 6))


def finish_kernel(core, whole, other, grad_one, grad_two, *, scale):
    @pl.when(core[0] == 0)
    def _():
        grad_one[...] = whole[0:3456].astype(F32) * scale
        grad_two[...] = other[0:3456].astype(F32) * scale

    @pl.when(core[0] == 1)
    def _():
        grad_one[...] = other[0:3456].astype(F32) * scale
        grad_two[...] = whole[0:3456].astype(F32) * scale


def in_hbm(array):
    return pltpu.with_memory_space_constraint(array, pltpu.HBM)


def call(kernel, out_shapes, scratch, flops, *operands):
    shapes = [pltpu.HBM(*s[:2]) if s[2:] else jax.ShapeDtypeStruct(*s) for s in out_shapes]
    moved = sum(o.size * o.dtype.itemsize for o in operands)
    return pl.pallas_call(
        kernel,
        out_shape=shapes,
        in_specs=[
            pl.BlockSpec(memory_space=pltpu.SMEM if o.dtype == jnp.int32 else pltpu.VMEM) for o in operands
        ],
        out_specs=[pl.BlockSpec(memory_space=pltpu.VMEM)] * len(shapes),
        scratch_shapes=[pltpu.VMEM(s, d) for s, d in scratch],
        compiler_params=pltpu.CompilerParams(vmem_limit_bytes=18 << 20),
        cost_estimate=pl.CostEstimate(flops=flops // 20, bytes_accessed=moved // 20, transcendentals=0),
        name=kernel.__name__,
    )(*operands)


def on_device(features, skip_grad, bottom_grad, conv_one, conv_two, conv_three):
    core = lax.axis_index("c")
    first = jnp.concatenate([bottom_grad[:, :1, :, :128], bottom_grad[:, :1, :, 128:]], axis=2)
    last = jnp.concatenate([bottom_grad[:, 1:, :, :128], bottom_grad[:, 1:, :, 128:]], axis=2)
    first = jnp.concatenate([features[:, :2], first.reshape(1, 2, 64, 128)], axis=0)
    last = jnp.concatenate([features[:, -2:], last.reshape(1, 2, 64, 128)], axis=0)
    first, last, first_core, core_ref, chip = lax.optimization_barrier(
        (first, last, core == 0, core.reshape(1), lax.axis_index("x").reshape(1))
    )
    fine_cells = features.size // 128 * lax.axis_size(GX) * lax.axis_size(GY)
    fine_scale = 1.0 / math.sqrt(fine_cells)
    coarse_scale = 1.0 / math.sqrt(fine_cells // 8)
    taps_one = conv_one.reshape(27, 128, 128)
    taps_two = conv_two.reshape(27, 128, 128)
    half_taps = jnp.swapaxes(conv_three.reshape(27, 128, 16), 1, 2).reshape(27, 2, 8, 128)
    half_taps = jnp.where(first_core, half_taps[:, 0], half_taps[:, 1])
    mine = lax.all_to_all(jnp.broadcast_to(half_taps, (16, 27, 8, 128)), GY, 0, 0)

    f_before, f_after = shifted(last, GY, 1), shifted(first, GY, -1)
    low, high = call(
        first_slab_kernel, [((20, 64, 128), BF16)] * 2, [], 0, features, f_before, f_after, bottom_grad
    )
    f_left, f_right = exchange_x(low, high)

    conv_flops = 2 * 1152 * 128 * 1024 * 3
    field = (6, 6, 64, 128)
    block = (4, 4, 64, 128)
    edge = (4, 2, 64, 128)
    field_keep, field_send, slope_one, slope_two, pooled = call(
        forward_kernel,
        [(field, BF16, True), (field, BF16, True), (field, BF16, True), (block, BF16, True), ((2, 2, 32, 128), BF16)],
        [((8, 8, 64, 128), BF16), ((1152, 384), BF16), (field, BF16), ((4, 2, 64, 128), F32)],
        3 * conv_flops, core_ref, features, f_before, f_after, f_left, f_right, taps_one, taps_two,
    )
    field_other = swap_cores(field_send)
    mine, pooled = lax.optimization_barrier((mine, pooled))
    theirs = swap_cores(mine)
    both = jnp.where(first_core, jnp.stack([mine, theirs]), jnp.stack([theirs, mine]))
    taps_three = jnp.transpose(both, (2, 1, 0, 3, 4)).reshape(27, 256, 128)
    p_pieces, _ = halo_pieces(pooled, 2, pooled, pooled)
    bottleneck, bundle, err_two, err_first, err_last = call(
        bottom_kernel,
        [((2, 2, 32, 256), BF16, True), ((24, 32, 128), BF16), (block, BF16), (edge, BF16), (edge, BF16)],
        [((6, 6, 32, 128), BF16), ((4, 4, 32, 256), BF16), ((768, 1152), BF16),
         ((4, 4, 32, 256), BF16), ((64, 128), F32)],
        conv_flops, *p_pieces, bottom_grad, f_before, f_after, f_left, f_right,
        taps_three, in_hbm(slope_two), in_hbm(skip_grad),
    )
    e_pieces, e_high = halo_pieces(err_two, 2, err_first, err_last)
    bundle, e_high = lax.optimization_barrier((bundle, e_high))
    (three,) = call(
        bottom_grads_kernel, [((64, PIECE, 128), BF16)], [((768, 1152), F32)],
        conv_flops // 2, core_ref, bundle, swap_cores(bundle),
    )
    three, *e_ends = lax.optimization_barrier((three, *e_pieces[3:]))
    err_one, err_keep, err_send = call(
        first_errors_kernel, [(field, BF16, True), (block, BF16), (block, BF16)],
        [((8, 8, 64, 128), BF16), ((384, 1152), BF16)],
        2 * conv_flops, core_ref, *e_pieces[:3], *e_ends, taps_two, slope_one,
    )
    err_other = swap_cores(err_send)
    (total,) = call(own_grads_kernel, [((1152, 384), F32)], [], conv_flops, field_keep, err_keep)
    (kept,) = call(
        pair_grads_kernel, [((64, 2 * PIECE, 128), BF16, True)], [((1152, 384), F32)],
        conv_flops, field_other, err_other, total, three,
    )
    part, three_part = call(
        sum_kernel, [((64, PIECE, 128), BF16, True), ((PIECE, 128), BF16)], [], 0,
        lax.all_to_all(kept, FLAT, 0, 0),
    )
    (input_grad,) = call(
        input_kernel, [(block, BF16, True)], [((384, 1152), BF16)],
        conv_flops, err_one, taps_one,
    )
    part, input_grad = lax.optimization_barrier((part, input_grad))
    whole = lax.all_to_all(part, FLAT, 0, 0).reshape(64 * PIECE, 128)
    both = swap_cores(three_part)
    both = jnp.where(first_core, jnp.stack([three_part, both]), jnp.stack([both, three_part]))
    grad_three = pl.pallas_call(
        functools.partial(place_kernel, scale=coarse_scale),
        out_shape=jax.ShapeDtypeStruct((27, 16, 128), F32),
        in_specs=[pl.BlockSpec(memory_space=pltpu.SMEM)] + [pl.BlockSpec(memory_space=pltpu.VMEM)] * 4,
        out_specs=pl.BlockSpec(memory_space=pltpu.VMEM),
        compiler_params=pltpu.CompilerParams(vmem_limit_bytes=8 << 20),
        name="place_kernel",
    )(chip, *ring_pieces([both] * 4, "x"))
    whole, grad_three = lax.optimization_barrier((whole, grad_three))
    grad_three = jnp.swapaxes(grad_three, 1, 2).reshape(3, 3, 3, 128, 16)
    grad_one, grad_two = pl.pallas_call(
        functools.partial(finish_kernel, scale=fine_scale),
        out_shape=[jax.ShapeDtypeStruct((3456, 128), F32)] * 2,
        in_specs=[pl.BlockSpec(memory_space=pltpu.SMEM)] + [pl.BlockSpec(memory_space=pltpu.VMEM)] * 2,
        out_specs=[pl.BlockSpec(memory_space=pltpu.VMEM)] * 2,
        compiler_params=pltpu.CompilerParams(vmem_limit_bytes=8 << 20),
        name="finish_kernel",
    )(core_ref, whole, swap_cores(whole))
    grad_one = grad_one.reshape(3, 3, 3, 128, 128)
    grad_two = grad_two.reshape(3, 3, 3, 128, 128)
    return (bottleneck, input_grad, grad_one, grad_two, grad_three)


def solution(mesh):
    fine = Mesh(mesh.devices.reshape(4, 2, 4, 4), ("x", "c", "z", "y"))
    cells = P(GX, GY, None, None)
    outs = P(None, None, None, None, GY)
    return jax.shard_map(
        on_device,
        mesh=fine,
        in_specs=(cells, cells, cells, P(), P(), outs),
        out_specs=(cells, cells, P(), P(), outs),
        check_vma=False,
    )
```

```python
import functools
import math

import jax
import jax.numpy as jnp
from jax import lax
from jax.experimental import pallas as pl
from jax.experimental.pallas import tpu as pltpu
from jax.sharding import Mesh
from jax.sharding import PartitionSpec as P

GX = ("x", "c")
GY = ("z", "y")
FLAT = ("x", "z", "y")
F32 = jnp.float32
BF16 = jnp.bfloat16
PIECE = 56


def shifted(array, axes, step):
    count = lax.axis_size(axes)
    return lax.ppermute(array, axes, [(i, (i + step) % count) for i in range(count)])


def swap_cores(array):
    return lax.ppermute(array, "c", [(0, 1), (1, 0)])


def ring_pieces(pieces, axis):
    sent = [lax.ppermute(pieces[d], axis, [(i, (i + d) % 4) for i in range(4)]) for d in (1, 2, 3)]
    return [pieces[0]] + sent


def slab_kernel(own, before, after, low, high):
    width, size_x = low.shape[0], own.shape[0]
    for slab, start in ((low, 0), (high, size_x - width)):
        rows = slice(start, start + width)
        columns = 0
        for part in (before, own, after):
            slab[:, columns : columns + part.shape[1]] = part[rows]
            columns += part.shape[1]


def first_slab_kernel(own, before, after, grads, low, high):
    for slab, start, row in ((low, 0, 0), (high, 2, 1)):
        for at in range(2):
            slab[at * 8 : at * 8 + 2] = before[start + at]
            slab[at * 8 + 2 : at * 8 + 6] = own[start + at]
            slab[at * 8 + 6 : at * 8 + 8] = after[start + at]
        slab[16] = before[4, row]
        slab[19] = after[4, row]
        for at_y in range(2):
            for half in range(2):
                part = grads[row, at_y, :, half * 128 : half * 128 + 128]
                slab[17 + at_y, half * 32 : half * 32 + 32] = part


def exchange_x(low, high):
    return shifted(high, GX, 1), shifted(low, GX, -1)


def halo_pieces(own, width, first, last):
    before, after = shifted(last, GY, 1), shifted(first, GY, -1)
    size_x, size_y, size_z, chans = own.shape
    slab = (width, size_y + 2 * width, size_z, chans)
    low, high = call(slab_kernel, [(slab, BF16)] * 2, [], 0, own, before, after)
    return (own, before, after, *exchange_x(low, high)), high


def fill_padded(padded, own, before, after, left, right):
    size_x, size_y = own.shape[0], own.shape[1]
    width = left.shape[0]
    padded[0:width] = left[...]
    padded[width + size_x : 2 * width + size_x] = right[...]
    middle = slice(width, width + size_x)
    padded[middle, 0:width] = before[...]
    padded[middle, width : width + size_y] = own[...]
    padded[middle, width + size_y : 2 * width + size_y] = after[...]


def slope_and_silu(values):
    sigma = 1.0 / (1.0 + jnp.exp(-values))
    return values * sigma, sigma * (1.0 + values * (1.0 - sigma))


def window_rows(source, row, count, skip=0):
    pieces = []
    for kx in range(3):
        for ky in range(3):
            block = source[row + kx + skip, ky + skip : ky + skip + count]
            pieces.append(block.reshape(block.shape[0] * block.shape[1], block.shape[2]))
    return jnp.concatenate(pieces, axis=1)


def roll_z(values, step):
    return pltpu.roll(values, step % values.shape[1], 1)


def join_taps(product, count, size_z, chans):
    parts = product.reshape(count, size_z, 3 * chans)
    return (
        roll_z(parts[:, :, 0:chans], 1)
        + parts[:, :, chans : 2 * chans]
        + roll_z(parts[:, :, 2 * chans : 3 * chans], -1)
    )


def spread_errors(errors):
    count, size_z, chans = errors.shape
    parts = [roll_z(errors, -1), errors, roll_z(errors, 1)]
    return jnp.concatenate([p.reshape(count * size_z, chans) for p in parts], axis=1).astype(BF16)


def fill_forward(packed, taps):
    for kx in range(3):
        for ky in range(3):
            for kz in range(3):
                at = kx * 3 + ky
                packed[at * 128 : at * 128 + 128, kz * 128 : kz * 128 + 128] = taps[at * 3 + kz]


def fill_backward(packed, taps):
    for kx in range(3):
        for ky in range(3):
            for kz in range(3):
                at = kx * 3 + ky
                packed[kz * 128 : kz * 128 + 128, at * 128 : at * 128 + 128] = taps[26 - at * 3 - kz]


def dot_nn(left, right):
    return lax.dot_general(left, right, (((1,), (0,)), ((), ())), preferred_element_type=F32)


def dot_nt(left, right):
    return lax.dot_general(left, right, (((1,), (1,)), ((), ())), preferred_element_type=F32)


def dot_tn(left, right):
    return lax.dot_general(left, right, (((0,), (0,)), ((), ())), preferred_element_type=F32)


def forward_kernel(core, own, before, after, left, right, taps_one, taps_two,
                   field_keep, field_send, slope_one, slope_two, pooled,
                   padded, packed, act_one, halves):
    for at in range(2):
        padded[at] = left[at * 8 : at * 8 + 8]
        padded[6 + at] = right[at * 8 : at * 8 + 8]
    padded[2:6, 0:2] = before[0:4]
    padded[2:6, 2:6] = own[...]
    padded[2:6, 6:8] = after[0:4]
    fill_forward(packed, taps_one)
    first_core = core[0] == 0

    def first(row, _):
        product = dot_nn(window_rows(padded, row, 6), packed[...])
        act, slope = slope_and_silu(join_taps(product, 6, 64, 128))
        act = act.astype(BF16)
        field = padded[row + 1, 1:7]
        act_one[row] = act
        field_keep[row] = jnp.where(first_core, field, act)
        field_send[row] = jnp.where(first_core, act, field)
        slope_one[row] = slope.astype(BF16)
        return 0

    lax.fori_loop(0, 6, first, 0)
    fill_forward(packed, taps_two)

    def second(row, _):
        product = dot_nn(window_rows(act_one, row, 4), packed[...])
        act, slope = slope_and_silu(join_taps(product, 4, 64, 128))
        slope_two[row] = slope.astype(BF16)
        act = act.astype(BF16).astype(F32)
        halves[row] = act.reshape(2, 2, 64, 128).sum(axis=1)
        return 0

    lax.fori_loop(0, 4, second, 0)
    for at_x in range(2):
        for at_y in range(2):
            total = 0.0
            for part in range(2):
                for start in range(2):
                    total = total + halves[2 * at_x + part, at_y, pl.ds(start, 32, stride=2), :]
            pooled[at_x, at_y] = (total * 0.125).astype(BF16)


def bottom_kernel(own, before, after, left, right, g_own, f_before, f_after, f_left, f_right,
                  taps_three, slope_two, skip, bottleneck, bundle, err_two, err_first, err_last,
                  padded, grads, packed, errors, wide):
    fill_padded(padded, own, before, after, left, right)
    for half in range(2):
        rows, lanes = slice(half * 32, half * 32 + 32), slice(half * 128, half * 128 + 128)
        grads[0, :, :, lanes] = f_left[16:20, rows]
        grads[3, :, :, lanes] = f_right[16:20, rows]
        for at in range(2):
            grads[1 + at, 0, :, lanes] = f_before[4, at, rows]
            grads[1 + at, 3, :, lanes] = f_after[4, at, rows]
    grads[1:3, 1:3] = g_own[...]
    for at in range(9):
        for kz in range(3):
            packed[kz * 256 : kz * 256 + 256, at * 128 : at * 128 + 128] = taps_three[at * 3 + kz]
    for row in range(4):
        product = dot_nt(window_rows(padded, row, 4), packed[...])
        act, slope = slope_and_silu(join_taps(product, 4, 32, 256))
        if row in (1, 2):
            bottleneck[row - 1] = act[1:3].astype(BF16)
        errs = (grads[row].astype(F32) * slope).astype(BF16)
        errors[row] = errs
        bundle[row * 4 : row * 4 + 4] = padded[row + 1, 1:5]
        if row in (1, 2):
            for at_y in range(2):
                for half in range(2):
                    at = 16 + ((row - 1) * 2 + at_y) * 2 + half
                    bundle[at] = errs[1 + at_y, :, half * 128 : half * 128 + 128]
    for row in range(2):
        total = jnp.zeros((64, 384), F32)
        for kx in range(3):
            for ky in range(3):
                block = errors[row + kx, ky : ky + 2].reshape(64, 256)
                at = kx * 3 + ky
                back = jnp.concatenate(
                    [taps_three[26 - at * 3 - kz] for kz in range(3)], axis=1
                )
                total = total + dot_nn(block, back)
        upward = join_taps(total, 2, 32, 128) * 0.125
        for at_y in range(2):
            wide[pl.ds(0, 32, stride=2), :] = upward[at_y]
            wide[pl.ds(1, 32, stride=2), :] = upward[at_y]
            for dx in range(2):
                for dy in range(2):
                    at = (2 * row + dx, 2 * at_y + dy)
                    err = skip[at].astype(F32) + wide[...]
                    err = (err * slope_two[at].astype(F32)).astype(BF16)
                    err_two[at] = err
                    edge = err_first if at_y == 0 else err_last
                    edge[2 * row + dx, dy] = err


def add_tap_grads(total, fields, errors):
    def step(row, _):
        total[...] += dot_tn(window_rows(fields, row, 4), spread_errors(errors[row].astype(F32)))
        return 0

    lax.fori_loop(0, 4, step, 0)


def own_grads_kernel(fields, errors, total):
    total[...] = jnp.zeros_like(total)
    add_tap_grads(total, fields, errors)


def pair_grads_kernel(fields, errors, own_total, three, out, total):
    total[...] = own_total[...]
    add_tap_grads(total, fields, errors)
    for at in range(9):
        for kz in range(3):
            start = (at * 3 + kz) * 128
            done = 0
            while done < 128:
                piece, row = divmod(start + done, PIECE)
                size = min(PIECE - row, 128 - done)
                rows = slice(at * 128 + done, at * 128 + done + size)
                out[piece, row : row + size] = total[rows, kz * 128 : kz * 128 + 128].astype(BF16)
                done += size
    out[61, 40:PIECE] = jnp.zeros((PIECE - 40, 128), BF16)
    out[62:64, 0:PIECE] = jnp.zeros((2, PIECE, 128), BF16)
    out[:, PIECE : 2 * PIECE] = three[...]


def bottom_grads_kernel(core, own, other, out, total):
    for step, bundle in ((0, own), (1, other)):
        for row in range(2):
            fields = []
            for kx in range(3):
                for ky in range(3):
                    at = (row + kx) * 4 + ky
                    fields.append(bundle[at : at + 2].reshape(64, 128))
            at = 16 + row * 4
            errors = [
                jnp.concatenate([bundle[at + 2 * y], bundle[at + 2 * y + 1]], axis=1).reshape(1, 32, 256)
                for y in range(2)
            ]
            errors = jnp.concatenate(errors, axis=0).astype(F32)
            term = dot_tn(spread_errors(errors), jnp.concatenate(fields, axis=1))
            if step == 0 and row == 0:
                total[...] = term
            else:
                total[...] += term
    first_core = core[0] == 0
    out[48:64, 48:56] = jnp.zeros((16, 8, 128), BF16)
    for unit in range(27):
        at_x, rows = unit // 7, unit % 7 * 8
        at, kz = unit // 3, unit % 3
        block = total[kz * 256 : kz * 256 + 256, at * 128 : at * 128 + 128]
        block = block.reshape(16, 2, 8, 128)
        block = jnp.where(first_core, block[:, 0], block[:, 1]).astype(BF16)
        out[at_x * 16 : at_x * 16 + 16, rows : rows + 8] = block


def first_errors_kernel(core, own, before, after, left, right, taps_two, slope_one,
                        err_one, err_keep, err_send, padded, packed):
    fill_padded(padded, own, before, after, left, right)
    fill_backward(packed, taps_two)

    def step(row, _):
        product = dot_nt(window_rows(padded, row, 6), packed[...])
        back = join_taps(product, 6, 64, 128)
        err_one[row] = (back * slope_one[row].astype(F32)).astype(BF16)
        return 0

    lax.fori_loop(0, 6, step, 0)
    first_core = core[0] == 0
    for row in range(4):
        first, second = err_one[row + 1, 1:5], own[row]
        err_keep[row] = jnp.where(first_core, first, second)
        err_send[row] = jnp.where(first_core, second, first)


def input_kernel(err_one, taps_one, out, packed):
    fill_backward(packed, taps_one)

    def step(row, _):
        product = dot_nt(window_rows(err_one, row, 4), packed[...])
        out[row] = join_taps(product, 4, 64, 128).astype(BF16)
        return 0

    lax.fori_loop(0, 4, step, 0)


def sum_kernel(pieces, out, three):
    total = pieces[0].astype(F32)
    for at in range(1, 64):
        total = total + pieces[at].astype(F32)
    total = total.astype(BF16)
    three[...] = total[PIECE : 2 * PIECE]
    for at in range(64):
        out[at] = total[0:PIECE]


def place_kernel(chip, pair_0, pair_1, pair_2, pair_3, out, *, scale):
    for distance, pair in enumerate((pair_0, pair_1, pair_2, pair_3)):
        at = lax.rem(chip[0] + 4 - distance, 4)

        def put(rows, pair=pair, at=at):
            both = [pair[c, rows * 8 : rows * 8 + 8].astype(F32) * scale for c in range(2)]
            out[at * 7 + rows] = jnp.concatenate(both, axis=0)

        for rows in range(6):
            put(rows)
        pl.when(at < 3)(functools.partial(put, 6))


def finish_kernel(core, whole, other, grad_one, grad_two, *, scale):
    @pl.when(core[0] == 0)
    def _():
        grad_one[...] = whole[0:3456].astype(F32) * scale
        grad_two[...] = other[0:3456].astype(F32) * scale

    @pl.when(core[0] == 1)
    def _():
        grad_one[...] = other[0:3456].astype(F32) * scale
        grad_two[...] = whole[0:3456].astype(F32) * scale


def in_hbm(array):
    return pltpu.with_memory_space_constraint(array, pltpu.HBM)


def call(kernel, out_shapes, scratch, flops, *operands):
    shapes = [pltpu.HBM(*s[:2]) if s[2:] else jax.ShapeDtypeStruct(*s) for s in out_shapes]
    moved = sum(o.size * o.dtype.itemsize for o in operands)
    return pl.pallas_call(
        kernel,
        out_shape=shapes,
        in_specs=[
            pl.BlockSpec(memory_space=pltpu.SMEM if o.dtype == jnp.int32 else pltpu.VMEM) for o in operands
        ],
        out_specs=[pl.BlockSpec(memory_space=pltpu.VMEM)] * len(shapes),
        scratch_shapes=[pltpu.VMEM(s, d) for s, d in scratch],
        compiler_params=pltpu.CompilerParams(vmem_limit_bytes=18 << 20),
        cost_estimate=pl.CostEstimate(flops=flops // 20, bytes_accessed=moved // 20, transcendentals=0),
        name=kernel.__name__,
    )(*operands)


def on_device(features, skip_grad, bottom_grad, conv_one, conv_two, conv_three):
    core = lax.axis_index("c")
    first = jnp.concatenate([bottom_grad[:, :1, :, :128], bottom_grad[:, :1, :, 128:]], axis=2)
    last = jnp.concatenate([bottom_grad[:, 1:, :, :128], bottom_grad[:, 1:, :, 128:]], axis=2)
    first = jnp.concatenate([features[:, :2], first.reshape(1, 2, 64, 128)], axis=0)
    last = jnp.concatenate([features[:, -2:], last.reshape(1, 2, 64, 128)], axis=0)
    first, last, first_core, core_ref, chip = lax.optimization_barrier(
        (first, last, core == 0, core.reshape(1), lax.axis_index("x").reshape(1))
    )
    fine_cells = features.size // 128 * lax.axis_size(GX) * lax.axis_size(GY)
    fine_scale = 1.0 / math.sqrt(fine_cells)
    coarse_scale = 1.0 / math.sqrt(fine_cells // 8)
    taps_one = conv_one.reshape(27, 128, 128)
    taps_two = conv_two.reshape(27, 128, 128)
    half_taps = jnp.swapaxes(conv_three.reshape(27, 128, 16), 1, 2).reshape(27, 2, 8, 128)
    half_taps = jnp.where(first_core, half_taps[:, 0], half_taps[:, 1])
    mine = lax.all_to_all(jnp.broadcast_to(half_taps, (16, 27, 8, 128)), GY, 0, 0)

    f_before, f_after = shifted(last, GY, 1), shifted(first, GY, -1)
    low, high = call(
        first_slab_kernel, [((20, 64, 128), BF16)] * 2, [], 4 * 10**11,
        features, f_before, f_after, bottom_grad,
    )
    f_left, f_right = exchange_x(low, high)

    conv_flops = 2 * 1152 * 128 * 1024 * 3
    field = (6, 6, 64, 128)
    block = (4, 4, 64, 128)
    edge = (4, 2, 64, 128)
    field_keep, field_send, slope_one, slope_two, pooled = call(
        forward_kernel,
        [(field, BF16, True), (field, BF16, True), (field, BF16, True), (block, BF16, True), ((2, 2, 32, 128), BF16)],
        [((8, 8, 64, 128), BF16), ((1152, 384), BF16), (field, BF16), ((4, 2, 64, 128), F32)],
        3 * conv_flops, core_ref, features, f_before, f_after, f_left, f_right, taps_one, taps_two,
    )
    field_other = swap_cores(field_send)
    mine, pooled = lax.optimization_barrier((mine, pooled))
    theirs = swap_cores(mine)
    both = jnp.where(first_core, jnp.stack([mine, theirs]), jnp.stack([theirs, mine]))
    taps_three = jnp.transpose(both, (2, 1, 0, 3, 4)).reshape(27, 256, 128)
    p_pieces, _ = halo_pieces(pooled, 2, pooled, pooled)
    bottleneck, bundle, err_two, err_first, err_last = call(
        bottom_kernel,
        [((2, 2, 32, 256), BF16, True), ((24, 32, 128), BF16), (block, BF16), (edge, BF16), (edge, BF16)],
        [((6, 6, 32, 128), BF16), ((4, 4, 32, 256), BF16), ((768, 1152), BF16),
         ((4, 4, 32, 256), BF16), ((64, 128), F32)],
        conv_flops, *p_pieces, bottom_grad, f_before, f_after, f_left, f_right,
        taps_three, in_hbm(slope_two), in_hbm(skip_grad),
    )
    e_pieces, e_high = halo_pieces(err_two, 2, err_first, err_last)
    bundle, e_high = lax.optimization_barrier((bundle, e_high))
    (three,) = call(
        bottom_grads_kernel, [((64, PIECE, 128), BF16)], [((768, 1152), F32)],
        conv_flops // 2, core_ref, bundle, swap_cores(bundle),
    )
    three, *e_ends = lax.optimization_barrier((three, *e_pieces[3:]))
    err_one, err_keep, err_send = call(
        first_errors_kernel, [(field, BF16, True), (block, BF16), (block, BF16)],
        [((8, 8, 64, 128), BF16), ((384, 1152), BF16)],
        2 * conv_flops, core_ref, *e_pieces[:3], *e_ends, taps_two, slope_one,
    )
    err_other = swap_cores(err_send)
    (total,) = call(own_grads_kernel, [((1152, 384), F32)], [], conv_flops, field_keep, err_keep)
    (kept,) = call(
        pair_grads_kernel, [((64, 2 * PIECE, 128), BF16, True)], [((1152, 384), F32)],
        conv_flops, field_other, err_other, total, three,
    )
    part, three_part = call(
        sum_kernel, [((64, PIECE, 128), BF16, True), ((PIECE, 128), BF16)], [], 0,
        lax.all_to_all(kept, FLAT, 0, 0),
    )
    (input_grad,) = call(
        input_kernel, [(block, BF16, True)], [((384, 1152), BF16)],
        conv_flops, err_one, taps_one,
    )
    part, input_grad = lax.optimization_barrier((part, input_grad))
    whole = lax.all_to_all(part, FLAT, 0, 0).reshape(64 * PIECE, 128)
    both = swap_cores(three_part)
    both = jnp.where(first_core, jnp.stack([three_part, both]), jnp.stack([both, three_part]))
    grad_three = pl.pallas_call(
        functools.partial(place_kernel, scale=coarse_scale),
        out_shape=jax.ShapeDtypeStruct((27, 16, 128), F32),
        in_specs=[pl.BlockSpec(memory_space=pltpu.SMEM)] + [pl.BlockSpec(memory_space=pltpu.VMEM)] * 4,
        out_specs=pl.BlockSpec(memory_space=pltpu.VMEM),
        compiler_params=pltpu.CompilerParams(vmem_limit_bytes=8 << 20),
        name="place_kernel",
    )(chip, *ring_pieces([both] * 4, "x"))
    whole, grad_three = lax.optimization_barrier((whole, grad_three))
    grad_three = jnp.swapaxes(grad_three, 1, 2).reshape(3, 3, 3, 128, 16)
    grad_one, grad_two = pl.pallas_call(
        functools.partial(finish_kernel, scale=fine_scale),
        out_shape=[jax.ShapeDtypeStruct((3456, 128), F32)] * 2,
        in_specs=[pl.BlockSpec(memory_space=pltpu.SMEM)] + [pl.BlockSpec(memory_space=pltpu.VMEM)] * 2,
        out_specs=[pl.BlockSpec(memory_space=pltpu.VMEM)] * 2,
        compiler_params=pltpu.CompilerParams(vmem_limit_bytes=8 << 20),
        name="finish_kernel",
    )(core_ref, whole, swap_cores(whole))
    grad_one = grad_one.reshape(3, 3, 3, 128, 128)
    grad_two = grad_two.reshape(3, 3, 3, 128, 128)
    return (bottleneck, input_grad, grad_one, grad_two, grad_three)


def solution(mesh):
    fine = Mesh(mesh.devices.reshape(4, 2, 4, 4), ("x", "c", "z", "y"))
    cells = P(GX, GY, None, None)
    outs = P(None, None, None, None, GY)
    return jax.shard_map(
        on_device,
        mesh=fine,
        in_specs=(cells, cells, cells, P(), P(), outs),
        out_specs=(cells, cells, P(), P(), outs),
        check_vma=False,
    )
```

```python
import functools
import math

import jax
import jax.numpy as jnp
from jax import lax
from jax.experimental import pallas as pl
from jax.experimental.pallas import tpu as pltpu
from jax.sharding import Mesh
from jax.sharding import PartitionSpec as P

GX = ("x", "c")
GY = ("z", "y")
FLAT = ("x", "z", "y")
F32 = jnp.float32
BF16 = jnp.bfloat16
PIECE = 56


def shifted(array, axes, step):
    count = lax.axis_size(axes)
    return lax.ppermute(array, axes, [(i, (i + step) % count) for i in range(count)])


def swap_cores(array):
    return lax.ppermute(array, "c", [(0, 1), (1, 0)])


def ring_pieces(pieces, axis):
    sent = [lax.ppermute(pieces[d], axis, [(i, (i + d) % 4) for i in range(4)]) for d in (1, 2, 3)]
    return [pieces[0]] + sent


def slab_kernel(own, before, after, low, high):
    width, size_x = low.shape[0], own.shape[0]
    for slab, start in ((low, 0), (high, size_x - width)):
        rows = slice(start, start + width)
        columns = 0
        for part in (before, own, after):
            slab[:, columns : columns + part.shape[1]] = part[rows]
            columns += part.shape[1]


def first_slab_kernel(own, before, after, grads, low, high):
    for slab, start, row in ((low, 0, 0), (high, 2, 1)):
        for at in range(2):
            slab[at * 8 : at * 8 + 2] = before[start + at]
            slab[at * 8 + 2 : at * 8 + 6] = own[start + at]
            slab[at * 8 + 6 : at * 8 + 8] = after[start + at]
        slab[16] = before[4, row]
        slab[19] = after[4, row]
        for at_y in range(2):
            for half in range(2):
                part = grads[row, at_y, :, half * 128 : half * 128 + 128]
                slab[17 + at_y, half * 32 : half * 32 + 32] = part


def exchange_x(low, high):
    return shifted(high, GX, 1), shifted(low, GX, -1)


def halo_pieces(own, width, first, last):
    before, after = shifted(last, GY, 1), shifted(first, GY, -1)
    size_x, size_y, size_z, chans = own.shape
    slab = (width, size_y + 2 * width, size_z, chans)
    low, high = call(slab_kernel, [(slab, BF16)] * 2, [], 0, own, before, after)
    return own, before, after, *exchange_x(low, high)


def fill_padded(padded, own, before, after, left, right):
    size_x, size_y = own.shape[0], own.shape[1]
    width = left.shape[0]
    padded[0:width] = left[...]
    padded[width + size_x : 2 * width + size_x] = right[...]
    middle = slice(width, width + size_x)
    padded[middle, 0:width] = before[...]
    padded[middle, width : width + size_y] = own[...]
    padded[middle, width + size_y : 2 * width + size_y] = after[...]


def slope_and_silu(values):
    sigma = 1.0 / (1.0 + jnp.exp(-values))
    return values * sigma, sigma * (1.0 + values * (1.0 - sigma))


def window_rows(source, row, count, skip=0):
    pieces = []
    for kx in range(3):
        for ky in range(3):
            block = source[row + kx + skip, ky + skip : ky + skip + count]
            pieces.append(block.reshape(block.shape[0] * block.shape[1], block.shape[2]))
    return jnp.concatenate(pieces, axis=1)


def roll_z(values, step):
    return pltpu.roll(values, step % values.shape[1], 1)


def join_taps(product, count, size_z, chans):
    parts = product.reshape(count, size_z, 3 * chans)
    return (
        roll_z(parts[:, :, 0:chans], 1)
        + parts[:, :, chans : 2 * chans]
        + roll_z(parts[:, :, 2 * chans : 3 * chans], -1)
    )


def spread_errors(errors):
    count, size_z, chans = errors.shape
    parts = [roll_z(errors, -1), errors, roll_z(errors, 1)]
    return jnp.concatenate([p.reshape(count * size_z, chans) for p in parts], axis=1).astype(BF16)


def fill_forward(packed, taps):
    for kx in range(3):
        for ky in range(3):
            for kz in range(3):
                at = kx * 3 + ky
                packed[at * 128 : at * 128 + 128, kz * 128 : kz * 128 + 128] = taps[at * 3 + kz]


def fill_backward(packed, taps):
    for kx in range(3):
        for ky in range(3):
            for kz in range(3):
                at = kx * 3 + ky
                packed[kz * 128 : kz * 128 + 128, at * 128 : at * 128 + 128] = taps[26 - at * 3 - kz]


def dot_nn(left, right):
    return lax.dot_general(left, right, (((1,), (0,)), ((), ())), preferred_element_type=F32)


def dot_nt(left, right):
    return lax.dot_general(left, right, (((1,), (1,)), ((), ())), preferred_element_type=F32)


def dot_tn(left, right):
    return lax.dot_general(left, right, (((0,), (0,)), ((), ())), preferred_element_type=F32)


def forward_kernel(core, own, before, after, left, right, taps_one, taps_two,
                   field_keep, field_send, slope_one, slope_two, pooled,
                   padded, packed, act_one, halves):
    for at in range(2):
        padded[at] = left[at * 8 : at * 8 + 8]
        padded[6 + at] = right[at * 8 : at * 8 + 8]
    padded[2:6, 0:2] = before[0:4]
    padded[2:6, 2:6] = own[...]
    padded[2:6, 6:8] = after[0:4]
    fill_forward(packed, taps_one)
    first_core = core[0] == 0

    def first(row, _):
        product = dot_nn(window_rows(padded, row, 6), packed[...])
        act, slope = slope_and_silu(join_taps(product, 6, 64, 128))
        act = act.astype(BF16)
        field = padded[row + 1, 1:7]
        act_one[row] = act
        field_keep[row] = jnp.where(first_core, field, act)
        field_send[row] = jnp.where(first_core, act, field)
        slope_one[row] = slope.astype(BF16)
        return 0

    lax.fori_loop(0, 6, first, 0)
    fill_forward(packed, taps_two)

    def second(row, _):
        product = dot_nn(window_rows(act_one, row, 4), packed[...])
        act, slope = slope_and_silu(join_taps(product, 4, 64, 128))
        slope_two[row] = slope.astype(BF16)
        act = act.astype(BF16).astype(F32)
        halves[row] = act.reshape(2, 2, 64, 128).sum(axis=1)
        return 0

    lax.fori_loop(0, 4, second, 0)
    for at_x in range(2):
        for at_y in range(2):
            total = 0.0
            for part in range(2):
                for start in range(2):
                    total = total + halves[2 * at_x + part, at_y, pl.ds(start, 32, stride=2), :]
            pooled[at_x, at_y] = (total * 0.125).astype(BF16)


def bottom_kernel(own, before, after, left, right, g_own, f_before, f_after, f_left, f_right,
                  taps_three, slope_two, skip, bottleneck, bundle, err_two, err_near, err_first, err_last,
                  padded, grads, packed, errors, wide):
    fill_padded(padded, own, before, after, left, right)
    for half in range(2):
        rows, lanes = slice(half * 32, half * 32 + 32), slice(half * 128, half * 128 + 128)
        grads[0, :, :, lanes] = f_left[16:20, rows]
        grads[3, :, :, lanes] = f_right[16:20, rows]
        for at in range(2):
            grads[1 + at, 0, :, lanes] = f_before[4, at, rows]
            grads[1 + at, 3, :, lanes] = f_after[4, at, rows]
    grads[1:3, 1:3] = g_own[...]
    for at in range(9):
        for kz in range(3):
            packed[kz * 256 : kz * 256 + 256, at * 128 : at * 128 + 128] = taps_three[at * 3 + kz]
    for row in range(4):
        product = dot_nt(window_rows(padded, row, 4), packed[...])
        act, slope = slope_and_silu(join_taps(product, 4, 32, 256))
        if row in (1, 2):
            bottleneck[row - 1] = act[1:3].astype(BF16)
        errs = (grads[row].astype(F32) * slope).astype(BF16)
        errors[row] = errs
        bundle[row * 4 : row * 4 + 4] = padded[row + 1, 1:5]
        if row in (1, 2):
            for at_y in range(2):
                for half in range(2):
                    at = 16 + ((row - 1) * 2 + at_y) * 2 + half
                    bundle[at] = errs[1 + at_y, :, half * 128 : half * 128 + 128]
    for row in range(2):
        total = jnp.zeros((64, 384), F32)
        for kx in range(3):
            for ky in range(3):
                block = errors[row + kx, ky : ky + 2].reshape(64, 256)
                at = kx * 3 + ky
                back = jnp.concatenate(
                    [taps_three[26 - at * 3 - kz] for kz in range(3)], axis=1
                )
                total = total + dot_nn(block, back)
        upward = join_taps(total, 2, 32, 128) * 0.125
        for at_y in range(2):
            wide[pl.ds(0, 32, stride=2), :] = upward[at_y]
            wide[pl.ds(1, 32, stride=2), :] = upward[at_y]
            for dx in range(2):
                for dy in range(2):
                    at = (2 * row + dx, 2 * at_y + dy)
                    err = skip[at].astype(F32) + wide[...]
                    err = (err * slope_two[at].astype(F32)).astype(BF16)
                    err_two[at] = err
                    err_near[at] = err
                    edge = err_first if at_y == 0 else err_last
                    edge[2 * row + dx, dy] = err


def add_tap_grads(total, fields, errors):
    def step(row, _):
        total[...] += dot_tn(window_rows(fields, row, 4), spread_errors(errors[row].astype(F32)))
        return 0

    lax.fori_loop(0, 4, step, 0)


def own_grads_kernel(fields, errors, total):
    total[...] = jnp.zeros_like(total)
    add_tap_grads(total, fields, errors)


def pair_grads_kernel(fields, errors, own_total, out, total):
    total[...] = own_total[...]
    add_tap_grads(total, fields, errors)
    for at in range(9):
        for kz in range(3):
            rows = (at * 3 + kz) * 128
            out[rows : rows + 128] = total[
                at * 128 : at * 128 + 128, kz * 128 : kz * 128 + 128
            ].astype(BF16)
    out[3456:3584] = jnp.zeros((128, 128), BF16)


def bottom_grads_kernel(core, own, other, out, total):
    for step, bundle in ((0, own), (1, other)):
        for row in range(2):
            fields = []
            for kx in range(3):
                for ky in range(3):
                    at = (row + kx) * 4 + ky
                    fields.append(bundle[at : at + 2].reshape(64, 128))
            at = 16 + row * 4
            errors = [
                jnp.concatenate([bundle[at + 2 * y], bundle[at + 2 * y + 1]], axis=1).reshape(1, 32, 256)
                for y in range(2)
            ]
            errors = jnp.concatenate(errors, axis=0).astype(F32)
            term = dot_tn(spread_errors(errors), jnp.concatenate(fields, axis=1))
            if step == 0 and row == 0:
                total[...] = term
            else:
                total[...] += term
    first_core = core[0] == 0
    out[48:64, 48:56] = jnp.zeros((16, 8, 128), BF16)
    for unit in range(27):
        at_x, rows = unit // 7, unit % 7 * 8
        at, kz = unit // 3, unit % 3
        block = total[kz * 256 : kz * 256 + 256, at * 128 : at * 128 + 128]
        block = block.reshape(16, 2, 8, 128)
        block = jnp.where(first_core, block[:, 0], block[:, 1]).astype(BF16)
        out[at_x * 16 : at_x * 16 + 16, rows : rows + 8] = block


def first_errors_kernel(core, own, before, after, left, right, taps_two, slope_one,
                        err_one, err_keep, err_send, padded, packed):
    fill_padded(padded, own, before, after, left, right)
    fill_backward(packed, taps_two)

    def step(row, _):
        product = dot_nt(window_rows(padded, row, 6), packed[...])
        back = join_taps(product, 6, 64, 128)
        err_one[row] = (back * slope_one[row].astype(F32)).astype(BF16)
        return 0

    lax.fori_loop(0, 6, step, 0)
    first_core = core[0] == 0
    for row in range(4):
        first, second = err_one[row + 1, 1:5], own[row]
        err_keep[row] = jnp.where(first_core, first, second)
        err_send[row] = jnp.where(first_core, second, first)


def input_kernel(err_one, taps_one, out, packed):
    fill_backward(packed, taps_one)

    def step(row, _):
        product = dot_nt(window_rows(err_one, row, 4), packed[...])
        out[row] = join_taps(product, 4, 64, 128).astype(BF16)
        return 0

    lax.fori_loop(0, 4, step, 0)


def sum_kernel(pieces, out):
    total = pieces[0].astype(F32)
    for at in range(1, 64):
        total = total + pieces[at].astype(F32)
    total = total.astype(BF16)
    for at in range(out.shape[0]):
        out[at] = total


def place_kernel(chip, pair_0, pair_1, pair_2, pair_3, out, *, scale):
    for distance, pair in enumerate((pair_0, pair_1, pair_2, pair_3)):
        at = lax.rem(chip[0] + 4 - distance, 4)

        def put(rows, pair=pair, at=at):
            both = [pair[c, rows * 8 : rows * 8 + 8].astype(F32) * scale for c in range(2)]
            out[at * 7 + rows] = jnp.concatenate(both, axis=0)

        for rows in range(6):
            put(rows)
        pl.when(at < 3)(functools.partial(put, 6))


def finish_kernel(core, whole, other, grad_one, grad_two, *, scale):
    @pl.when(core[0] == 0)
    def _():
        grad_one[...] = whole[0:3456].astype(F32) * scale
        grad_two[...] = other[0:3456].astype(F32) * scale

    @pl.when(core[0] == 1)
    def _():
        grad_one[...] = other[0:3456].astype(F32) * scale
        grad_two[...] = whole[0:3456].astype(F32) * scale


def in_hbm(array):
    return pltpu.with_memory_space_constraint(array, pltpu.HBM)


def call(kernel, out_shapes, scratch, flops, *operands):
    shapes = [pltpu.HBM(*s[:2]) if s[2:] else jax.ShapeDtypeStruct(*s) for s in out_shapes]
    moved = sum(o.size * o.dtype.itemsize for o in operands)
    return pl.pallas_call(
        kernel,
        out_shape=shapes,
        in_specs=[
            pl.BlockSpec(memory_space=pltpu.SMEM if o.dtype == jnp.int32 else pltpu.VMEM) for o in operands
        ],
        out_specs=[pl.BlockSpec(memory_space=pltpu.VMEM)] * len(shapes),
        scratch_shapes=[pltpu.VMEM(s, d) for s, d in scratch],
        compiler_params=pltpu.CompilerParams(vmem_limit_bytes=18 << 20),
        cost_estimate=pl.CostEstimate(flops=flops // 20, bytes_accessed=moved // 20, transcendentals=0),
        name=kernel.__name__,
    )(*operands)


def on_device(features, skip_grad, bottom_grad, conv_one, conv_two, conv_three):
    core = lax.axis_index("c")
    first = jnp.concatenate([bottom_grad[:, :1, :, :128], bottom_grad[:, :1, :, 128:]], axis=2)
    last = jnp.concatenate([bottom_grad[:, 1:, :, :128], bottom_grad[:, 1:, :, 128:]], axis=2)
    first = jnp.concatenate([features[:, :2], first.reshape(1, 2, 64, 128)], axis=0)
    last = jnp.concatenate([features[:, -2:], last.reshape(1, 2, 64, 128)], axis=0)
    first, last, first_core, core_ref, chip = lax.optimization_barrier(
        (first, last, core == 0, core.reshape(1), lax.axis_index("x").reshape(1))
    )
    fine_cells = features.size // 128 * lax.axis_size(GX) * lax.axis_size(GY)
    fine_scale = 1.0 / math.sqrt(fine_cells)
    coarse_scale = 1.0 / math.sqrt(fine_cells // 8)
    taps_one = conv_one.reshape(27, 128, 128)
    taps_two = conv_two.reshape(27, 128, 128)
    half_taps = jnp.swapaxes(conv_three.reshape(27, 128, 16), 1, 2).reshape(27, 2, 8, 128)
    half_taps = jnp.where(first_core, half_taps[:, 0], half_taps[:, 1])
    mine = lax.all_to_all(jnp.broadcast_to(half_taps, (16, 27, 8, 128)), GY, 0, 0)

    f_before, f_after = shifted(last, GY, 1), shifted(first, GY, -1)
    low, high = call(
        first_slab_kernel, [((20, 64, 128), BF16)] * 2, [], 4 * 10**11,
        features, f_before, f_after, bottom_grad,
    )
    f_left, f_right = exchange_x(low, high)

    conv_flops = 2 * 1152 * 128 * 1024 * 3
    field = (6, 6, 64, 128)
    block = (4, 4, 64, 128)
    edge = (4, 2, 64, 128)
    field_keep, field_send, slope_one, slope_two, pooled = call(
        forward_kernel,
        [(field, BF16, True), (field, BF16, True), (field, BF16, True), (block, BF16, True), ((2, 2, 32, 128), BF16)],
        [((8, 8, 64, 128), BF16), ((1152, 384), BF16), (field, BF16), ((4, 2, 64, 128), F32)],
        3 * conv_flops, core_ref, features, f_before, f_after, f_left, f_right, taps_one, taps_two,
    )
    field_other = swap_cores(field_send)
    mine, pooled = lax.optimization_barrier((mine, pooled))
    theirs = swap_cores(mine)
    both = jnp.where(first_core, jnp.stack([mine, theirs]), jnp.stack([theirs, mine]))
    taps_three = jnp.transpose(both, (2, 1, 0, 3, 4)).reshape(27, 256, 128)
    p_pieces = halo_pieces(pooled, 2, pooled, pooled)
    bottleneck, bundle, err_two, err_near, err_first, err_last = call(
        bottom_kernel,
        [((2, 2, 32, 256), BF16, True), ((24, 32, 128), BF16), (block, BF16, True), (block, BF16), (edge, BF16), (edge, BF16)],
        [((6, 6, 32, 128), BF16), ((4, 4, 32, 256), BF16), ((768, 1152), BF16),
         ((4, 4, 32, 256), BF16), ((64, 128), F32)],
        conv_flops, *p_pieces, bottom_grad, f_before, f_after, f_left, f_right,
        taps_three, in_hbm(slope_two), in_hbm(skip_grad),
    )
    (three,) = call(
        bottom_grads_kernel, [((64, PIECE, 128), BF16, True)], [((768, 1152), F32)],
        conv_flops // 2, core_ref, bundle, swap_cores(bundle),
    )
    e_before, e_after = shifted(err_last, GY, 1), shifted(err_first, GY, -1)
    three, e_before, e_after = lax.optimization_barrier((three, e_before, e_after))
    low, high = call(slab_kernel, [((2, 8, 64, 128), BF16)] * 2, [], 0, err_near, e_before, e_after)
    three_pieces = lax.all_to_all(three, FLAT, 0, 0)
    err_one, err_keep, err_send = call(
        first_errors_kernel, [(field, BF16, True), (block, BF16), (block, BF16)],
        [((8, 8, 64, 128), BF16), ((384, 1152), BF16)],
        10**11, core_ref, in_hbm(err_two), e_before, e_after, *exchange_x(low, high),
        taps_two, in_hbm(slope_one),
    )
    err_other = swap_cores(err_send)
    (total,) = call(own_grads_kernel, [((1152, 384), F32)], [], conv_flops, field_keep, err_keep)
    (kept,) = call(
        pair_grads_kernel, [((3584, 128), BF16, True)], [((1152, 384), F32)],
        conv_flops, field_other, err_other, total,
    )
    kept, three_pieces = lax.optimization_barrier((kept, three_pieces))
    kept = kept.reshape(64, PIECE, 128)
    (part,) = call(
        sum_kernel, [((64, PIECE, 128), BF16, True)], [], 0, lax.all_to_all(kept, FLAT, 0, 0)
    )
    (three_part,) = call(sum_kernel, [((1, PIECE, 128), BF16)], [], 0, three_pieces)
    three_part = three_part[0]
    (input_grad,) = call(
        input_kernel, [(block, BF16, True)], [((384, 1152), BF16)],
        conv_flops, err_one, taps_one,
    )
    part, input_grad = lax.optimization_barrier((part, input_grad))
    whole = lax.all_to_all(part, FLAT, 0, 0).reshape(64 * PIECE, 128)
    both = swap_cores(three_part)
    both = jnp.where(first_core, jnp.stack([three_part, both]), jnp.stack([both, three_part]))
    grad_three = pl.pallas_call(
        functools.partial(place_kernel, scale=coarse_scale),
        out_shape=jax.ShapeDtypeStruct((27, 16, 128), F32),
        in_specs=[pl.BlockSpec(memory_space=pltpu.SMEM)] + [pl.BlockSpec(memory_space=pltpu.VMEM)] * 4,
        out_specs=pl.BlockSpec(memory_space=pltpu.VMEM),
        compiler_params=pltpu.CompilerParams(vmem_limit_bytes=8 << 20),
        name="place_kernel",
    )(chip, *ring_pieces([both] * 4, "x"))
    whole, grad_three = lax.optimization_barrier((whole, grad_three))
    grad_three = jnp.swapaxes(grad_three, 1, 2).reshape(3, 3, 3, 128, 16)
    grad_one, grad_two = pl.pallas_call(
        functools.partial(finish_kernel, scale=fine_scale),
        out_shape=[jax.ShapeDtypeStruct((3456, 128), F32)] * 2,
        in_specs=[pl.BlockSpec(memory_space=pltpu.SMEM)] + [pl.BlockSpec(memory_space=pltpu.VMEM)] * 2,
        out_specs=[pl.BlockSpec(memory_space=pltpu.VMEM)] * 2,
        compiler_params=pltpu.CompilerParams(vmem_limit_bytes=8 << 20),
        name="finish_kernel",
    )(core_ref, whole, swap_cores(whole))
    grad_one = grad_one.reshape(3, 3, 3, 128, 128)
    grad_two = grad_two.reshape(3, 3, 3, 128, 128)
    return (bottleneck, input_grad, grad_one, grad_two, grad_three)


def solution(mesh):
    fine = Mesh(mesh.devices.reshape(4, 2, 4, 4), ("x", "c", "z", "y"))
    cells = P(GX, GY, None, None)
    outs = P(None, None, None, None, GY)
    return jax.shard_map(
        on_device,
        mesh=fine,
        in_specs=(cells, cells, cells, P(), P(), outs),
        out_specs=(cells, cells, P(), P(), outs),
        check_vma=False,
    )
```

```python
import functools
import math

import jax
import jax.numpy as jnp
from jax import lax
from jax.experimental import pallas as pl
from jax.experimental.pallas import tpu as pltpu
from jax.sharding import Mesh
from jax.sharding import PartitionSpec as P

GX = ("x", "c")
GY = ("z", "y")
FLAT = ("x", "z", "y")
F32 = jnp.float32
BF16 = jnp.bfloat16
PIECE = 56


def shifted(array, axes, step):
    count = lax.axis_size(axes)
    return lax.ppermute(array, axes, [(i, (i + step) % count) for i in range(count)])


def swap_cores(array):
    return lax.ppermute(array, "c", [(0, 1), (1, 0)])


def ring_pieces(pieces, axis):
    sent = [lax.ppermute(pieces[d], axis, [(i, (i + d) % 4) for i in range(4)]) for d in (1, 2, 3)]
    return [pieces[0]] + sent


def slab_kernel(own, before, after, low, high):
    width, size_x = low.shape[0], own.shape[0]
    for slab, start in ((low, 0), (high, size_x - width)):
        rows = slice(start, start + width)
        columns = 0
        for part in (before, own, after):
            slab[:, columns : columns + part.shape[1]] = part[rows]
            columns += part.shape[1]


def first_edge_kernel(own, grads, first, last):
    for edge, start in ((first, 0), (last, 1)):
        edge[0:4] = own[:, 2 * start : 2 * start + 2]
        for half in range(2):
            edge[4, :, half * 32 : half * 32 + 32] = grads[:, start, :, half * 128 : half * 128 + 128]


def first_slab_kernel(own, before, after, grads, low, high):
    for slab, start, row in ((low, 0, 0), (high, 2, 1)):
        for at in range(2):
            slab[at * 8 : at * 8 + 2] = before[start + at]
            slab[at * 8 + 2 : at * 8 + 6] = own[start + at]
            slab[at * 8 + 6 : at * 8 + 8] = after[start + at]
        slab[16] = before[4, row]
        slab[19] = after[4, row]
        for at_y in range(2):
            for half in range(2):
                part = grads[row, at_y, :, half * 128 : half * 128 + 128]
                slab[17 + at_y, half * 32 : half * 32 + 32] = part


def exchange_x(low, high):
    return shifted(high, GX, 1), shifted(low, GX, -1)


def halo_pieces(own, width, first, last):
    before, after = shifted(last, GY, 1), shifted(first, GY, -1)
    size_x, size_y, size_z, chans = own.shape
    slab = (width, size_y + 2 * width, size_z, chans)
    low, high = call(slab_kernel, [(slab, BF16)] * 2, [], 0, own, before, after)
    return own, before, after, *exchange_x(low, high)


def fill_padded(padded, own, before, after, left, right):
    size_x, size_y = own.shape[0], own.shape[1]
    width = left.shape[0]
    padded[0:width] = left[...]
    padded[width + size_x : 2 * width + size_x] = right[...]
    middle = slice(width, width + size_x)
    padded[middle, 0:width] = before[...]
    padded[middle, width : width + size_y] = own[...]
    padded[middle, width + size_y : 2 * width + size_y] = after[...]


def slope_and_silu(values):
    sigma = 1.0 / (1.0 + jnp.exp(-values))
    return values * sigma, sigma * (1.0 + values * (1.0 - sigma))


def window_rows(source, row, count, skip=0):
    pieces = []
    for kx in range(3):
        for ky in range(3):
            block = source[row + kx + skip, ky + skip : ky + skip + count]
            pieces.append(block.reshape(block.shape[0] * block.shape[1], block.shape[2]))
    return jnp.concatenate(pieces, axis=1)


def roll_z(values, step):
    return pltpu.roll(values, step % values.shape[1], 1)


def join_taps(product, count, size_z, chans):
    parts = product.reshape(count, size_z, 3 * chans)
    return (
        roll_z(parts[:, :, 0:chans], 1)
        + parts[:, :, chans : 2 * chans]
        + roll_z(parts[:, :, 2 * chans : 3 * chans], -1)
    )


def spread_errors(errors):
    count, size_z, chans = errors.shape
    parts = [roll_z(errors, -1), errors, roll_z(errors, 1)]
    return jnp.concatenate([p.reshape(count * size_z, chans) for p in parts], axis=1).astype(BF16)


def fill_forward(packed, taps):
    for kx in range(3):
        for ky in range(3):
            for kz in range(3):
                at = kx * 3 + ky
                packed[at * 128 : at * 128 + 128, kz * 128 : kz * 128 + 128] = taps[at * 3 + kz]


def fill_backward(packed, taps):
    for kx in range(3):
        for ky in range(3):
            for kz in range(3):
                at = kx * 3 + ky
                packed[kz * 128 : kz * 128 + 128, at * 128 : at * 128 + 128] = taps[26 - at * 3 - kz]


def dot_nn(left, right):
    return lax.dot_general(left, right, (((1,), (0,)), ((), ())), preferred_element_type=F32)


def dot_nt(left, right):
    return lax.dot_general(left, right, (((1,), (1,)), ((), ())), preferred_element_type=F32)


def dot_tn(left, right):
    return lax.dot_general(left, right, (((0,), (0,)), ((), ())), preferred_element_type=F32)


def forward_kernel(core, own, before, after, left, right, taps_one, taps_two,
                   field_keep, field_send, slope_one, slope_two, pooled,
                   padded, packed, act_one, halves):
    for at in range(2):
        padded[at] = left[at * 8 : at * 8 + 8]
        padded[6 + at] = right[at * 8 : at * 8 + 8]
    padded[2:6, 0:2] = before[0:4]
    padded[2:6, 2:6] = own[...]
    padded[2:6, 6:8] = after[0:4]
    fill_forward(packed, taps_one)
    first_core = core[0] == 0

    def first(row, _):
        product = dot_nn(window_rows(padded, row, 6), packed[...])
        act, slope = slope_and_silu(join_taps(product, 6, 64, 128))
        act = act.astype(BF16)
        field = padded[row + 1, 1:7]
        act_one[row] = act
        field_keep[row] = jnp.where(first_core, field, act)
        field_send[row] = jnp.where(first_core, act, field)

        @pl.when((row >= 1) & (row <= 4))
        def _():
            slope_one[row - 1] = slope[1:5].astype(BF16)

        return 0

    lax.fori_loop(0, 6, first, 0)
    fill_forward(packed, taps_two)

    def second(row, _):
        product = dot_nn(window_rows(act_one, row, 4), packed[...])
        act, slope = slope_and_silu(join_taps(product, 4, 64, 128))
        slope_two[row] = slope.astype(BF16)
        act = act.astype(BF16).astype(F32)
        halves[row] = act.reshape(2, 2, 64, 128).sum(axis=1)
        return 0

    lax.fori_loop(0, 4, second, 0)
    for at_x in range(2):
        for at_y in range(2):
            total = 0.0
            for part in range(2):
                for start in range(2):
                    total = total + halves[2 * at_x + part, at_y, pl.ds(start, 32, stride=2), :]
            pooled[at_x, at_y] = (total * 0.125).astype(BF16)


def bottom_kernel(own, before, after, left, right, g_own, f_before, f_after, f_left, f_right,
                  taps_three, slope_two, skip, bottleneck, bundle, err_two, err_near, err_first, err_last,
                  padded, grads, packed, errors, wide):
    fill_padded(padded, own, before, after, left, right)
    for half in range(2):
        rows, lanes = slice(half * 32, half * 32 + 32), slice(half * 128, half * 128 + 128)
        grads[0, :, :, lanes] = f_left[16:20, rows]
        grads[3, :, :, lanes] = f_right[16:20, rows]
        for at in range(2):
            grads[1 + at, 0, :, lanes] = f_before[4, at, rows]
            grads[1 + at, 3, :, lanes] = f_after[4, at, rows]
    grads[1:3, 1:3] = g_own[...]
    for at in range(9):
        for kz in range(3):
            packed[kz * 256 : kz * 256 + 256, at * 128 : at * 128 + 128] = taps_three[at * 3 + kz]
    for row in range(4):
        product = dot_nt(window_rows(padded, row, 4), packed[...])
        act, slope = slope_and_silu(join_taps(product, 4, 32, 256))
        if row in (1, 2):
            bottleneck[row - 1] = act[1:3].astype(BF16)
        errs = (grads[row].astype(F32) * slope).astype(BF16)
        errors[row] = errs
        bundle[row * 4 : row * 4 + 4] = padded[row + 1, 1:5]
        if row in (1, 2):
            for at_y in range(2):
                for half in range(2):
                    at = 16 + ((row - 1) * 2 + at_y) * 2 + half
                    bundle[at] = errs[1 + at_y, :, half * 128 : half * 128 + 128]
    for row in range(2):
        total = jnp.zeros((64, 384), F32)
        for kx in range(3):
            for ky in range(3):
                block = errors[row + kx, ky : ky + 2].reshape(64, 256)
                at = kx * 3 + ky
                back = jnp.concatenate(
                    [taps_three[26 - at * 3 - kz] for kz in range(3)], axis=1
                )
                total = total + dot_nn(block, back)
        upward = join_taps(total, 2, 32, 128) * 0.125
        for at_y in range(2):
            wide[pl.ds(0, 32, stride=2), :] = upward[at_y]
            wide[pl.ds(1, 32, stride=2), :] = upward[at_y]
            for dx in range(2):
                for dy in range(2):
                    at = (2 * row + dx, 2 * at_y + dy)
                    err = skip[at].astype(F32) + wide[...]
                    err = (err * slope_two[at].astype(F32)).astype(BF16)
                    err_two[at] = err
                    err_near[at] = err
                    if dy == at_y:
                        edge = err_first if at_y == 0 else err_last
                        edge[2 * row + dx, 0] = err


def add_tap_grads(total, fields, errors):
    def step(row, _):
        total[...] += dot_tn(window_rows(fields, row, 4), spread_errors(errors[row].astype(F32)))
        return 0

    lax.fori_loop(0, 4, step, 0)


def own_grads_kernel(fields, errors, total):
    total[...] = jnp.zeros_like(total)
    add_tap_grads(total, fields, errors)


def pair_grads_kernel(fields, errors, own_total, out, total):
    total[...] = own_total[...]
    add_tap_grads(total, fields, errors)
    for at in range(9):
        for kz in range(3):
            rows = (at * 3 + kz) * 128
            out[rows : rows + 128] = total[
                at * 128 : at * 128 + 128, kz * 128 : kz * 128 + 128
            ].astype(BF16)
    out[3456:3584] = jnp.zeros((128, 128), BF16)


def bottom_grads_kernel(core, own, other, out, total):
    for step, bundle in ((0, own), (1, other)):
        for row in range(2):
            fields = []
            for kx in range(3):
                for ky in range(3):
                    at = (row + kx) * 4 + ky
                    fields.append(bundle[at : at + 2].reshape(64, 128))
            at = 16 + row * 4
            errors = [
                jnp.concatenate([bundle[at + 2 * y], bundle[at + 2 * y + 1]], axis=1).reshape(1, 32, 256)
                for y in range(2)
            ]
            errors = jnp.concatenate(errors, axis=0).astype(F32)
            term = dot_tn(spread_errors(errors), jnp.concatenate(fields, axis=1))
            if step == 0 and row == 0:
                total[...] = term
            else:
                total[...] += term
    first_core = core[0] == 0
    out[48:64, 48:56] = jnp.zeros((16, 8, 128), BF16)
    for unit in range(27):
        at_x, rows = unit // 7, unit % 7 * 8
        at, kz = unit // 3, unit % 3
        block = total[kz * 256 : kz * 256 + 256, at * 128 : at * 128 + 128]
        block = block.reshape(16, 2, 8, 128)
        block = jnp.where(first_core, block[:, 0], block[:, 1]).astype(BF16)
        out[at_x * 16 : at_x * 16 + 16, rows : rows + 8] = block


def first_errors_kernel(core, own, before, after, left, right, taps_two, slope_one,
                        err_one, err_first, err_last, err_keep, err_send, padded, packed):
    fill_padded(padded, own, before, after, left, right)
    fill_backward(packed, taps_two)
    first_core = core[0] == 0

    def step(row, _):
        product = dot_nt(window_rows(padded, row, 4), packed[...])
        back = join_taps(product, 4, 64, 128)
        first, second = (back * slope_one[row].astype(F32)).astype(BF16), own[row]
        err_one[row] = first
        err_first[row] = first[0:1]
        err_last[row] = first[3:4]
        err_keep[row] = jnp.where(first_core, first, second)
        err_send[row] = jnp.where(first_core, second, first)
        return 0

    lax.fori_loop(0, 4, step, 0)


def input_kernel(own, before, after, left, right, taps_one, out, padded, packed):
    fill_padded(padded, own, before, after, left, right)
    fill_backward(packed, taps_one)

    def step(row, _):
        product = dot_nt(window_rows(padded, row, 4), packed[...])
        out[row] = join_taps(product, 4, 64, 128).astype(BF16)
        return 0

    lax.fori_loop(0, 4, step, 0)


def sum_kernel(pieces, out):
    total = pieces[0].astype(F32)
    for at in range(1, 64):
        total = total + pieces[at].astype(F32)
    total = total.astype(BF16)
    for at in range(out.shape[0]):
        out[at] = total


def place_kernel(chip, pair_0, pair_1, pair_2, pair_3, out, *, scale):
    for distance, pair in enumerate((pair_0, pair_1, pair_2, pair_3)):
        at = lax.rem(chip[0] + 4 - distance, 4)

        def put(rows, pair=pair, at=at):
            both = [pair[c, rows * 8 : rows * 8 + 8].astype(F32) * scale for c in range(2)]
            out[at * 7 + rows] = jnp.concatenate(both, axis=0)

        for rows in range(6):
            put(rows)
        pl.when(at < 3)(functools.partial(put, 6))


def finish_kernel(core, whole, other, grad_one, grad_two, *, scale):
    @pl.when(core[0] == 0)
    def _():
        grad_one[...] = whole[0:3456].astype(F32) * scale
        grad_two[...] = other[0:3456].astype(F32) * scale

    @pl.when(core[0] == 1)
    def _():
        grad_one[...] = other[0:3456].astype(F32) * scale
        grad_two[...] = whole[0:3456].astype(F32) * scale


def in_hbm(array):
    return pltpu.with_memory_space_constraint(array, pltpu.HBM)


def call(kernel, out_shapes, scratch, flops, *operands):
    shapes = [pltpu.HBM(*s[:2]) if s[2:] else jax.ShapeDtypeStruct(*s) for s in out_shapes]
    moved = sum(o.size * o.dtype.itemsize for o in operands)
    return pl.pallas_call(
        kernel,
        out_shape=shapes,
        in_specs=[
            pl.BlockSpec(memory_space=pltpu.SMEM if o.dtype == jnp.int32 else pltpu.VMEM) for o in operands
        ],
        out_specs=[pl.BlockSpec(memory_space=pltpu.VMEM)] * len(shapes),
        scratch_shapes=[pltpu.VMEM(s, d) for s, d in scratch],
        compiler_params=pltpu.CompilerParams(vmem_limit_bytes=18 << 20),
        cost_estimate=pl.CostEstimate(flops=flops // 20, bytes_accessed=moved // 20, transcendentals=0),
        name=kernel.__name__,
    )(*operands)


def on_device(features, skip_grad, bottom_grad, conv_one, conv_two, conv_three):
    core = lax.axis_index("c")
    first, last = call(
        first_edge_kernel, [((5, 2, 64, 128), BF16)] * 2, [], 0, in_hbm(features), in_hbm(bottom_grad)
    )
    first, last, first_core, core_ref, chip = lax.optimization_barrier(
        (first, last, core == 0, core.reshape(1), lax.axis_index("x").reshape(1))
    )
    fine_cells = features.size // 128 * lax.axis_size(GX) * lax.axis_size(GY)
    fine_scale = 1.0 / math.sqrt(fine_cells)
    coarse_scale = 1.0 / math.sqrt(fine_cells // 8)
    taps_one = conv_one.reshape(27, 128, 128)
    taps_two = conv_two.reshape(27, 128, 128)
    half_taps = jnp.swapaxes(conv_three.reshape(27, 128, 16), 1, 2).reshape(27, 2, 8, 128)
    half_taps = jnp.where(first_core, half_taps[:, 0], half_taps[:, 1])
    mine = lax.all_to_all(jnp.broadcast_to(half_taps, (16, 27, 8, 128)), GY, 0, 0)

    f_before, f_after = shifted(last, GY, 1), shifted(first, GY, -1)
    low, high = call(
        first_slab_kernel, [((20, 64, 128), BF16)] * 2, [], 4 * 10**11,
        features, f_before, f_after, bottom_grad,
    )
    f_left, f_right = exchange_x(low, high)

    conv_flops = 2 * 1152 * 128 * 1024 * 3
    field = (6, 6, 64, 128)
    block = (4, 4, 64, 128)
    edge = (4, 1, 64, 128)
    field_keep, field_send, slope_one, slope_two, pooled = call(
        forward_kernel,
        [(field, BF16, True), (field, BF16, True), (block, BF16, True), (block, BF16, True), ((2, 2, 32, 128), BF16)],
        [((8, 8, 64, 128), BF16), ((1152, 384), BF16), (field, BF16), ((4, 2, 64, 128), F32)],
        3 * conv_flops, core_ref, features, f_before, f_after, f_left, f_right, taps_one, taps_two,
    )
    field_other = swap_cores(field_send)
    mine, pooled = lax.optimization_barrier((mine, pooled))
    theirs = swap_cores(mine)
    both = jnp.where(first_core, jnp.stack([mine, theirs]), jnp.stack([theirs, mine]))
    taps_three = jnp.transpose(both, (2, 1, 0, 3, 4)).reshape(27, 256, 128)
    p_pieces = halo_pieces(pooled, 2, pooled, pooled)
    bottleneck, bundle, err_two, err_near, err_first, err_last = call(
        bottom_kernel,
        [((2, 2, 32, 256), BF16, True), ((24, 32, 128), BF16), (block, BF16, True), (block, BF16), (edge, BF16), (edge, BF16)],
        [((6, 6, 32, 128), BF16), ((4, 4, 32, 256), BF16), ((768, 1152), BF16),
         ((4, 4, 32, 256), BF16), ((64, 128), F32)],
        conv_flops, *p_pieces, bottom_grad, f_before, f_after, f_left, f_right,
        taps_three, in_hbm(slope_two), in_hbm(skip_grad),
    )
    (three,) = call(
        bottom_grads_kernel, [((64, PIECE, 128), BF16, True)], [((768, 1152), F32)],
        conv_flops // 2, core_ref, bundle, swap_cores(bundle),
    )
    e_before, e_after = shifted(err_last, GY, 1), shifted(err_first, GY, -1)
    three, e_before, e_after = lax.optimization_barrier((three, e_before, e_after))
    low, high = call(slab_kernel, [((1, 6, 64, 128), BF16)] * 2, [], 0, err_near, e_before, e_after)
    three_pieces = lax.all_to_all(three, FLAT, 0, 0)
    err_one, one_first, one_last, err_keep, err_send = call(
        first_errors_kernel,
        [(block, BF16, True), (edge, BF16, True), (edge, BF16, True), (block, BF16), (block, BF16)],
        [(field, BF16), ((384, 1152), BF16)],
        2 * 10**11, core_ref, in_hbm(err_two), e_before, e_after, *exchange_x(low, high),
        taps_two, in_hbm(slope_one),
    )
    err_other = swap_cores(err_send)
    (total,) = call(own_grads_kernel, [((1152, 384), F32)], [], conv_flops, field_keep, err_keep)
    (kept,) = call(
        pair_grads_kernel, [((3584, 128), BF16, True)], [((1152, 384), F32)],
        conv_flops, field_other, err_other, total,
    )
    kept, three_pieces, one_first, one_last = lax.optimization_barrier(
        (kept, three_pieces, one_first, one_last)
    )
    kept = kept.reshape(64, PIECE, 128)
    (part,) = call(
        sum_kernel, [((64, PIECE, 128), BF16, True)], [], 0, lax.all_to_all(kept, FLAT, 0, 0)
    )
    (three_part,) = call(sum_kernel, [((1, PIECE, 128), BF16)], [], 0, three_pieces)
    three_part = three_part[0]
    (input_grad,) = call(
        input_kernel, [(block, BF16, True)], [(field, BF16), ((384, 1152), BF16)],
        conv_flops // 4, *halo_pieces(err_one, 1, one_first, one_last), taps_one,
    )
    part, input_grad = lax.optimization_barrier((part, input_grad))
    whole = lax.all_to_all(part, FLAT, 0, 0).reshape(64 * PIECE, 128)
    both = swap_cores(three_part)
    both = jnp.where(first_core, jnp.stack([three_part, both]), jnp.stack([both, three_part]))
    grad_three = pl.pallas_call(
        functools.partial(place_kernel, scale=coarse_scale),
        out_shape=jax.ShapeDtypeStruct((27, 16, 128), F32),
        in_specs=[pl.BlockSpec(memory_space=pltpu.SMEM)] + [pl.BlockSpec(memory_space=pltpu.VMEM)] * 4,
        out_specs=pl.BlockSpec(memory_space=pltpu.VMEM),
        compiler_params=pltpu.CompilerParams(vmem_limit_bytes=8 << 20),
        name="place_kernel",
    )(chip, *ring_pieces([both] * 4, "x"))
    whole, grad_three = lax.optimization_barrier((whole, grad_three))
    grad_three = jnp.swapaxes(grad_three, 1, 2).reshape(3, 3, 3, 128, 16)
    grad_one, grad_two = pl.pallas_call(
        functools.partial(finish_kernel, scale=fine_scale),
        out_shape=[jax.ShapeDtypeStruct((3456, 128), F32)] * 2,
        in_specs=[pl.BlockSpec(memory_space=pltpu.SMEM)] + [pl.BlockSpec(memory_space=pltpu.VMEM)] * 2,
        out_specs=[pl.BlockSpec(memory_space=pltpu.VMEM)] * 2,
        compiler_params=pltpu.CompilerParams(vmem_limit_bytes=8 << 20),
        name="finish_kernel",
    )(core_ref, whole, swap_cores(whole))
    grad_one = grad_one.reshape(3, 3, 3, 128, 128)
    grad_two = grad_two.reshape(3, 3, 3, 128, 128)
    return (bottleneck, input_grad, grad_one, grad_two, grad_three)


def solution(mesh):
    fine = Mesh(mesh.devices.reshape(4, 2, 4, 4), ("x", "c", "z", "y"))
    cells = P(GX, GY, None, None)
    outs = P(None, None, None, None, GY)
    return jax.shard_map(
        on_device,
        mesh=fine,
        in_specs=(cells, cells, cells, P(), P(), outs),
        out_specs=(cells, cells, P(), P(), outs),
        check_vma=False,
    )
```

```python
import functools
import math

import jax
import jax.numpy as jnp
from jax import lax
from jax.experimental import pallas as pl
from jax.experimental.pallas import tpu as pltpu
from jax.sharding import Mesh
from jax.sharding import PartitionSpec as P

GX = ("x", "c")
GY = ("z", "y")
FLAT = ("x", "z", "y")
F32 = jnp.float32
BF16 = jnp.bfloat16
PIECE = 56


def shifted(array, axes, step):
    count = lax.axis_size(axes)
    return lax.ppermute(array, axes, [(i, (i + step) % count) for i in range(count)])


def swap_cores(array):
    return lax.ppermute(array, "c", [(0, 1), (1, 0)])


def ring_pieces(pieces, axis):
    sent = [lax.ppermute(pieces[d], axis, [(i, (i + d) % 4) for i in range(4)]) for d in (1, 2, 3)]
    return [pieces[0]] + sent


def slab_kernel(own, before, after, low, high):
    width, size_x = low.shape[0], own.shape[0]
    for slab, start in ((low, 0), (high, size_x - width)):
        rows = slice(start, start + width)
        columns = 0
        for part in (before, own, after):
            slab[:, columns : columns + part.shape[1]] = part[rows]
            columns += part.shape[1]


def first_edge_kernel(own, grads, first, last):
    for edge, start in ((first, 0), (last, 1)):
        edge[0:4] = own[:, 2 * start : 2 * start + 2]
        for half in range(2):
            edge[4, :, half * 32 : half * 32 + 32] = grads[:, start, :, half * 128 : half * 128 + 128]


def first_slab_kernel(own, before, after, grads, low, high):
    for slab, start, row in ((low, 0, 0), (high, 2, 1)):
        for at in range(2):
            slab[at * 8 : at * 8 + 2] = before[start + at]
            slab[at * 8 + 2 : at * 8 + 6] = own[start + at]
            slab[at * 8 + 6 : at * 8 + 8] = after[start + at]
        slab[16] = before[4, row]
        slab[19] = after[4, row]
        for at_y in range(2):
            for half in range(2):
                part = grads[row, at_y, :, half * 128 : half * 128 + 128]
                slab[17 + at_y, half * 32 : half * 32 + 32] = part


def exchange_x(low, high):
    return shifted(high, GX, 1), shifted(low, GX, -1)


def halo_pieces(own, width, first, last):
    before, after = shifted(last, GY, 1), shifted(first, GY, -1)
    size_x, size_y, size_z, chans = own.shape
    slab = (width, size_y + 2 * width, size_z, chans)
    low, high = call(slab_kernel, [(slab, BF16)] * 2, [], 0, own, before, after)
    return own, before, after, *exchange_x(low, high)


def fill_padded(padded, own, before, after, left, right):
    size_x, size_y = own.shape[0], own.shape[1]
    width = left.shape[0]
    padded[0:width] = left[...]
    padded[width + size_x : 2 * width + size_x] = right[...]
    middle = slice(width, width + size_x)
    padded[middle, 0:width] = before[...]
    padded[middle, width : width + size_y] = own[...]
    padded[middle, width + size_y : 2 * width + size_y] = after[...]


def slope_and_silu(values):
    sigma = 1.0 / (1.0 + jnp.exp(-values))
    return values * sigma, sigma * (1.0 + values * (1.0 - sigma))


def window_rows(source, row, count, skip=0, rows=1):
    pieces = []
    for kx in range(3):
        for ky in range(3):
            block = source[pl.ds(row + kx + skip, rows), ky + skip : ky + skip + count]
            pieces.append(block.reshape(rows * block.shape[1] * block.shape[2], block.shape[3]))
    return jnp.concatenate(pieces, axis=1)


def roll_z(values, step):
    return pltpu.roll(values, step % values.shape[1], 1)


def join_taps(product, count, size_z, chans):
    parts = product.reshape(count, size_z, 3 * chans)
    return (
        roll_z(parts[:, :, 0:chans], 1)
        + parts[:, :, chans : 2 * chans]
        + roll_z(parts[:, :, 2 * chans : 3 * chans], -1)
    )


def spread_errors(errors):
    count, size_z, chans = errors.shape
    parts = [roll_z(errors, -1), errors, roll_z(errors, 1)]
    return jnp.concatenate([p.reshape(count * size_z, chans) for p in parts], axis=1).astype(BF16)


def fill_forward(packed, taps):
    for kx in range(3):
        for ky in range(3):
            for kz in range(3):
                at = kx * 3 + ky
                packed[at * 128 : at * 128 + 128, kz * 128 : kz * 128 + 128] = taps[at * 3 + kz]


def fill_backward(packed, taps):
    for kx in range(3):
        for ky in range(3):
            for kz in range(3):
                at = kx * 3 + ky
                packed[kz * 128 : kz * 128 + 128, at * 128 : at * 128 + 128] = taps[26 - at * 3 - kz]


def dot_nn(left, right):
    return lax.dot_general(left, right, (((1,), (0,)), ((), ())), preferred_element_type=F32)


def dot_nt(left, right):
    return lax.dot_general(left, right, (((1,), (1,)), ((), ())), preferred_element_type=F32)


def dot_tn(left, right):
    return lax.dot_general(left, right, (((0,), (0,)), ((), ())), preferred_element_type=F32)


def forward_kernel(core, own, before, after, left, right, taps_one, taps_two,
                   field_keep, field_send, slope_one, slope_two, pooled,
                   padded, packed, act_one, halves):
    for at in range(2):
        padded[at] = left[at * 8 : at * 8 + 8]
        padded[6 + at] = right[at * 8 : at * 8 + 8]
    padded[2:6, 0:2] = before[0:4]
    padded[2:6, 2:6] = own[...]
    padded[2:6, 6:8] = after[0:4]
    fill_forward(packed, taps_one)
    first_core = core[0] == 0

    def first(step, _):
        product = dot_nn(window_rows(padded, step * 2, 6, rows=2), packed[...])
        act, slope = slope_and_silu(join_taps(product, 12, 64, 128))
        act = act.astype(BF16)
        for at in range(2):
            row = step * 2 + at
            part = act[6 * at : 6 * at + 6]
            field = padded[row + 1, 1:7]
            act_one[row] = part
            field_keep[row] = jnp.where(first_core, field, part)
            field_send[row] = jnp.where(first_core, part, field)

            @pl.when((row >= 1) & (row <= 4))
            def _():
                slope_one[row - 1] = slope[6 * at + 1 : 6 * at + 5].astype(BF16)

        return 0

    lax.fori_loop(0, 3, first, 0)
    fill_forward(packed, taps_two)

    def second(step, _):
        product = dot_nn(window_rows(act_one, step * 2, 4, rows=2), packed[...])
        act, slope = slope_and_silu(join_taps(product, 8, 64, 128))
        slope = slope.astype(BF16)
        act = act.astype(BF16).astype(F32)
        for at in range(2):
            row = step * 2 + at
            slope_two[row] = slope[4 * at : 4 * at + 4]
            halves[row] = act[4 * at : 4 * at + 4].reshape(2, 2, 64, 128).sum(axis=1)
        return 0

    lax.fori_loop(0, 2, second, 0)
    for at_x in range(2):
        for at_y in range(2):
            total = 0.0
            for part in range(2):
                for start in range(2):
                    total = total + halves[2 * at_x + part, at_y, pl.ds(start, 32, stride=2), :]
            pooled[at_x, at_y] = (total * 0.125).astype(BF16)


def bottom_kernel(own, before, after, left, right, g_own, f_before, f_after, f_left, f_right,
                  taps_three, slope_two, skip, bottleneck, bundle, err_two, err_first, err_last,
                  padded, grads, packed, errors, wide):
    fill_padded(padded, own, before, after, left, right)
    for half in range(2):
        rows, lanes = slice(half * 32, half * 32 + 32), slice(half * 128, half * 128 + 128)
        grads[0, :, :, lanes] = f_left[16:20, rows]
        grads[3, :, :, lanes] = f_right[16:20, rows]
        for at in range(2):
            grads[1 + at, 0, :, lanes] = f_before[4, at, rows]
            grads[1 + at, 3, :, lanes] = f_after[4, at, rows]
    grads[1:3, 1:3] = g_own[...]
    for at in range(9):
        for kz in range(3):
            packed[kz * 256 : kz * 256 + 256, at * 128 : at * 128 + 128] = taps_three[at * 3 + kz]
    for row in range(4):
        product = dot_nt(window_rows(padded, row, 4), packed[...])
        act, slope = slope_and_silu(join_taps(product, 4, 32, 256))
        if row in (1, 2):
            bottleneck[row - 1] = act[1:3].astype(BF16)
        errs = (grads[row].astype(F32) * slope).astype(BF16)
        errors[row] = errs
        bundle[row * 4 : row * 4 + 4] = padded[row + 1, 1:5]
        if row in (1, 2):
            for at_y in range(2):
                for half in range(2):
                    at = 16 + ((row - 1) * 2 + at_y) * 2 + half
                    bundle[at] = errs[1 + at_y, :, half * 128 : half * 128 + 128]
    for row in range(2):
        total = jnp.zeros((64, 384), F32)
        for kx in range(3):
            for ky in range(3):
                block = errors[row + kx, ky : ky + 2].reshape(64, 256)
                at = kx * 3 + ky
                back = jnp.concatenate(
                    [taps_three[26 - at * 3 - kz] for kz in range(3)], axis=1
                )
                total = total + dot_nn(block, back)
        upward = join_taps(total, 2, 32, 128) * 0.125
        for at_y in range(2):
            wide[pl.ds(0, 32, stride=2), :] = upward[at_y]
            wide[pl.ds(1, 32, stride=2), :] = upward[at_y]
            for dx in range(2):
                for dy in range(2):
                    at = (2 * row + dx, 2 * at_y + dy)
                    err = skip[at].astype(F32) + wide[...]
                    err = (err * slope_two[at].astype(F32)).astype(BF16)
                    err_two[at] = err
                    if dy == at_y:
                        edge = err_first if at_y == 0 else err_last
                        edge[2 * row + dx, 0] = err


def add_tap_grads(total, fields, errors):
    def step(at, _):
        spread = spread_errors(errors[pl.ds(at * 2, 2)].reshape(8, 64, 128).astype(F32))
        total[...] += dot_tn(window_rows(fields, at * 2, 4, rows=2), spread)
        return 0

    lax.fori_loop(0, 2, step, 0)


def own_grads_kernel(fields, errors, total):
    total[...] = jnp.zeros_like(total)
    add_tap_grads(total, fields, errors)


def pair_grads_kernel(fields, errors, own_total, three, out, total):
    total[...] = own_total[...]
    add_tap_grads(total, fields, errors)
    for at in range(9):
        for kz in range(3):
            start = (at * 3 + kz) * 128
            done = 0
            while done < 128:
                piece, row = divmod(start + done, PIECE)
                size = min(PIECE - row, 128 - done)
                rows = slice(at * 128 + done, at * 128 + done + size)
                out[piece, row : row + size] = total[rows, kz * 128 : kz * 128 + 128].astype(BF16)
                done += size
    out[61, 40:PIECE] = jnp.zeros((PIECE - 40, 128), BF16)
    out[62:64, 0:PIECE] = jnp.zeros((2, PIECE, 128), BF16)
    out[:, PIECE : 2 * PIECE] = three[...]


def bottom_grads_kernel(core, own, other, out, total):
    for step, bundle in ((0, own), (1, other)):
        for row in range(2):
            fields = []
            for kx in range(3):
                for ky in range(3):
                    at = (row + kx) * 4 + ky
                    fields.append(bundle[at : at + 2].reshape(64, 128))
            at = 16 + row * 4
            errors = [
                jnp.concatenate([bundle[at + 2 * y], bundle[at + 2 * y + 1]], axis=1).reshape(1, 32, 256)
                for y in range(2)
            ]
            errors = jnp.concatenate(errors, axis=0).astype(F32)
            term = dot_tn(spread_errors(errors), jnp.concatenate(fields, axis=1))
            if step == 0 and row == 0:
                total[...] = term
            else:
                total[...] += term
    first_core = core[0] == 0
    out[48:64, 48:56] = jnp.zeros((16, 8, 128), BF16)
    for unit in range(27):
        at_x, rows = unit // 7, unit % 7 * 8
        at, kz = unit // 3, unit % 3
        block = total[kz * 256 : kz * 256 + 256, at * 128 : at * 128 + 128]
        block = block.reshape(16, 2, 8, 128)
        block = jnp.where(first_core, block[:, 0], block[:, 1]).astype(BF16)
        out[at_x * 16 : at_x * 16 + 16, rows : rows + 8] = block


def first_errors_kernel(core, own, before, after, left, right, taps_two, slope_one,
                        err_one, err_first, err_last, err_keep, err_send, padded, packed):
    fill_padded(padded, own, before, after, left, right)
    fill_backward(packed, taps_two)
    first_core = core[0] == 0

    def step(at, _):
        product = dot_nt(window_rows(padded, at * 2, 4, rows=2), packed[...])
        back = join_taps(product, 8, 64, 128)
        for half in range(2):
            row = at * 2 + half
            first = back[4 * half : 4 * half + 4] * slope_one[row].astype(F32)
            first, second = first.astype(BF16), own[row]
            err_one[row] = first
            err_first[row] = first[0:1]
            err_last[row] = first[3:4]
            err_keep[row] = jnp.where(first_core, first, second)
            err_send[row] = jnp.where(first_core, second, first)
        return 0

    lax.fori_loop(0, 2, step, 0)


def input_kernel(own, before, after, left, right, taps_one, out, padded, packed):
    fill_padded(padded, own, before, after, left, right)
    fill_backward(packed, taps_one)

    def step(row, _):
        product = dot_nt(window_rows(padded, row, 4), packed[...])
        out[row] = join_taps(product, 4, 64, 128).astype(BF16)
        return 0

    lax.fori_loop(0, 4, step, 0)


def sum_kernel(pieces, out, three):
    total = pieces[0].astype(F32)
    for at in range(1, 64):
        total = total + pieces[at].astype(F32)
    total = total.astype(BF16)
    three[...] = total[PIECE : 2 * PIECE]
    for at in range(64):
        out[at] = total[0:PIECE]


def place_kernel(chip, pair_0, pair_1, pair_2, pair_3, out, *, scale):
    for distance, pair in enumerate((pair_0, pair_1, pair_2, pair_3)):
        at = lax.rem(chip[0] + 4 - distance, 4)

        def put(rows, pair=pair, at=at):
            both = [pair[c, rows * 8 : rows * 8 + 8].astype(F32) * scale for c in range(2)]
            out[at * 7 + rows] = jnp.concatenate(both, axis=0)

        for rows in range(6):
            put(rows)
        pl.when(at < 3)(functools.partial(put, 6))


def finish_kernel(core, whole, other, grad_one, grad_two, *, scale):
    @pl.when(core[0] == 0)
    def _():
        grad_one[...] = whole[0:3456].astype(F32) * scale
        grad_two[...] = other[0:3456].astype(F32) * scale

    @pl.when(core[0] == 1)
    def _():
        grad_one[...] = other[0:3456].astype(F32) * scale
        grad_two[...] = whole[0:3456].astype(F32) * scale


def in_hbm(array):
    return pltpu.with_memory_space_constraint(array, pltpu.HBM)


def call(kernel, out_shapes, scratch, flops, *operands):
    shapes = [pltpu.HBM(*s[:2]) if s[2:] else jax.ShapeDtypeStruct(*s) for s in out_shapes]
    moved = sum(o.size * o.dtype.itemsize for o in operands)
    return pl.pallas_call(
        kernel,
        out_shape=shapes,
        in_specs=[
            pl.BlockSpec(memory_space=pltpu.SMEM if o.dtype == jnp.int32 else pltpu.VMEM) for o in operands
        ],
        out_specs=[pl.BlockSpec(memory_space=pltpu.VMEM)] * len(shapes),
        scratch_shapes=[pltpu.VMEM(s, d) for s, d in scratch],
        compiler_params=pltpu.CompilerParams(vmem_limit_bytes=18 << 20),
        cost_estimate=pl.CostEstimate(flops=flops // 20, bytes_accessed=moved // 20, transcendentals=0),
        name=kernel.__name__,
    )(*operands)


def on_device(features, skip_grad, bottom_grad, conv_one, conv_two, conv_three):
    core = lax.axis_index("c")
    first, last = call(
        first_edge_kernel, [((5, 2, 64, 128), BF16)] * 2, [], 0, in_hbm(features), in_hbm(bottom_grad)
    )
    first, last, first_core, core_ref, chip = lax.optimization_barrier(
        (first, last, core == 0, core.reshape(1), lax.axis_index("x").reshape(1))
    )
    fine_cells = features.size // 128 * lax.axis_size(GX) * lax.axis_size(GY)
    fine_scale = 1.0 / math.sqrt(fine_cells)
    coarse_scale = 1.0 / math.sqrt(fine_cells // 8)
    taps_one = conv_one.reshape(27, 128, 128)
    taps_two = conv_two.reshape(27, 128, 128)
    half_taps = jnp.swapaxes(conv_three.reshape(27, 128, 16), 1, 2).reshape(27, 2, 8, 128)
    half_taps = jnp.where(first_core, half_taps[:, 0], half_taps[:, 1])
    mine = lax.all_to_all(jnp.broadcast_to(half_taps, (16, 27, 8, 128)), GY, 0, 0)

    f_before, f_after = shifted(last, GY, 1), shifted(first, GY, -1)
    low, high = call(
        first_slab_kernel, [((20, 64, 128), BF16)] * 2, [], 4 * 10**11,
        features, f_before, f_after, bottom_grad,
    )
    f_left, f_right = exchange_x(low, high)

    conv_flops = 2 * 1152 * 128 * 1024 * 3
    field = (6, 6, 64, 128)
    block = (4, 4, 64, 128)
    edge = (4, 1, 64, 128)
    field_keep, field_send, slope_one, slope_two, pooled = call(
        forward_kernel,
        [(field, BF16, True), (field, BF16, True), (block, BF16, True), (block, BF16, True), ((2, 2, 32, 128), BF16)],
        [((8, 8, 64, 128), BF16), ((1152, 384), BF16), (field, BF16), ((4, 2, 64, 128), F32)],
        3 * conv_flops, core_ref, features, f_before, f_after, f_left, f_right, taps_one, taps_two,
    )
    field_other = swap_cores(field_send)
    mine, pooled = lax.optimization_barrier((mine, pooled))
    theirs = swap_cores(mine)
    both = jnp.where(first_core, jnp.stack([mine, theirs]), jnp.stack([theirs, mine]))
    taps_three = jnp.transpose(both, (2, 1, 0, 3, 4)).reshape(27, 256, 128)
    p_pieces = halo_pieces(pooled, 2, pooled, pooled)
    bottleneck, bundle, err_two, err_first, err_last = call(
        bottom_kernel,
        [((2, 2, 32, 256), BF16, True), ((24, 32, 128), BF16), (block, BF16), (edge, BF16), (edge, BF16)],
        [((6, 6, 32, 128), BF16), ((4, 4, 32, 256), BF16), ((768, 1152), BF16),
         ((4, 4, 32, 256), BF16), ((64, 128), F32)],
        conv_flops, *p_pieces, bottom_grad, f_before, f_after, f_left, f_right,
        taps_three, in_hbm(slope_two), in_hbm(skip_grad),
    )
    e_before, e_after = shifted(err_last, GY, 1), shifted(err_first, GY, -1)
    low, high = call(slab_kernel, [((1, 6, 64, 128), BF16)] * 2, [], 0, err_two, e_before, e_after)
    bundle, low, high = lax.optimization_barrier((bundle, low, high))
    e_left, e_right = exchange_x(low, high)
    (three,) = call(
        bottom_grads_kernel, [((64, PIECE, 128), BF16)], [((768, 1152), F32)],
        conv_flops // 2, core_ref, bundle, swap_cores(bundle),
    )
    three, e_left, e_right = lax.optimization_barrier((three, e_left, e_right))
    err_one, one_first, one_last, err_keep, err_send = call(
        first_errors_kernel,
        [(block, BF16, True), (edge, BF16, True), (edge, BF16, True), (block, BF16), (block, BF16)],
        [(field, BF16), ((384, 1152), BF16)],
        conv_flops, core_ref, err_two, e_before, e_after, e_left, e_right, taps_two, slope_one,
    )
    err_other = swap_cores(err_send)
    (total,) = call(own_grads_kernel, [((1152, 384), F32)], [], conv_flops, field_keep, err_keep)
    (kept,) = call(
        pair_grads_kernel, [((64, 2 * PIECE, 128), BF16, True)], [((1152, 384), F32)],
        conv_flops, field_other, err_other, total, three,
    )
    kept, one_first, one_last = lax.optimization_barrier((kept, one_first, one_last))
    part, three_part = call(
        sum_kernel, [((64, PIECE, 128), BF16, True), ((PIECE, 128), BF16)], [], 0,
        lax.all_to_all(kept, FLAT, 0, 0),
    )
    (input_grad,) = call(
        input_kernel, [(block, BF16, True)], [(field, BF16), ((384, 1152), BF16)],
        conv_flops // 4, *halo_pieces(err_one, 1, one_first, one_last), taps_one,
    )
    part, input_grad = lax.optimization_barrier((part, input_grad))
    whole = lax.all_to_all(part, FLAT, 0, 0).reshape(64 * PIECE, 128)
    both = swap_cores(three_part)
    both = jnp.where(first_core, jnp.stack([three_part, both]), jnp.stack([both, three_part]))
    grad_three = pl.pallas_call(
        functools.partial(place_kernel, scale=coarse_scale),
        out_shape=jax.ShapeDtypeStruct((27, 16, 128), F32),
        in_specs=[pl.BlockSpec(memory_space=pltpu.SMEM)] + [pl.BlockSpec(memory_space=pltpu.VMEM)] * 4,
        out_specs=pl.BlockSpec(memory_space=pltpu.VMEM),
        compiler_params=pltpu.CompilerParams(vmem_limit_bytes=8 << 20),
        name="place_kernel",
    )(chip, *ring_pieces([both] * 4, "x"))
    whole, grad_three = lax.optimization_barrier((whole, grad_three))
    grad_three = jnp.swapaxes(grad_three, 1, 2).reshape(3, 3, 3, 128, 16)
    grad_one, grad_two = pl.pallas_call(
        functools.partial(finish_kernel, scale=fine_scale),
        out_shape=[jax.ShapeDtypeStruct((3456, 128), F32)] * 2,
        in_specs=[pl.BlockSpec(memory_space=pltpu.SMEM)] + [pl.BlockSpec(memory_space=pltpu.VMEM)] * 2,
        out_specs=[pl.BlockSpec(memory_space=pltpu.VMEM)] * 2,
        compiler_params=pltpu.CompilerParams(vmem_limit_bytes=8 << 20),
        name="finish_kernel",
    )(core_ref, whole, swap_cores(whole))
    grad_one = grad_one.reshape(3, 3, 3, 128, 128)
    grad_two = grad_two.reshape(3, 3, 3, 128, 128)
    return (bottleneck, input_grad, grad_one, grad_two, grad_three)


def solution(mesh):
    fine = Mesh(mesh.devices.reshape(4, 2, 4, 4), ("x", "c", "z", "y"))
    cells = P(GX, GY, None, None)
    outs = P(None, None, None, None, GY)
    return jax.shard_map(
        on_device,
        mesh=fine,
        in_specs=(cells, cells, cells, P(), P(), outs),
        out_specs=(cells, cells, P(), P(), outs),
        check_vma=False,
    )
```

```python
import functools
import math

import jax
import jax.numpy as jnp
from jax import lax
from jax.experimental import pallas as pl
from jax.experimental.pallas import tpu as pltpu
from jax.sharding import Mesh
from jax.sharding import PartitionSpec as P

GX = ("x", "c")
GY = ("z", "y")
FLAT = ("x", "z", "y")
F32 = jnp.float32
BF16 = jnp.bfloat16
PIECE = 56


def shifted(array, axes, step):
    count = lax.axis_size(axes)
    return lax.ppermute(array, axes, [(i, (i + step) % count) for i in range(count)])


def swap_cores(array):
    return lax.ppermute(array, "c", [(0, 1), (1, 0)])


def ring_pieces(pieces, axis):
    sent = [lax.ppermute(pieces[d], axis, [(i, (i + d) % 4) for i in range(4)]) for d in (1, 2, 3)]
    return [pieces[0]] + sent


def slab_kernel(own, before, after, low, high):
    width, size_x = low.shape[0], own.shape[0]
    for slab, start in ((low, 0), (high, size_x - width)):
        rows = slice(start, start + width)
        columns = 0
        for part in (before, own, after):
            slab[:, columns : columns + part.shape[1]] = part[rows]
            columns += part.shape[1]


def first_edge_kernel(own, grads, first, last):
    for edge, start in ((first, 0), (last, 1)):
        edge[0:4] = own[:, 2 * start : 2 * start + 2]
        for half in range(2):
            edge[4, :, half * 32 : half * 32 + 32] = grads[:, start, :, half * 128 : half * 128 + 128]


def first_slab_kernel(own, before, after, grads, low, high):
    for slab, start, row in ((low, 0, 0), (high, 2, 1)):
        for at in range(2):
            slab[at * 8 : at * 8 + 2] = before[start + at]
            slab[at * 8 + 2 : at * 8 + 6] = own[start + at]
            slab[at * 8 + 6 : at * 8 + 8] = after[start + at]
        slab[16] = before[4, row]
        slab[19] = after[4, row]
        for at_y in range(2):
            for half in range(2):
                part = grads[row, at_y, :, half * 128 : half * 128 + 128]
                slab[17 + at_y, half * 32 : half * 32 + 32] = part


def exchange_x(low, high):
    return shifted(high, GX, 1), shifted(low, GX, -1)


def halo_pieces(own, width, first, last):
    before, after = shifted(last, GY, 1), shifted(first, GY, -1)
    size_x, size_y, size_z, chans = own.shape
    slab = (width, size_y + 2 * width, size_z, chans)
    low, high = call(slab_kernel, [(slab, BF16)] * 2, [], 0, own, before, after)
    return own, before, after, *exchange_x(low, high)


def fill_padded(padded, own, before, after, left, right):
    size_x, size_y = own.shape[0], own.shape[1]
    width = left.shape[0]
    padded[0:width] = left[...]
    padded[width + size_x : 2 * width + size_x] = right[...]
    middle = slice(width, width + size_x)
    padded[middle, 0:width] = before[...]
    padded[middle, width : width + size_y] = own[...]
    padded[middle, width + size_y : 2 * width + size_y] = after[...]


def slope_and_silu(values):
    sigma = 1.0 / (1.0 + jnp.exp(-values))
    return values * sigma, sigma * (1.0 + values * (1.0 - sigma))


def window_rows(source, row, count, skip=0, rows=1):
    pieces = []
    for kx in range(3):
        for ky in range(3):
            block = source[pl.ds(row + kx + skip, rows), ky + skip : ky + skip + count]
            pieces.append(block.reshape(rows * block.shape[1] * block.shape[2], block.shape[3]))
    return jnp.concatenate(pieces, axis=1)


def roll_z(values, step):
    return pltpu.roll(values, step % values.shape[1], 1)


def join_taps(product, count, size_z, chans):
    parts = product.reshape(count, size_z, 3 * chans)
    return (
        roll_z(parts[:, :, 0:chans], 1)
        + parts[:, :, chans : 2 * chans]
        + roll_z(parts[:, :, 2 * chans : 3 * chans], -1)
    )


def spread_errors(errors):
    count, size_z, chans = errors.shape
    parts = [roll_z(errors, -1), errors, roll_z(errors, 1)]
    return jnp.concatenate([p.reshape(count * size_z, chans) for p in parts], axis=1).astype(BF16)


def fill_forward(packed, taps):
    for kx in range(3):
        for ky in range(3):
            for kz in range(3):
                at = kx * 3 + ky
                packed[at * 128 : at * 128 + 128, kz * 128 : kz * 128 + 128] = taps[at * 3 + kz]


def fill_backward(packed, taps):
    for kx in range(3):
        for ky in range(3):
            for kz in range(3):
                at = kx * 3 + ky
                packed[kz * 128 : kz * 128 + 128, at * 128 : at * 128 + 128] = taps[26 - at * 3 - kz]


def dot_nn(left, right):
    return lax.dot_general(left, right, (((1,), (0,)), ((), ())), preferred_element_type=F32)


def dot_nt(left, right):
    return lax.dot_general(left, right, (((1,), (1,)), ((), ())), preferred_element_type=F32)


def dot_tn(left, right):
    return lax.dot_general(left, right, (((0,), (0,)), ((), ())), preferred_element_type=F32)


def forward_kernel(core, own, before, after, left, right, taps_one, taps_two,
                   field_keep, field_send, slope_one, slope_two, pooled,
                   padded, packed, act_one, halves):
    for at in range(2):
        padded[at] = left[at * 8 : at * 8 + 8]
        padded[6 + at] = right[at * 8 : at * 8 + 8]
    padded[2:6, 0:2] = before[0:4]
    padded[2:6, 2:6] = own[...]
    padded[2:6, 6:8] = after[0:4]
    fill_forward(packed, taps_one)
    first_core = core[0] == 0

    def first(step, _):
        product = dot_nn(window_rows(padded, step * 2, 6, rows=2), packed[...])
        act, slope = slope_and_silu(join_taps(product, 12, 64, 128))
        act = act.astype(BF16)
        for at in range(2):
            row = step * 2 + at
            part = act[6 * at : 6 * at + 6]
            field = padded[row + 1, 1:7]
            act_one[row] = part
            field_keep[row] = jnp.where(first_core, field, part)
            field_send[row] = jnp.where(first_core, part, field)

            @pl.when((row >= 1) & (row <= 4))
            def _():
                slope_one[row - 1] = slope[6 * at + 1 : 6 * at + 5].astype(BF16)

        return 0

    lax.fori_loop(0, 3, first, 0)
    fill_forward(packed, taps_two)

    def second(step, _):
        product = dot_nn(window_rows(act_one, step * 2, 4, rows=2), packed[...])
        act, slope = slope_and_silu(join_taps(product, 8, 64, 128))
        slope = slope.astype(BF16)
        act = act.astype(BF16).astype(F32)
        for at in range(2):
            row = step * 2 + at
            slope_two[row] = slope[4 * at : 4 * at + 4]
            halves[row] = act[4 * at : 4 * at + 4].reshape(2, 2, 64, 128).sum(axis=1)
        return 0

    lax.fori_loop(0, 2, second, 0)
    for at_x in range(2):
        for at_y in range(2):
            total = 0.0
            for part in range(2):
                for start in range(2):
                    total = total + halves[2 * at_x + part, at_y, pl.ds(start, 32, stride=2), :]
            pooled[at_x, at_y] = (total * 0.125).astype(BF16)


def bottom_kernel(own, before, after, left, right, g_own, f_before, f_after, f_left, f_right,
                  taps_three, slope_two, skip, bottleneck, bundle, err_two, err_first, err_last,
                  padded, grads, packed, errors, wide):
    fill_padded(padded, own, before, after, left, right)
    for half in range(2):
        rows, lanes = slice(half * 32, half * 32 + 32), slice(half * 128, half * 128 + 128)
        grads[0, :, :, lanes] = f_left[16:20, rows]
        grads[3, :, :, lanes] = f_right[16:20, rows]
        for at in range(2):
            grads[1 + at, 0, :, lanes] = f_before[4, at, rows]
            grads[1 + at, 3, :, lanes] = f_after[4, at, rows]
    grads[1:3, 1:3] = g_own[...]
    for at in range(9):
        for kz in range(3):
            packed[kz * 256 : kz * 256 + 256, at * 128 : at * 128 + 128] = taps_three[at * 3 + kz]
    for row in range(4):
        product = dot_nt(window_rows(padded, row, 4), packed[...])
        act, slope = slope_and_silu(join_taps(product, 4, 32, 256))
        if row in (1, 2):
            bottleneck[row - 1] = act[1:3].astype(BF16)
        errs = (grads[row].astype(F32) * slope).astype(BF16)
        errors[row] = errs
        bundle[row * 4 : row * 4 + 4] = padded[row + 1, 1:5]
        if row in (1, 2):
            for at_y in range(2):
                for half in range(2):
                    at = 16 + ((row - 1) * 2 + at_y) * 2 + half
                    bundle[at] = errs[1 + at_y, :, half * 128 : half * 128 + 128]
    for row in range(2):
        total = jnp.zeros((64, 384), F32)
        for kx in range(3):
            for ky in range(3):
                block = errors[row + kx, ky : ky + 2].reshape(64, 256)
                at = kx * 3 + ky
                back = jnp.concatenate(
                    [taps_three[26 - at * 3 - kz] for kz in range(3)], axis=1
                )
                total = total + dot_nn(block, back)
        upward = join_taps(total, 2, 32, 128) * 0.125
        for at_y in range(2):
            wide[pl.ds(0, 32, stride=2), :] = upward[at_y]
            wide[pl.ds(1, 32, stride=2), :] = upward[at_y]
            for dx in range(2):
                for dy in range(2):
                    at = (2 * row + dx, 2 * at_y + dy)
                    err = skip[at].astype(F32) + wide[...]
                    err = (err * slope_two[at].astype(F32)).astype(BF16)
                    err_two[at] = err
                    if dy == at_y:
                        edge = err_first if at_y == 0 else err_last
                        edge[2 * row + dx, 0] = err


def add_tap_grads(total, fields, errors):
    def step(at, _):
        spread = spread_errors(errors[pl.ds(at * 2, 2)].reshape(8, 64, 128).astype(F32))
        total[...] += dot_tn(window_rows(fields, at * 2, 4, rows=2), spread)
        return 0

    lax.fori_loop(0, 2, step, 0)


def own_grads_kernel(fields, errors, total):
    total[...] = jnp.zeros_like(total)
    add_tap_grads(total, fields, errors)


def pair_grads_kernel(fields, errors, own_total, three, out, total):
    total[...] = own_total[...]
    add_tap_grads(total, fields, errors)
    for at in range(9):
        for kz in range(3):
            start = (at * 3 + kz) * 128
            done = 0
            while done < 128:
                piece, row = divmod(start + done, PIECE)
                size = min(PIECE - row, 128 - done)
                rows = slice(at * 128 + done, at * 128 + done + size)
                out[piece, row : row + size] = total[rows, kz * 128 : kz * 128 + 128].astype(BF16)
                done += size
    out[61, 40:PIECE] = jnp.zeros((PIECE - 40, 128), BF16)
    out[62:64, 0:PIECE] = jnp.zeros((2, PIECE, 128), BF16)
    out[:, PIECE : 2 * PIECE] = three[...]


def bottom_grads_kernel(core, own, other, out, total):
    for step, bundle in ((0, own), (1, other)):
        for row in range(2):
            fields = []
            for kx in range(3):
                for ky in range(3):
                    at = (row + kx) * 4 + ky
                    fields.append(bundle[at : at + 2].reshape(64, 128))
            at = 16 + row * 4
            errors = [
                jnp.concatenate([bundle[at + 2 * y], bundle[at + 2 * y + 1]], axis=1).reshape(1, 32, 256)
                for y in range(2)
            ]
            errors = jnp.concatenate(errors, axis=0).astype(F32)
            term = dot_tn(spread_errors(errors), jnp.concatenate(fields, axis=1))
            if step == 0 and row == 0:
                total[...] = term
            else:
                total[...] += term
    first_core = core[0] == 0
    out[48:64, 48:56] = jnp.zeros((16, 8, 128), BF16)
    for unit in range(27):
        at_x, rows = unit // 7, unit % 7 * 8
        at, kz = unit // 3, unit % 3
        block = total[kz * 256 : kz * 256 + 256, at * 128 : at * 128 + 128]
        block = block.reshape(16, 2, 8, 128)
        block = jnp.where(first_core, block[:, 0], block[:, 1]).astype(BF16)
        out[at_x * 16 : at_x * 16 + 16, rows : rows + 8] = block


def first_errors_kernel(core, own, before, after, left, right, taps_two, slope_one,
                        err_one, err_first, err_last, err_keep, err_send, padded, packed):
    fill_padded(padded, own, before, after, left, right)
    fill_backward(packed, taps_two)
    first_core = core[0] == 0

    def step(at, _):
        product = dot_nt(window_rows(padded, at * 2, 4, rows=2), packed[...])
        back = join_taps(product, 8, 64, 128)
        for half in range(2):
            row = at * 2 + half
            first = back[4 * half : 4 * half + 4] * slope_one[row].astype(F32)
            first, second = first.astype(BF16), own[row]
            err_one[row] = first
            err_first[row] = first[0:1]
            err_last[row] = first[3:4]
            err_keep[row] = jnp.where(first_core, first, second)
            err_send[row] = jnp.where(first_core, second, first)
        return 0

    lax.fori_loop(0, 2, step, 0)


def input_kernel(own, before, after, left, right, taps_one, out, padded, packed):
    fill_padded(padded, own, before, after, left, right)
    fill_backward(packed, taps_one)

    def step(at, _):
        product = dot_nt(window_rows(padded, at * 2, 4, rows=2), packed[...])
        out[pl.ds(at * 2, 2)] = join_taps(product, 8, 64, 128).reshape(2, 4, 64, 128).astype(BF16)
        return 0

    lax.fori_loop(0, 2, step, 0)


def sum_kernel(pieces, out, three):
    total = pieces[0].astype(F32)
    for at in range(1, 64):
        total = total + pieces[at].astype(F32)
    total = total.astype(BF16)
    three[...] = total[PIECE : 2 * PIECE]
    for at in range(64):
        out[at] = total[0:PIECE]


def place_kernel(chip, pair_0, pair_1, pair_2, pair_3, out, *, scale):
    for distance, pair in enumerate((pair_0, pair_1, pair_2, pair_3)):
        at = lax.rem(chip[0] + 4 - distance, 4)

        def put(rows, pair=pair, at=at):
            both = [pair[c, rows * 8 : rows * 8 + 8].astype(F32) * scale for c in range(2)]
            out[at * 7 + rows] = jnp.concatenate(both, axis=0)

        for rows in range(6):
            put(rows)
        pl.when(at < 3)(functools.partial(put, 6))


def finish_kernel(core, whole, other, grad_one, grad_two, *, scale):
    @pl.when(core[0] == 0)
    def _():
        grad_one[...] = whole[0:3456].astype(F32) * scale
        grad_two[...] = other[0:3456].astype(F32) * scale

    @pl.when(core[0] == 1)
    def _():
        grad_one[...] = other[0:3456].astype(F32) * scale
        grad_two[...] = whole[0:3456].astype(F32) * scale


def in_hbm(array):
    return pltpu.with_memory_space_constraint(array, pltpu.HBM)


def call(kernel, out_shapes, scratch, flops, *operands):
    shapes = [pltpu.HBM(*s[:2]) if s[2:] else jax.ShapeDtypeStruct(*s) for s in out_shapes]
    moved = sum(o.size * o.dtype.itemsize for o in operands)
    return pl.pallas_call(
        kernel,
        out_shape=shapes,
        in_specs=[
            pl.BlockSpec(memory_space=pltpu.SMEM if o.dtype == jnp.int32 else pltpu.VMEM) for o in operands
        ],
        out_specs=[pl.BlockSpec(memory_space=pltpu.VMEM)] * len(shapes),
        scratch_shapes=[pltpu.VMEM(s, d) for s, d in scratch],
        compiler_params=pltpu.CompilerParams(vmem_limit_bytes=18 << 20),
        cost_estimate=pl.CostEstimate(flops=flops // 20, bytes_accessed=moved // 20, transcendentals=0),
        name=kernel.__name__,
    )(*operands)


def on_device(features, skip_grad, bottom_grad, conv_one, conv_two, conv_three):
    core = lax.axis_index("c")
    first, last = call(
        first_edge_kernel, [((5, 2, 64, 128), BF16)] * 2, [], 0, in_hbm(features), in_hbm(bottom_grad)
    )
    first, last, first_core, core_ref, chip = lax.optimization_barrier(
        (first, last, core == 0, core.reshape(1), lax.axis_index("x").reshape(1))
    )
    fine_cells = features.size // 128 * lax.axis_size(GX) * lax.axis_size(GY)
    fine_scale = 1.0 / math.sqrt(fine_cells)
    coarse_scale = 1.0 / math.sqrt(fine_cells // 8)
    taps_one = conv_one.reshape(27, 128, 128)
    taps_two = conv_two.reshape(27, 128, 128)
    half_taps = jnp.swapaxes(conv_three.reshape(27, 128, 16), 1, 2).reshape(27, 2, 8, 128)
    half_taps = jnp.where(first_core, half_taps[:, 0], half_taps[:, 1])
    mine = lax.all_to_all(jnp.broadcast_to(half_taps, (16, 27, 8, 128)), GY, 0, 0)

    f_before, f_after = shifted(last, GY, 1), shifted(first, GY, -1)
    low, high = call(
        first_slab_kernel, [((20, 64, 128), BF16)] * 2, [], 4 * 10**11,
        features, f_before, f_after, bottom_grad,
    )
    f_left, f_right = exchange_x(low, high)

    conv_flops = 2 * 1152 * 128 * 1024 * 3
    field = (6, 6, 64, 128)
    block = (4, 4, 64, 128)
    edge = (4, 1, 64, 128)
    field_keep, field_send, slope_one, slope_two, pooled = call(
        forward_kernel,
        [(field, BF16, True), (field, BF16, True), (block, BF16, True), (block, BF16, True), ((2, 2, 32, 128), BF16)],
        [((8, 8, 64, 128), BF16), ((1152, 384), BF16), (field, BF16), ((4, 2, 64, 128), F32)],
        3 * conv_flops, core_ref, features, f_before, f_after, f_left, f_right, taps_one, taps_two,
    )
    field_other = swap_cores(field_send)
    mine, pooled = lax.optimization_barrier((mine, pooled))
    theirs = swap_cores(mine)
    both = jnp.where(first_core, jnp.stack([mine, theirs]), jnp.stack([theirs, mine]))
    taps_three = jnp.transpose(both, (2, 1, 0, 3, 4)).reshape(27, 256, 128)
    p_pieces = halo_pieces(pooled, 2, pooled, pooled)
    bottleneck, bundle, err_two, err_first, err_last = call(
        bottom_kernel,
        [((2, 2, 32, 256), BF16, True), ((24, 32, 128), BF16), (block, BF16), (edge, BF16), (edge, BF16)],
        [((6, 6, 32, 128), BF16), ((4, 4, 32, 256), BF16), ((768, 1152), BF16),
         ((4, 4, 32, 256), BF16), ((64, 128), F32)],
        conv_flops, *p_pieces, bottom_grad, f_before, f_after, f_left, f_right,
        taps_three, in_hbm(slope_two), in_hbm(skip_grad),
    )
    e_before, e_after = shifted(err_last, GY, 1), shifted(err_first, GY, -1)
    low, high = call(slab_kernel, [((1, 6, 64, 128), BF16)] * 2, [], 0, err_two, e_before, e_after)
    bundle, low, high = lax.optimization_barrier((bundle, low, high))
    e_left, e_right = exchange_x(low, high)
    (three,) = call(
        bottom_grads_kernel, [((64, PIECE, 128), BF16)], [((768, 1152), F32)],
        conv_flops // 2, core_ref, bundle, swap_cores(bundle),
    )
    three, e_left, e_right = lax.optimization_barrier((three, e_left, e_right))
    err_one, one_first, one_last, err_keep, err_send = call(
        first_errors_kernel,
        [(block, BF16, True), (edge, BF16, True), (edge, BF16, True), (block, BF16), (block, BF16)],
        [(field, BF16), ((384, 1152), BF16)],
        conv_flops, core_ref, err_two, e_before, e_after, e_left, e_right, taps_two, slope_one,
    )
    err_other = swap_cores(err_send)
    (total,) = call(own_grads_kernel, [((1152, 384), F32)], [], conv_flops, field_keep, err_keep)
    (kept,) = call(
        pair_grads_kernel, [((64, 2 * PIECE, 128), BF16, True)], [((1152, 384), F32)],
        conv_flops, field_other, err_other, total, three,
    )
    kept, one_first, one_last = lax.optimization_barrier((kept, one_first, one_last))
    one_before, one_after = shifted(one_last, GY, 1), shifted(one_first, GY, -1)
    part, three_part = call(
        sum_kernel, [((64, PIECE, 128), BF16, True), ((PIECE, 128), BF16)], [], 0,
        lax.all_to_all(kept, FLAT, 0, 0),
    )
    part, one_before, one_after = lax.optimization_barrier((part, one_before, one_after))
    low, high = call(slab_kernel, [((1, 6, 64, 128), BF16)] * 2, [], 0, err_one, one_before, one_after)
    one_left, one_right = exchange_x(low, high)
    whole = lax.all_to_all(part, FLAT, 0, 0).reshape(64 * PIECE, 128)
    both = swap_cores(three_part)
    both = jnp.where(first_core, jnp.stack([three_part, both]), jnp.stack([both, three_part]))
    grad_three = pl.pallas_call(
        functools.partial(place_kernel, scale=coarse_scale),
        out_shape=jax.ShapeDtypeStruct((27, 16, 128), F32),
        in_specs=[pl.BlockSpec(memory_space=pltpu.SMEM)] + [pl.BlockSpec(memory_space=pltpu.VMEM)] * 4,
        out_specs=pl.BlockSpec(memory_space=pltpu.VMEM),
        compiler_params=pltpu.CompilerParams(vmem_limit_bytes=8 << 20),
        name="place_kernel",
    )(chip, *ring_pieces([both] * 4, "x"))
    whole, grad_three, one_left, one_right = lax.optimization_barrier(
        (whole, grad_three, one_left, one_right)
    )
    (input_grad,) = call(
        input_kernel, [(block, BF16, True)], [(field, BF16), ((384, 1152), BF16)],
        conv_flops // 4, in_hbm(err_one), in_hbm(one_before), in_hbm(one_after), one_left, one_right,
        in_hbm(taps_one),
    )
    grad_three = jnp.swapaxes(grad_three, 1, 2).reshape(3, 3, 3, 128, 16)
    grad_one, grad_two = pl.pallas_call(
        functools.partial(finish_kernel, scale=fine_scale),
        out_shape=[jax.ShapeDtypeStruct((3456, 128), F32)] * 2,
        in_specs=[pl.BlockSpec(memory_space=pltpu.SMEM)] + [pl.BlockSpec(memory_space=pltpu.VMEM)] * 2,
        out_specs=[pl.BlockSpec(memory_space=pltpu.VMEM)] * 2,
        compiler_params=pltpu.CompilerParams(vmem_limit_bytes=8 << 20),
        name="finish_kernel",
    )(core_ref, whole, swap_cores(whole))
    grad_one = grad_one.reshape(3, 3, 3, 128, 128)
    grad_two = grad_two.reshape(3, 3, 3, 128, 128)
    return (bottleneck, input_grad, grad_one, grad_two, grad_three)


def solution(mesh):
    fine = Mesh(mesh.devices.reshape(4, 2, 4, 4), ("x", "c", "z", "y"))
    cells = P(GX, GY, None, None)
    outs = P(None, None, None, None, GY)
    return jax.shard_map(
        on_device,
        mesh=fine,
        in_specs=(cells, cells, cells, P(), P(), outs),
        out_specs=(cells, cells, P(), P(), outs),
        check_vma=False,
    )
```

```python
import functools
import math

import jax
import jax.numpy as jnp
from jax import lax
from jax.experimental import pallas as pl
from jax.experimental.pallas import tpu as pltpu
from jax.sharding import Mesh
from jax.sharding import PartitionSpec as P

GX = ("x", "c")
GY = ("z", "y")
FLAT = ("x", "z", "y")
F32 = jnp.float32
BF16 = jnp.bfloat16
PIECE = 56


def shifted(array, axes, step):
    count = lax.axis_size(axes)
    return lax.ppermute(array, axes, [(i, (i + step) % count) for i in range(count)])


def swap_cores(array):
    return lax.ppermute(array, "c", [(0, 1), (1, 0)])


def ring_pieces(pieces, axis):
    sent = [lax.ppermute(pieces[d], axis, [(i, (i + d) % 4) for i in range(4)]) for d in (1, 2, 3)]
    return [pieces[0]] + sent


def slab_kernel(own, before, after, low, high):
    width, size_x = low.shape[0], own.shape[0]
    for slab, start in ((low, 0), (high, size_x - width)):
        rows = slice(start, start + width)
        columns = 0
        for part in (before, own, after):
            slab[:, columns : columns + part.shape[1]] = part[rows]
            columns += part.shape[1]


def first_edge_kernel(own, grads, first, last):
    for edge, start in ((first, 0), (last, 1)):
        edge[0:4] = own[:, 2 * start : 2 * start + 2]
        for half in range(2):
            edge[4, :, half * 32 : half * 32 + 32] = grads[:, start, :, half * 128 : half * 128 + 128]


def first_slab_kernel(own, before, after, grads, low, high):
    for slab, start, row in ((low, 0, 0), (high, 2, 1)):
        for at in range(2):
            slab[at * 8 : at * 8 + 2] = before[start + at]
            slab[at * 8 + 2 : at * 8 + 6] = own[start + at]
            slab[at * 8 + 6 : at * 8 + 8] = after[start + at]
        slab[16] = before[4, row]
        slab[19] = after[4, row]
        for at_y in range(2):
            for half in range(2):
                part = grads[row, at_y, :, half * 128 : half * 128 + 128]
                slab[17 + at_y, half * 32 : half * 32 + 32] = part


def exchange_x(low, high):
    return shifted(high, GX, 1), shifted(low, GX, -1)


def halo_pieces(own, width, first, last):
    before, after = shifted(last, GY, 1), shifted(first, GY, -1)
    size_x, size_y, size_z, chans = own.shape
    slab = (width, size_y + 2 * width, size_z, chans)
    low, high = call(slab_kernel, [(slab, BF16)] * 2, [], 0, own, before, after)
    return own, before, after, *exchange_x(low, high)


def fill_padded(padded, own, before, after, left, right):
    size_x, size_y = own.shape[0], own.shape[1]
    width = left.shape[0]
    padded[0:width] = left[...]
    padded[width + size_x : 2 * width + size_x] = right[...]
    middle = slice(width, width + size_x)
    padded[middle, 0:width] = before[...]
    padded[middle, width : width + size_y] = own[...]
    padded[middle, width + size_y : 2 * width + size_y] = after[...]


def slope_and_silu(values):
    sigma = 1.0 / (1.0 + jnp.exp(-values))
    return values * sigma, sigma * (1.0 + values * (1.0 - sigma))


def window_rows(source, row, count, skip=0, rows=1):
    pieces = []
    for kx in range(3):
        for ky in range(3):
            block = source[pl.ds(row + kx + skip, rows), ky + skip : ky + skip + count]
            pieces.append(block.reshape(rows * block.shape[1] * block.shape[2], block.shape[3]))
    return jnp.concatenate(pieces, axis=1)


def roll_z(values, step):
    return pltpu.roll(values, step % values.shape[1], 1)


def join_taps(product, count, size_z, chans):
    parts = product.reshape(count, size_z, 3 * chans)
    return (
        roll_z(parts[:, :, 0:chans], 1)
        + parts[:, :, chans : 2 * chans]
        + roll_z(parts[:, :, 2 * chans : 3 * chans], -1)
    )


def spread_errors(errors):
    count, size_z, chans = errors.shape
    parts = [roll_z(errors, -1), errors, roll_z(errors, 1)]
    return jnp.concatenate([p.reshape(count * size_z, chans) for p in parts], axis=1).astype(BF16)


def fill_forward(packed, taps):
    for kx in range(3):
        for ky in range(3):
            for kz in range(3):
                at = kx * 3 + ky
                packed[at * 128 : at * 128 + 128, kz * 128 : kz * 128 + 128] = taps[at * 3 + kz]


def fill_backward(packed, taps):
    for kx in range(3):
        for ky in range(3):
            for kz in range(3):
                at = kx * 3 + ky
                packed[kz * 128 : kz * 128 + 128, at * 128 : at * 128 + 128] = taps[26 - at * 3 - kz]


def dot_nn(left, right):
    return lax.dot_general(left, right, (((1,), (0,)), ((), ())), preferred_element_type=F32)


def dot_nt(left, right):
    return lax.dot_general(left, right, (((1,), (1,)), ((), ())), preferred_element_type=F32)


def dot_tn(left, right):
    return lax.dot_general(left, right, (((0,), (0,)), ((), ())), preferred_element_type=F32)


def forward_kernel(core, own, before, after, left, right, taps_one, taps_two,
                   field_keep, field_send, slope_one, slope_two, pooled,
                   padded, packed, act_one, halves):
    for at in range(2):
        padded[at] = left[at * 8 : at * 8 + 8]
        padded[6 + at] = right[at * 8 : at * 8 + 8]
    padded[2:6, 0:2] = before[0:4]
    padded[2:6, 2:6] = own[...]
    padded[2:6, 6:8] = after[0:4]
    fill_forward(packed, taps_one)
    first_core = core[0] == 0

    def first(step, _):
        product = dot_nn(window_rows(padded, step * 2, 6, rows=2), packed[...])
        act, slope = slope_and_silu(join_taps(product, 12, 64, 128))
        act = act.astype(BF16)
        for at in range(2):
            row = step * 2 + at
            part = act[6 * at : 6 * at + 6]
            field = padded[row + 1, 1:7]
            act_one[row] = part
            field_keep[row] = jnp.where(first_core, field, part)
            field_send[row] = jnp.where(first_core, part, field)

            @pl.when((row >= 1) & (row <= 4))
            def _():
                slope_one[row - 1] = slope[6 * at + 1 : 6 * at + 5].astype(BF16)

        return 0

    lax.fori_loop(0, 3, first, 0)
    fill_forward(packed, taps_two)

    def second(step, _):
        product = dot_nn(window_rows(act_one, step * 2, 4, rows=2), packed[...])
        act, slope = slope_and_silu(join_taps(product, 8, 64, 128))
        slope = slope.astype(BF16)
        act = act.astype(BF16).astype(F32)
        for at in range(2):
            row = step * 2 + at
            slope_two[row] = slope[4 * at : 4 * at + 4]
            halves[row] = act[4 * at : 4 * at + 4].reshape(2, 2, 64, 128).sum(axis=1)
        return 0

    lax.fori_loop(0, 2, second, 0)
    for at_x in range(2):
        for at_y in range(2):
            total = 0.0
            for part in range(2):
                for start in range(2):
                    total = total + halves[2 * at_x + part, at_y, pl.ds(start, 32, stride=2), :]
            pooled[at_x, at_y] = (total * 0.125).astype(BF16)


def bottom_kernel(own, before, after, left, right, g_own, f_before, f_after, f_left, f_right,
                  taps_three, slope_two, skip, bottleneck, bundle, err_two, err_first, err_last,
                  padded, grads, packed, errors, wide):
    fill_padded(padded, own, before, after, left, right)
    for half in range(2):
        rows, lanes = slice(half * 32, half * 32 + 32), slice(half * 128, half * 128 + 128)
        grads[0, :, :, lanes] = f_left[16:20, rows]
        grads[3, :, :, lanes] = f_right[16:20, rows]
        for at in range(2):
            grads[1 + at, 0, :, lanes] = f_before[4, at, rows]
            grads[1 + at, 3, :, lanes] = f_after[4, at, rows]
    grads[1:3, 1:3] = g_own[...]
    for at in range(9):
        for kz in range(3):
            packed[kz * 256 : kz * 256 + 256, at * 128 : at * 128 + 128] = taps_three[at * 3 + kz]
    product = dot_nt(window_rows(padded, 0, 4, rows=4), packed[...])
    acts, slopes = slope_and_silu(join_taps(product, 16, 32, 256))
    for row in range(4):
        columns = slice(4 * row, 4 * row + 4)
        if row in (1, 2):
            bottleneck[row - 1] = acts[columns][1:3].astype(BF16)
        errs = (grads[row].astype(F32) * slopes[columns]).astype(BF16)
        errors[row] = errs
        bundle[row * 4 : row * 4 + 4] = padded[row + 1, 1:5]
        if row in (1, 2):
            for at_y in range(2):
                for half in range(2):
                    at = 16 + ((row - 1) * 2 + at_y) * 2 + half
                    bundle[at] = errs[1 + at_y, :, half * 128 : half * 128 + 128]
    total = jnp.zeros((128, 384), F32)
    for kx in range(3):
        for ky in range(3):
            block = errors[kx : kx + 2, ky : ky + 2].reshape(128, 256)
            at = kx * 3 + ky
            back = jnp.concatenate([taps_three[26 - at * 3 - kz] for kz in range(3)], axis=1)
            total = total + dot_nn(block, back)
    upwards = join_taps(total, 4, 32, 128) * 0.125
    for row in range(2):
        upward = upwards[2 * row : 2 * row + 2]
        for at_y in range(2):
            wide[pl.ds(0, 32, stride=2), :] = upward[at_y]
            wide[pl.ds(1, 32, stride=2), :] = upward[at_y]
            for dx in range(2):
                for dy in range(2):
                    at = (2 * row + dx, 2 * at_y + dy)
                    err = skip[at].astype(F32) + wide[...]
                    err = (err * slope_two[at].astype(F32)).astype(BF16)
                    err_two[at] = err
                    if dy == at_y:
                        edge = err_first if at_y == 0 else err_last
                        edge[2 * row + dx, 0] = err


def tap_grads(fields, errors):
    spread = spread_errors(errors[...].reshape(16, 64, 128).astype(F32))
    return dot_tn(window_rows(fields, 0, 4, rows=4), spread)


def own_grads_kernel(fields, errors, total):
    total[...] = tap_grads(fields, errors)


def pair_grads_kernel(fields, errors, own_total, three, out, total):
    total[...] = own_total[...] + tap_grads(fields, errors)
    for at in range(9):
        for kz in range(3):
            start = (at * 3 + kz) * 128
            done = 0
            while done < 128:
                piece, row = divmod(start + done, PIECE)
                size = min(PIECE - row, 128 - done)
                rows = slice(at * 128 + done, at * 128 + done + size)
                out[piece, row : row + size] = total[rows, kz * 128 : kz * 128 + 128].astype(BF16)
                done += size
    out[61, 40:PIECE] = jnp.zeros((PIECE - 40, 128), BF16)
    out[62:64, 0:PIECE] = jnp.zeros((2, PIECE, 128), BF16)
    out[:, PIECE : 2 * PIECE] = three[...]


def bottom_grads_kernel(core, own, other, out, total):
    fields, errors = [], []
    for bundle in (own, other):
        for row in range(2):
            columns = []
            for kx in range(3):
                for ky in range(3):
                    at = (row + kx) * 4 + ky
                    columns.append(bundle[at : at + 2].reshape(64, 128))
            fields.append(jnp.concatenate(columns, axis=1))
            for at_y in range(2):
                at = 16 + row * 4 + 2 * at_y
                errors.append(jnp.concatenate([bundle[at], bundle[at + 1]], axis=1).reshape(1, 32, 256))
    errors = jnp.concatenate(errors, axis=0).astype(F32)
    total[...] = dot_tn(spread_errors(errors), jnp.concatenate(fields, axis=0))
    first_core = core[0] == 0
    out[48:64, 48:56] = jnp.zeros((16, 8, 128), BF16)
    for unit in range(27):
        at_x, rows = unit // 7, unit % 7 * 8
        at, kz = unit // 3, unit % 3
        block = total[kz * 256 : kz * 256 + 256, at * 128 : at * 128 + 128]
        block = block.reshape(16, 2, 8, 128)
        block = jnp.where(first_core, block[:, 0], block[:, 1]).astype(BF16)
        out[at_x * 16 : at_x * 16 + 16, rows : rows + 8] = block


def first_errors_kernel(core, own, before, after, left, right, taps_two, slope_one,
                        err_one, err_first, err_last, err_keep, err_send, padded, packed):
    fill_padded(padded, own, before, after, left, right)
    fill_backward(packed, taps_two)
    first_core = core[0] == 0

    def step(at, _):
        product = dot_nt(window_rows(padded, at * 2, 4, rows=2), packed[...])
        back = join_taps(product, 8, 64, 128)
        for half in range(2):
            row = at * 2 + half
            first = back[4 * half : 4 * half + 4] * slope_one[row].astype(F32)
            first, second = first.astype(BF16), own[row]
            err_one[row] = first
            err_first[row] = first[0:1]
            err_last[row] = first[3:4]
            err_keep[row] = jnp.where(first_core, first, second)
            err_send[row] = jnp.where(first_core, second, first)
        return 0

    lax.fori_loop(0, 2, step, 0)


def input_kernel(own, before, after, left, right, taps_one, out, padded, packed):
    fill_padded(padded, own, before, after, left, right)
    fill_backward(packed, taps_one)

    def step(at, _):
        product = dot_nt(window_rows(padded, at * 2, 4, rows=2), packed[...])
        out[pl.ds(at * 2, 2)] = join_taps(product, 8, 64, 128).reshape(2, 4, 64, 128).astype(BF16)
        return 0

    lax.fori_loop(0, 2, step, 0)


def sum_kernel(pieces, out, three):
    total = pieces[0].astype(F32)
    for at in range(1, 64):
        total = total + pieces[at].astype(F32)
    total = total.astype(BF16)
    three[...] = total[PIECE : 2 * PIECE]
    for at in range(64):
        out[at] = total[0:PIECE]


def place_kernel(chip, pair_0, pair_1, pair_2, pair_3, out, *, scale):
    for distance, pair in enumerate((pair_0, pair_1, pair_2, pair_3)):
        at = lax.rem(chip[0] + 4 - distance, 4)

        def put(rows, pair=pair, at=at):
            both = [pair[c, rows * 8 : rows * 8 + 8].astype(F32) * scale for c in range(2)]
            out[at * 7 + rows] = jnp.concatenate(both, axis=0)

        for rows in range(6):
            put(rows)
        pl.when(at < 3)(functools.partial(put, 6))


def finish_kernel(core, whole, other, grad_one, grad_two, *, scale):
    @pl.when(core[0] == 0)
    def _():
        grad_one[...] = whole[0:3456].astype(F32) * scale
        grad_two[...] = other[0:3456].astype(F32) * scale

    @pl.when(core[0] == 1)
    def _():
        grad_one[...] = other[0:3456].astype(F32) * scale
        grad_two[...] = whole[0:3456].astype(F32) * scale


def in_hbm(array):
    return pltpu.with_memory_space_constraint(array, pltpu.HBM)


def call(kernel, out_shapes, scratch, flops, *operands):
    shapes = [pltpu.HBM(*s[:2]) if s[2:] else jax.ShapeDtypeStruct(*s) for s in out_shapes]
    moved = sum(o.size * o.dtype.itemsize for o in operands)
    return pl.pallas_call(
        kernel,
        out_shape=shapes,
        in_specs=[
            pl.BlockSpec(memory_space=pltpu.SMEM if o.dtype == jnp.int32 else pltpu.VMEM) for o in operands
        ],
        out_specs=[pl.BlockSpec(memory_space=pltpu.VMEM)] * len(shapes),
        scratch_shapes=[pltpu.VMEM(s, d) for s, d in scratch],
        compiler_params=pltpu.CompilerParams(vmem_limit_bytes=18 << 20),
        cost_estimate=pl.CostEstimate(flops=flops // 20, bytes_accessed=moved // 20, transcendentals=0),
        name=kernel.__name__,
    )(*operands)


def on_device(features, skip_grad, bottom_grad, conv_one, conv_two, conv_three):
    core = lax.axis_index("c")
    first, last = call(
        first_edge_kernel, [((5, 2, 64, 128), BF16)] * 2, [], 0, in_hbm(features), in_hbm(bottom_grad)
    )
    first, last, first_core, core_ref, chip = lax.optimization_barrier(
        (first, last, core == 0, core.reshape(1), lax.axis_index("x").reshape(1))
    )
    fine_cells = features.size // 128 * lax.axis_size(GX) * lax.axis_size(GY)
    fine_scale = 1.0 / math.sqrt(fine_cells)
    coarse_scale = 1.0 / math.sqrt(fine_cells // 8)
    taps_one = conv_one.reshape(27, 128, 128)
    taps_two = conv_two.reshape(27, 128, 128)
    half_taps = jnp.swapaxes(conv_three.reshape(27, 128, 16), 1, 2).reshape(27, 2, 8, 128)
    half_taps = jnp.where(first_core, half_taps[:, 0], half_taps[:, 1])
    mine = lax.all_to_all(jnp.broadcast_to(half_taps, (16, 27, 8, 128)), GY, 0, 0)

    f_before, f_after = shifted(last, GY, 1), shifted(first, GY, -1)
    low, high = call(
        first_slab_kernel, [((20, 64, 128), BF16)] * 2, [], 4 * 10**11,
        features, f_before, f_after, bottom_grad,
    )
    f_left, f_right = exchange_x(low, high)

    conv_flops = 2 * 1152 * 128 * 1024 * 3
    field = (6, 6, 64, 128)
    block = (4, 4, 64, 128)
    edge = (4, 1, 64, 128)
    field_keep, field_send, slope_one, slope_two, pooled = call(
        forward_kernel,
        [(field, BF16, True), (field, BF16, True), (block, BF16, True), (block, BF16, True), ((2, 2, 32, 128), BF16)],
        [((8, 8, 64, 128), BF16), ((1152, 384), BF16), (field, BF16), ((4, 2, 64, 128), F32)],
        3 * conv_flops, core_ref, features, f_before, f_after, f_left, f_right, taps_one, taps_two,
    )
    field_other = swap_cores(field_send)
    mine, pooled = lax.optimization_barrier((mine, pooled))
    theirs = swap_cores(mine)
    both = jnp.where(first_core, jnp.stack([mine, theirs]), jnp.stack([theirs, mine]))
    taps_three = jnp.transpose(both, (2, 1, 0, 3, 4)).reshape(27, 256, 128)
    p_pieces = halo_pieces(pooled, 2, pooled, pooled)
    bottleneck, bundle, err_two, err_first, err_last = call(
        bottom_kernel,
        [((2, 2, 32, 256), BF16, True), ((24, 32, 128), BF16), (block, BF16), (edge, BF16), (edge, BF16)],
        [((6, 6, 32, 128), BF16), ((4, 4, 32, 256), BF16), ((768, 1152), BF16),
         ((4, 4, 32, 256), BF16), ((64, 128), F32)],
        conv_flops, *p_pieces, bottom_grad, f_before, f_after, f_left, f_right,
        taps_three, in_hbm(slope_two), in_hbm(skip_grad),
    )
    e_before, e_after = shifted(err_last, GY, 1), shifted(err_first, GY, -1)
    low, high = call(slab_kernel, [((1, 6, 64, 128), BF16)] * 2, [], 0, err_two, e_before, e_after)
    bundle, low, high = lax.optimization_barrier((bundle, low, high))
    e_left, e_right = exchange_x(low, high)
    (three,) = call(
        bottom_grads_kernel, [((64, PIECE, 128), BF16)], [((768, 1152), F32)],
        conv_flops // 2, core_ref, bundle, swap_cores(bundle),
    )
    three, e_left, e_right = lax.optimization_barrier((three, e_left, e_right))
    err_one, one_first, one_last, err_keep, err_send = call(
        first_errors_kernel,
        [(block, BF16, True), (edge, BF16, True), (edge, BF16, True), (block, BF16), (block, BF16)],
        [(field, BF16), ((384, 1152), BF16)],
        conv_flops, core_ref, err_two, e_before, e_after, e_left, e_right, taps_two, slope_one,
    )
    err_other = swap_cores(err_send)
    (total,) = call(own_grads_kernel, [((1152, 384), F32)], [], conv_flops, field_keep, err_keep)
    (kept,) = call(
        pair_grads_kernel, [((64, 2 * PIECE, 128), BF16, True)], [((1152, 384), F32)],
        conv_flops, field_other, err_other, total, three,
    )
    kept, one_first, one_last = lax.optimization_barrier((kept, one_first, one_last))
    one_before, one_after = shifted(one_last, GY, 1), shifted(one_first, GY, -1)
    part, three_part = call(
        sum_kernel, [((64, PIECE, 128), BF16, True), ((PIECE, 128), BF16)], [], 0,
        lax.all_to_all(kept, FLAT, 0, 0),
    )
    part, one_before, one_after = lax.optimization_barrier((part, one_before, one_after))
    low, high = call(slab_kernel, [((1, 6, 64, 128), BF16)] * 2, [], 0, err_one, one_before, one_after)
    one_left, one_right = exchange_x(low, high)
    whole = lax.all_to_all(part, FLAT, 0, 0).reshape(64 * PIECE, 128)
    both = swap_cores(three_part)
    both = jnp.where(first_core, jnp.stack([three_part, both]), jnp.stack([both, three_part]))
    grad_three = pl.pallas_call(
        functools.partial(place_kernel, scale=coarse_scale),
        out_shape=jax.ShapeDtypeStruct((27, 16, 128), F32),
        in_specs=[pl.BlockSpec(memory_space=pltpu.SMEM)] + [pl.BlockSpec(memory_space=pltpu.VMEM)] * 4,
        out_specs=pl.BlockSpec(memory_space=pltpu.VMEM),
        compiler_params=pltpu.CompilerParams(vmem_limit_bytes=8 << 20),
        name="place_kernel",
    )(chip, *ring_pieces([both] * 4, "x"))
    whole, grad_three, one_left, one_right = lax.optimization_barrier(
        (whole, grad_three, one_left, one_right)
    )
    (input_grad,) = call(
        input_kernel, [(block, BF16, True)], [(field, BF16), ((384, 1152), BF16)],
        conv_flops // 4, in_hbm(err_one), in_hbm(one_before), in_hbm(one_after), one_left, one_right,
        in_hbm(taps_one),
    )
    grad_three = jnp.swapaxes(grad_three, 1, 2).reshape(3, 3, 3, 128, 16)
    grad_one, grad_two = pl.pallas_call(
        functools.partial(finish_kernel, scale=fine_scale),
        out_shape=[jax.ShapeDtypeStruct((3456, 128), F32)] * 2,
        in_specs=[pl.BlockSpec(memory_space=pltpu.SMEM)] + [pl.BlockSpec(memory_space=pltpu.VMEM)] * 2,
        out_specs=[pl.BlockSpec(memory_space=pltpu.VMEM)] * 2,
        compiler_params=pltpu.CompilerParams(vmem_limit_bytes=8 << 20),
        name="finish_kernel",
    )(core_ref, whole, swap_cores(whole))
    grad_one = grad_one.reshape(3, 3, 3, 128, 128)
    grad_two = grad_two.reshape(3, 3, 3, 128, 128)
    return (bottleneck, input_grad, grad_one, grad_two, grad_three)


def solution(mesh):
    fine = Mesh(mesh.devices.reshape(4, 2, 4, 4), ("x", "c", "z", "y"))
    cells = P(GX, GY, None, None)
    outs = P(None, None, None, None, GY)
    return jax.shard_map(
        on_device,
        mesh=fine,
        in_specs=(cells, cells, cells, P(), P(), outs),
        out_specs=(cells, cells, P(), P(), outs),
        check_vma=False,
    )
```

```python
import functools
import math

import jax
import jax.numpy as jnp
from jax import lax
from jax.experimental import pallas as pl
from jax.experimental.pallas import tpu as pltpu
from jax.sharding import Mesh
from jax.sharding import PartitionSpec as P

GX = ("x", "c")
GY = ("z", "y")
FLAT = ("x", "z", "y")
F32 = jnp.float32
BF16 = jnp.bfloat16
PIECE = 56


def shifted(array, axes, step):
    count = lax.axis_size(axes)
    return lax.ppermute(array, axes, [(i, (i + step) % count) for i in range(count)])


def swap_cores(array):
    return lax.ppermute(array, "c", [(0, 1), (1, 0)])


def ring_pieces(pieces, axis):
    sent = [lax.ppermute(pieces[d], axis, [(i, (i + d) % 4) for i in range(4)]) for d in (1, 2, 3)]
    return [pieces[0]] + sent


def slab_kernel(own, before, after, low, high):
    width, size_x = low.shape[0], own.shape[0]
    for slab, start in ((low, 0), (high, size_x - width)):
        rows = slice(start, start + width)
        columns = 0
        for part in (before, own, after):
            slab[:, columns : columns + part.shape[1]] = part[rows]
            columns += part.shape[1]


def first_edge_kernel(own, grads, first, last):
    for edge, start in ((first, 0), (last, 1)):
        edge[0:4] = own[:, 2 * start : 2 * start + 2]
        for half in range(2):
            edge[4, :, half * 32 : half * 32 + 32] = grads[:, start, :, half * 128 : half * 128 + 128]


def first_slab_kernel(own, before, after, grads, low, high):
    for slab, start, row in ((low, 0, 0), (high, 2, 1)):
        for at in range(2):
            slab[at * 8 : at * 8 + 2] = before[start + at]
            slab[at * 8 + 2 : at * 8 + 6] = own[start + at]
            slab[at * 8 + 6 : at * 8 + 8] = after[start + at]
        slab[16] = before[4, row]
        slab[19] = after[4, row]
        for at_y in range(2):
            for half in range(2):
                part = grads[row, at_y, :, half * 128 : half * 128 + 128]
                slab[17 + at_y, half * 32 : half * 32 + 32] = part


def exchange_x(low, high):
    return shifted(high, GX, 1), shifted(low, GX, -1)


def halo_pieces(own, width, first, last):
    before, after = shifted(last, GY, 1), shifted(first, GY, -1)
    size_x, size_y, size_z, chans = own.shape
    slab = (width, size_y + 2 * width, size_z, chans)
    low, high = call(slab_kernel, [(slab, BF16)] * 2, [], 0, own, before, after)
    return own, before, after, *exchange_x(low, high)


def fill_padded(padded, own, before, after, left, right):
    size_x, size_y = own.shape[0], own.shape[1]
    width = left.shape[0]
    padded[0:width] = left[...]
    padded[width + size_x : 2 * width + size_x] = right[...]
    middle = slice(width, width + size_x)
    padded[middle, 0:width] = before[...]
    padded[middle, width : width + size_y] = own[...]
    padded[middle, width + size_y : 2 * width + size_y] = after[...]


def slope_and_silu(values):
    sigma = 1.0 / (1.0 + jnp.exp(-values))
    return values * sigma, sigma * (1.0 + values * (1.0 - sigma))


def window_rows(source, row, count, skip=0, rows=1):
    pieces = []
    for kx in range(3):
        for ky in range(3):
            block = source[pl.ds(row + kx + skip, rows), ky + skip : ky + skip + count]
            pieces.append(block.reshape(rows * block.shape[1] * block.shape[2], block.shape[3]))
    return jnp.concatenate(pieces, axis=1)


def roll_z(values, step):
    return pltpu.roll(values, step % values.shape[1], 1)


def join_taps(product, count, size_z, chans):
    parts = product.reshape(count, size_z, 3 * chans)
    return (
        roll_z(parts[:, :, 0:chans], 1)
        + parts[:, :, chans : 2 * chans]
        + roll_z(parts[:, :, 2 * chans : 3 * chans], -1)
    )


def spread_errors(errors):
    count, size_z, chans = errors.shape
    parts = [roll_z(errors, -1), errors, roll_z(errors, 1)]
    return jnp.concatenate([p.reshape(count * size_z, chans) for p in parts], axis=1).astype(BF16)


def fill_forward(packed, taps):
    for kx in range(3):
        for ky in range(3):
            for kz in range(3):
                at = kx * 3 + ky
                packed[at * 128 : at * 128 + 128, kz * 128 : kz * 128 + 128] = taps[at * 3 + kz]


def fill_backward(packed, taps):
    for kx in range(3):
        for ky in range(3):
            for kz in range(3):
                at = kx * 3 + ky
                packed[kz * 128 : kz * 128 + 128, at * 128 : at * 128 + 128] = taps[26 - at * 3 - kz]


def dot_nn(left, right):
    return lax.dot_general(left, right, (((1,), (0,)), ((), ())), preferred_element_type=F32)


def dot_nt(left, right):
    return lax.dot_general(left, right, (((1,), (1,)), ((), ())), preferred_element_type=F32)


def dot_tn(left, right):
    return lax.dot_general(left, right, (((0,), (0,)), ((), ())), preferred_element_type=F32)


def forward_kernel(core, own, before, after, left, right, taps_one, taps_two,
                   field_keep, field_send, slope_one, slope_two, pooled,
                   padded, packed, act_one, halves):
    for at in range(2):
        padded[at] = left[at * 8 : at * 8 + 8]
        padded[6 + at] = right[at * 8 : at * 8 + 8]
    padded[2:6, 0:2] = before[0:4]
    padded[2:6, 2:6] = own[...]
    padded[2:6, 6:8] = after[0:4]
    fill_forward(packed, taps_one)
    first_core = core[0] == 0

    def first(step, _):
        product = dot_nn(window_rows(padded, step * 2, 6, rows=2), packed[...])
        act, slope = slope_and_silu(join_taps(product, 12, 64, 128))
        act = act.astype(BF16)
        for at in range(2):
            row = step * 2 + at
            part = act[6 * at : 6 * at + 6]
            field = padded[row + 1, 1:7]
            act_one[row] = part
            field_keep[row] = jnp.where(first_core, field, part)
            field_send[row] = jnp.where(first_core, part, field)

            @pl.when((row >= 1) & (row <= 4))
            def _():
                slope_one[row - 1] = slope[6 * at + 1 : 6 * at + 5].astype(BF16)

        return 0

    lax.fori_loop(0, 3, first, 0)
    fill_forward(packed, taps_two)

    def second(step, _):
        product = dot_nn(window_rows(act_one, step * 2, 4, rows=2), packed[...])
        act, slope = slope_and_silu(join_taps(product, 8, 64, 128))
        slope = slope.astype(BF16)
        act = act.astype(BF16).astype(F32)
        for at in range(2):
            row = step * 2 + at
            slope_two[row] = slope[4 * at : 4 * at + 4]
            halves[row] = act[4 * at : 4 * at + 4].reshape(2, 2, 64, 128).sum(axis=1)
        return 0

    lax.fori_loop(0, 2, second, 0)
    for at_x in range(2):
        for at_y in range(2):
            total = 0.0
            for part in range(2):
                for start in range(2):
                    total = total + halves[2 * at_x + part, at_y, pl.ds(start, 32, stride=2), :]
            pooled[at_x, at_y] = (total * 0.125).astype(BF16)


def bottom_kernel(own, before, after, left, right, g_own, f_before, f_after, f_left, f_right,
                  taps_three, slope_two, skip, bottleneck, bundle, err_two, err_first, err_last,
                  padded, grads, packed, errors, wide):
    fill_padded(padded, own, before, after, left, right)
    for half in range(2):
        rows, lanes = slice(half * 32, half * 32 + 32), slice(half * 128, half * 128 + 128)
        grads[0, :, :, lanes] = f_left[16:20, rows]
        grads[3, :, :, lanes] = f_right[16:20, rows]
        for at in range(2):
            grads[1 + at, 0, :, lanes] = f_before[4, at, rows]
            grads[1 + at, 3, :, lanes] = f_after[4, at, rows]
    grads[1:3, 1:3] = g_own[...]
    for at in range(9):
        for kz in range(3):
            packed[kz * 256 : kz * 256 + 256, at * 128 : at * 128 + 128] = taps_three[at * 3 + kz]
    product = dot_nt(window_rows(padded, 0, 4, rows=4), packed[...])
    acts, slopes = slope_and_silu(join_taps(product, 16, 32, 256))
    for row in range(4):
        columns = slice(4 * row, 4 * row + 4)
        if row in (1, 2):
            bottleneck[row - 1] = acts[columns][1:3].astype(BF16)
        errs = (grads[row].astype(F32) * slopes[columns]).astype(BF16)
        errors[row] = errs
        bundle[row * 4 : row * 4 + 4] = padded[row + 1, 1:5]
        if row in (1, 2):
            for at_y in range(2):
                for half in range(2):
                    at = 16 + ((row - 1) * 2 + at_y) * 2 + half
                    bundle[at] = errs[1 + at_y, :, half * 128 : half * 128 + 128]
    total = jnp.zeros((128, 384), F32)
    for kx in range(3):
        for ky in range(3):
            block = errors[kx : kx + 2, ky : ky + 2].reshape(128, 256)
            at = kx * 3 + ky
            back = jnp.concatenate([taps_three[26 - at * 3 - kz] for kz in range(3)], axis=1)
            total = total + dot_nn(block, back)
    upwards = join_taps(total, 4, 32, 128) * 0.125
    for row in range(2):
        upward = upwards[2 * row : 2 * row + 2]
        for at_y in range(2):
            wide[pl.ds(0, 32, stride=2), :] = upward[at_y]
            wide[pl.ds(1, 32, stride=2), :] = upward[at_y]
            for dx in range(2):
                for dy in range(2):
                    at = (2 * row + dx, 2 * at_y + dy)
                    err = skip[at].astype(F32) + wide[...]
                    err = (err * slope_two[at].astype(F32)).astype(BF16)
                    err_two[at] = err
                    if dy == at_y:
                        edge = err_first if at_y == 0 else err_last
                        edge[2 * row + dx, 0] = err


def tap_grads(fields, errors):
    spread = spread_errors(errors[...].reshape(16, 64, 128).astype(F32))
    return dot_tn(window_rows(fields, 0, 4, rows=4), spread)


def own_grads_kernel(fields, errors, total):
    total[...] = tap_grads(fields, errors)


def pair_grads_kernel(fields, errors, own_total, three, out, total):
    total[...] = own_total[...] + tap_grads(fields, errors)
    for at in range(9):
        for kz in range(3):
            start = (at * 3 + kz) * 128
            done = 0
            while done < 128:
                piece, row = divmod(start + done, PIECE)
                size = min(PIECE - row, 128 - done)
                rows = slice(at * 128 + done, at * 128 + done + size)
                out[piece, row : row + size] = total[rows, kz * 128 : kz * 128 + 128].astype(BF16)
                done += size
    out[61, 40:PIECE] = jnp.zeros((PIECE - 40, 128), BF16)
    out[62:64, 0:PIECE] = jnp.zeros((2, PIECE, 128), BF16)
    out[:, PIECE : 2 * PIECE] = three[...]


def bottom_grads_kernel(core, own, other, out, total):
    fields, errors = [], []
    for bundle in (own, other):
        for row in range(2):
            columns = []
            for kx in range(3):
                for ky in range(3):
                    at = (row + kx) * 4 + ky
                    columns.append(bundle[at : at + 2].reshape(64, 128))
            fields.append(jnp.concatenate(columns, axis=1))
            for at_y in range(2):
                at = 16 + row * 4 + 2 * at_y
                errors.append(jnp.concatenate([bundle[at], bundle[at + 1]], axis=1).reshape(1, 32, 256))
    errors = jnp.concatenate(errors, axis=0).astype(F32)
    total[...] = dot_tn(spread_errors(errors), jnp.concatenate(fields, axis=0))
    first_core = core[0] == 0
    out[48:64, 48:56] = jnp.zeros((16, 8, 128), BF16)
    for unit in range(27):
        at_x, rows = unit // 7, unit % 7 * 8
        at, kz = unit // 3, unit % 3
        block = total[kz * 256 : kz * 256 + 256, at * 128 : at * 128 + 128]
        block = block.reshape(16, 2, 8, 128)
        block = jnp.where(first_core, block[:, 0], block[:, 1]).astype(BF16)
        out[at_x * 16 : at_x * 16 + 16, rows : rows + 8] = block


def first_errors_kernel(core, own, before, after, left, right, taps_two, slope_one,
                        err_one, err_first, err_last, err_keep, err_send, padded, packed):
    fill_padded(padded, own, before, after, left, right)
    fill_backward(packed, taps_two)
    first_core = core[0] == 0

    def step(at, _):
        product = dot_nt(window_rows(padded, at * 2, 4, rows=2), packed[...])
        back = join_taps(product, 8, 64, 128)
        for half in range(2):
            row = at * 2 + half
            first = back[4 * half : 4 * half + 4] * slope_one[row].astype(F32)
            first, second = first.astype(BF16), own[row]
            err_one[row] = first
            err_first[row] = first[0:1]
            err_last[row] = first[3:4]
            err_keep[row] = jnp.where(first_core, first, second)
            err_send[row] = jnp.where(first_core, second, first)
        return 0

    lax.fori_loop(0, 2, step, 0)


def inner_input_kernel(own, before, after, taps_one, out, padded, packed):
    padded[:, 0:1] = before[...]
    padded[:, 1:5] = own[...]
    padded[:, 5:6] = after[...]
    fill_backward(packed, taps_one)
    product = dot_nt(window_rows(padded, 0, 4, rows=2), packed[...])
    out[...] = join_taps(product, 8, 64, 128).reshape(2, 4, 64, 128).astype(BF16)


def outer_input_kernel(own, before, after, left, right, taps_one, inner, out, padded, packed):
    fill_padded(padded, own, before, after, left, right)
    fill_backward(packed, taps_one)
    out[1:3] = inner[...]
    windows = [window_rows(padded, 0, 4), window_rows(padded, 3, 4)]
    product = dot_nt(jnp.concatenate(windows, axis=0), packed[...])
    rows = join_taps(product, 8, 64, 128).astype(BF16)
    out[0] = rows[0:4]
    out[3] = rows[4:8]


def sum_kernel(pieces, out, three):
    total = pieces[0].astype(F32)
    for at in range(1, 64):
        total = total + pieces[at].astype(F32)
    total = total.astype(BF16)
    three[...] = total[PIECE : 2 * PIECE]
    for at in range(64):
        out[at] = total[0:PIECE]


def place_kernel(chip, pair_0, pair_1, pair_2, pair_3, out, *, scale):
    for distance, pair in enumerate((pair_0, pair_1, pair_2, pair_3)):
        at = lax.rem(chip[0] + 4 - distance, 4)

        def put(rows, pair=pair, at=at):
            both = [pair[c, rows * 8 : rows * 8 + 8].astype(F32) * scale for c in range(2)]
            out[at * 7 + rows] = jnp.concatenate(both, axis=0)

        for rows in range(6):
            put(rows)
        pl.when(at < 3)(functools.partial(put, 6))


def finish_kernel(core, whole, other, grad_one, grad_two, *, scale):
    @pl.when(core[0] == 0)
    def _():
        grad_one[...] = whole[0:3456].astype(F32) * scale
        grad_two[...] = other[0:3456].astype(F32) * scale

    @pl.when(core[0] == 1)
    def _():
        grad_one[...] = other[0:3456].astype(F32) * scale
        grad_two[...] = whole[0:3456].astype(F32) * scale


def in_hbm(array):
    return pltpu.with_memory_space_constraint(array, pltpu.HBM)


def call(kernel, out_shapes, scratch, flops, *operands):
    shapes = [pltpu.HBM(*s[:2]) if s[2:] else jax.ShapeDtypeStruct(*s) for s in out_shapes]
    moved = sum(o.size * o.dtype.itemsize for o in operands)
    return pl.pallas_call(
        kernel,
        out_shape=shapes,
        in_specs=[
            pl.BlockSpec(memory_space=pltpu.SMEM if o.dtype == jnp.int32 else pltpu.VMEM) for o in operands
        ],
        out_specs=[pl.BlockSpec(memory_space=pltpu.VMEM)] * len(shapes),
        scratch_shapes=[pltpu.VMEM(s, d) for s, d in scratch],
        compiler_params=pltpu.CompilerParams(vmem_limit_bytes=18 << 20),
        cost_estimate=pl.CostEstimate(flops=flops // 20, bytes_accessed=moved // 20, transcendentals=0),
        name=kernel.__name__,
    )(*operands)


def on_device(features, skip_grad, bottom_grad, conv_one, conv_two, conv_three):
    core = lax.axis_index("c")
    first, last = call(
        first_edge_kernel, [((5, 2, 64, 128), BF16)] * 2, [], 0, in_hbm(features), in_hbm(bottom_grad)
    )
    first, last, first_core, core_ref, chip = lax.optimization_barrier(
        (first, last, core == 0, core.reshape(1), lax.axis_index("x").reshape(1))
    )
    fine_cells = features.size // 128 * lax.axis_size(GX) * lax.axis_size(GY)
    fine_scale = 1.0 / math.sqrt(fine_cells)
    coarse_scale = 1.0 / math.sqrt(fine_cells // 8)
    taps_one = conv_one.reshape(27, 128, 128)
    taps_two = conv_two.reshape(27, 128, 128)
    half_taps = jnp.swapaxes(conv_three.reshape(27, 128, 16), 1, 2).reshape(27, 2, 8, 128)
    half_taps = jnp.where(first_core, half_taps[:, 0], half_taps[:, 1])
    mine = lax.all_to_all(jnp.broadcast_to(half_taps, (16, 27, 8, 128)), GY, 0, 0)

    f_before, f_after = shifted(last, GY, 1), shifted(first, GY, -1)
    low, high = call(
        first_slab_kernel, [((20, 64, 128), BF16)] * 2, [], 4 * 10**11,
        features, f_before, f_after, bottom_grad,
    )
    f_left, f_right = exchange_x(low, high)

    conv_flops = 2 * 1152 * 128 * 1024 * 3
    field = (6, 6, 64, 128)
    block = (4, 4, 64, 128)
    edge = (4, 1, 64, 128)
    field_keep, field_send, slope_one, slope_two, pooled = call(
        forward_kernel,
        [(field, BF16, True), (field, BF16, True), (block, BF16, True), (block, BF16, True), ((2, 2, 32, 128), BF16)],
        [((8, 8, 64, 128), BF16), ((1152, 384), BF16), (field, BF16), ((4, 2, 64, 128), F32)],
        3 * conv_flops, core_ref, features, f_before, f_after, f_left, f_right, taps_one, taps_two,
    )
    field_other = swap_cores(field_send)
    mine, pooled = lax.optimization_barrier((mine, pooled))
    theirs = swap_cores(mine)
    both = jnp.where(first_core, jnp.stack([mine, theirs]), jnp.stack([theirs, mine]))
    taps_three = jnp.transpose(both, (2, 1, 0, 3, 4)).reshape(27, 256, 128)
    p_pieces = halo_pieces(pooled, 2, pooled, pooled)
    bottleneck, bundle, err_two, err_first, err_last = call(
        bottom_kernel,
        [((2, 2, 32, 256), BF16, True), ((24, 32, 128), BF16), (block, BF16), (edge, BF16), (edge, BF16)],
        [((6, 6, 32, 128), BF16), ((4, 4, 32, 256), BF16), ((768, 1152), BF16),
         ((4, 4, 32, 256), BF16), ((64, 128), F32)],
        conv_flops, *p_pieces, bottom_grad, f_before, f_after, f_left, f_right,
        taps_three, in_hbm(slope_two), in_hbm(skip_grad),
    )
    e_before, e_after = shifted(err_last, GY, 1), shifted(err_first, GY, -1)
    low, high = call(slab_kernel, [((1, 6, 64, 128), BF16)] * 2, [], 0, err_two, e_before, e_after)
    bundle, low, high = lax.optimization_barrier((bundle, low, high))
    e_left, e_right = exchange_x(low, high)
    (three,) = call(
        bottom_grads_kernel, [((64, PIECE, 128), BF16)], [((768, 1152), F32)],
        conv_flops // 2, core_ref, bundle, swap_cores(bundle),
    )
    three, e_left, e_right = lax.optimization_barrier((three, e_left, e_right))
    err_one, one_first, one_last, err_keep, err_send = call(
        first_errors_kernel,
        [(block, BF16, True), (edge, BF16, True), (edge, BF16, True), (block, BF16), (block, BF16)],
        [(field, BF16), ((384, 1152), BF16)],
        conv_flops, core_ref, err_two, e_before, e_after, e_left, e_right, taps_two, slope_one,
    )
    err_other = swap_cores(err_send)
    (total,) = call(own_grads_kernel, [((1152, 384), F32)], [], conv_flops, field_keep, err_keep)
    (kept,) = call(
        pair_grads_kernel, [((64, 2 * PIECE, 128), BF16, True)], [((1152, 384), F32)],
        conv_flops, field_other, err_other, total, three,
    )
    kept, one_first, one_last = lax.optimization_barrier((kept, one_first, one_last))
    one_before, one_after = shifted(one_last, GY, 1), shifted(one_first, GY, -1)
    part, three_part = call(
        sum_kernel, [((64, PIECE, 128), BF16, True), ((PIECE, 128), BF16)], [], 0,
        lax.all_to_all(kept, FLAT, 0, 0),
    )
    part, one_before, one_after = lax.optimization_barrier((part, one_before, one_after))
    low, high = call(slab_kernel, [((1, 6, 64, 128), BF16)] * 2, [], 0, err_one, one_before, one_after)
    one_left, one_right = exchange_x(low, high)
    whole = lax.all_to_all(part, FLAT, 0, 0).reshape(64 * PIECE, 128)
    both = swap_cores(three_part)
    both = jnp.where(first_core, jnp.stack([three_part, both]), jnp.stack([both, three_part]))
    grad_three = pl.pallas_call(
        functools.partial(place_kernel, scale=coarse_scale),
        out_shape=jax.ShapeDtypeStruct((27, 16, 128), F32),
        in_specs=[pl.BlockSpec(memory_space=pltpu.SMEM)] + [pl.BlockSpec(memory_space=pltpu.VMEM)] * 4,
        out_specs=pl.BlockSpec(memory_space=pltpu.VMEM),
        compiler_params=pltpu.CompilerParams(vmem_limit_bytes=8 << 20),
        name="place_kernel",
    )(chip, *ring_pieces([both] * 4, "x"))
    (inner,) = call(
        inner_input_kernel, [((2, 4, 64, 128), BF16, True)], [((4, 6, 64, 128), BF16), ((384, 1152), BF16)],
        conv_flops // 4, err_one, one_before, one_after, taps_one,
    )
    whole, grad_three, one_left, one_right, inner = lax.optimization_barrier(
        (whole, grad_three, one_left, one_right, inner)
    )
    (input_grad,) = call(
        outer_input_kernel, [(block, BF16, True)], [(field, BF16), ((384, 1152), BF16)],
        conv_flops // 4, in_hbm(err_one), in_hbm(one_before), in_hbm(one_after), one_left, one_right,
        in_hbm(taps_one), in_hbm(inner),
    )
    grad_three = jnp.swapaxes(grad_three, 1, 2).reshape(3, 3, 3, 128, 16)
    grad_one, grad_two = pl.pallas_call(
        functools.partial(finish_kernel, scale=fine_scale),
        out_shape=[jax.ShapeDtypeStruct((3456, 128), F32)] * 2,
        in_specs=[pl.BlockSpec(memory_space=pltpu.SMEM)] + [pl.BlockSpec(memory_space=pltpu.VMEM)] * 2,
        out_specs=[pl.BlockSpec(memory_space=pltpu.VMEM)] * 2,
        compiler_params=pltpu.CompilerParams(vmem_limit_bytes=8 << 20),
        name="finish_kernel",
    )(core_ref, whole, swap_cores(whole))
    grad_one = grad_one.reshape(3, 3, 3, 128, 128)
    grad_two = grad_two.reshape(3, 3, 3, 128, 128)
    return (bottleneck, input_grad, grad_one, grad_two, grad_three)


def solution(mesh):
    fine = Mesh(mesh.devices.reshape(4, 2, 4, 4), ("x", "c", "z", "y"))
    cells = P(GX, GY, None, None)
    outs = P(None, None, None, None, GY)
    return jax.shard_map(
        on_device,
        mesh=fine,
        in_specs=(cells, cells, cells, P(), P(), outs),
        out_specs=(cells, cells, P(), P(), outs),
        check_vma=False,
    )
```

```python
import functools
import math

import jax
import jax.numpy as jnp
from jax import lax
from jax.experimental import pallas as pl
from jax.experimental.pallas import tpu as pltpu
from jax.sharding import Mesh
from jax.sharding import PartitionSpec as P

GX = ("x", "c")
GY = ("z", "y")
FLAT = ("x", "z", "y")
F32 = jnp.float32
BF16 = jnp.bfloat16
PIECE = 56


def shifted(array, axes, step):
    count = lax.axis_size(axes)
    return lax.ppermute(array, axes, [(i, (i + step) % count) for i in range(count)])


def swap_cores(array):
    return lax.ppermute(array, "c", [(0, 1), (1, 0)])


def ring_pieces(pieces, axis):
    sent = [lax.ppermute(pieces[d], axis, [(i, (i + d) % 4) for i in range(4)]) for d in (1, 2, 3)]
    return [pieces[0]] + sent


def slab_kernel(own, before, after, low, high):
    width, size_x = low.shape[0], own.shape[0]
    for slab, start in ((low, 0), (high, size_x - width)):
        rows = slice(start, start + width)
        columns = 0
        for part in (before, own, after):
            slab[:, columns : columns + part.shape[1]] = part[rows]
            columns += part.shape[1]


def first_edge_kernel(own, grads, first, last):
    for edge, start in ((first, 0), (last, 1)):
        edge[0:4] = own[:, 2 * start : 2 * start + 2]
        for half in range(2):
            edge[4, :, half * 32 : half * 32 + 32] = grads[:, start, :, half * 128 : half * 128 + 128]


def first_slab_kernel(own, before, after, grads, low, high):
    for slab, start, row in ((low, 0, 0), (high, 2, 1)):
        for at in range(2):
            slab[at * 8 : at * 8 + 2] = before[start + at]
            slab[at * 8 + 2 : at * 8 + 6] = own[start + at]
            slab[at * 8 + 6 : at * 8 + 8] = after[start + at]
        slab[16] = before[4, row]
        slab[19] = after[4, row]
        for at_y in range(2):
            for half in range(2):
                part = grads[row, at_y, :, half * 128 : half * 128 + 128]
                slab[17 + at_y, half * 32 : half * 32 + 32] = part


def exchange_x(low, high):
    return shifted(high, GX, 1), shifted(low, GX, -1)


def fill_padded(padded, own, before, after, left, right):
    size_x, size_y = own.shape[0], own.shape[1]
    width = left.shape[0]
    padded[0:width] = left[...]
    padded[width + size_x : 2 * width + size_x] = right[...]
    middle = slice(width, width + size_x)
    padded[middle, 0:width] = before[...]
    padded[middle, width : width + size_y] = own[...]
    padded[middle, width + size_y : 2 * width + size_y] = after[...]


def slope_and_silu(values):
    sigma = 1.0 / (1.0 + jnp.exp(-values))
    return values * sigma, sigma * (1.0 + values * (1.0 - sigma))


def window_rows(source, row, count, skip=0, rows=1):
    pieces = []
    for kx in range(3):
        for ky in range(3):
            block = source[pl.ds(row + kx + skip, rows), ky + skip : ky + skip + count]
            pieces.append(block.reshape(rows * block.shape[1] * block.shape[2], block.shape[3]))
    return jnp.concatenate(pieces, axis=1)


def roll_z(values, step):
    return pltpu.roll(values, step % values.shape[1], 1)


def join_taps(product, count, size_z, chans):
    parts = product.reshape(count, size_z, 3 * chans)
    return (
        roll_z(parts[:, :, 0:chans], 1)
        + parts[:, :, chans : 2 * chans]
        + roll_z(parts[:, :, 2 * chans : 3 * chans], -1)
    )


def spread_errors(errors):
    count, size_z, chans = errors.shape
    parts = [roll_z(errors, -1), errors, roll_z(errors, 1)]
    return jnp.concatenate([p.reshape(count * size_z, chans) for p in parts], axis=1).astype(BF16)


def fill_forward(packed, taps):
    for kx in range(3):
        for ky in range(3):
            for kz in range(3):
                at = kx * 3 + ky
                packed[at * 128 : at * 128 + 128, kz * 128 : kz * 128 + 128] = taps[at * 3 + kz]


def fill_backward(packed, taps):
    for kx in range(3):
        for ky in range(3):
            for kz in range(3):
                at = kx * 3 + ky
                packed[kz * 128 : kz * 128 + 128, at * 128 : at * 128 + 128] = taps[26 - at * 3 - kz]


def dot_nn(left, right):
    return lax.dot_general(left, right, (((1,), (0,)), ((), ())), preferred_element_type=F32)


def dot_nt(left, right):
    return lax.dot_general(left, right, (((1,), (1,)), ((), ())), preferred_element_type=F32)


def dot_tn(left, right):
    return lax.dot_general(left, right, (((0,), (0,)), ((), ())), preferred_element_type=F32)


def forward_kernel(core, own, before, after, left, right, taps_one, taps_two,
                   field_keep, field_send, slope_one, slope_two, pooled,
                   padded, packed, act_one, halves):
    for at in range(2):
        padded[at] = left[at * 8 : at * 8 + 8]
        padded[6 + at] = right[at * 8 : at * 8 + 8]
    padded[2:6, 0:2] = before[0:4]
    padded[2:6, 2:6] = own[...]
    padded[2:6, 6:8] = after[0:4]
    fill_forward(packed, taps_one)
    first_core = core[0] == 0

    def first(step, _):
        product = dot_nn(window_rows(padded, step * 2, 6, rows=2), packed[...])
        act, slope = slope_and_silu(join_taps(product, 12, 64, 128))
        act = act.astype(BF16)
        for at in range(2):
            row = step * 2 + at
            part = act[6 * at : 6 * at + 6]
            field = padded[row + 1, 1:7]
            act_one[row] = part
            field_keep[row] = jnp.where(first_core, field, part)
            field_send[row] = jnp.where(first_core, part, field)

            @pl.when((row >= 1) & (row <= 4))
            def _():
                slope_one[row - 1] = slope[6 * at + 1 : 6 * at + 5].astype(BF16)

        return 0

    lax.fori_loop(0, 3, first, 0)
    fill_forward(packed, taps_two)

    def second(step, _):
        product = dot_nn(window_rows(act_one, step * 2, 4, rows=2), packed[...])
        act, slope = slope_and_silu(join_taps(product, 8, 64, 128))
        slope = slope.astype(BF16)
        act = act.astype(BF16).astype(F32)
        for at in range(2):
            row = step * 2 + at
            slope_two[row] = slope[4 * at : 4 * at + 4]
            halves[row] = act[4 * at : 4 * at + 4].reshape(2, 2, 64, 128).sum(axis=1)
        return 0

    lax.fori_loop(0, 2, second, 0)
    for at_x in range(2):
        for at_y in range(2):
            total = 0.0
            for part in range(2):
                for start in range(2):
                    total = total + halves[2 * at_x + part, at_y, pl.ds(start, 32, stride=2), :]
            pooled[at_x, at_y] = (total * 0.125).astype(BF16)


def interleave_kernel(core, mine, theirs, out):
    first_core = core[0] == 0

    def step(tap, _):
        own, other = mine[:, tap].astype(F32), theirs[:, tap].astype(F32)
        parts = [jnp.where(first_core, own, other), jnp.where(first_core, other, own)]
        parts = [p.reshape(16, 1, 8, 128) for p in parts]
        out[tap] = jnp.concatenate(parts, axis=1).reshape(256, 128).astype(BF16)
        return 0

    lax.fori_loop(0, 27, step, 0)


def bottom_kernel(own, before, after, left, right, g_own, f_before, f_after, f_left, f_right,
                  taps_three, slope_two, skip, bottleneck, bundle, err_two, err_first, err_last,
                  padded, grads, packed, errors, wide):
    fill_padded(padded, own, before, after, left, right)
    for half in range(2):
        rows, lanes = slice(half * 32, half * 32 + 32), slice(half * 128, half * 128 + 128)
        grads[0, :, :, lanes] = f_left[16:20, rows]
        grads[3, :, :, lanes] = f_right[16:20, rows]
        for at in range(2):
            grads[1 + at, 0, :, lanes] = f_before[4, at, rows]
            grads[1 + at, 3, :, lanes] = f_after[4, at, rows]
    grads[1:3, 1:3] = g_own[...]
    for at in range(9):
        for kz in range(3):
            packed[kz * 256 : kz * 256 + 256, at * 128 : at * 128 + 128] = taps_three[at * 3 + kz]
    product = dot_nt(window_rows(padded, 0, 4, rows=4), packed[...])
    acts, slopes = slope_and_silu(join_taps(product, 16, 32, 256))
    for row in range(4):
        columns = slice(4 * row, 4 * row + 4)
        if row in (1, 2):
            bottleneck[row - 1] = acts[columns][1:3].astype(BF16)
        errs = (grads[row].astype(F32) * slopes[columns]).astype(BF16)
        errors[row] = errs
        bundle[row * 4 : row * 4 + 4] = padded[row + 1, 1:5]
        if row in (1, 2):
            for at_y in range(2):
                for half in range(2):
                    at = 16 + ((row - 1) * 2 + at_y) * 2 + half
                    bundle[at] = errs[1 + at_y, :, half * 128 : half * 128 + 128]
    total = jnp.zeros((128, 384), F32)
    for kx in range(3):
        for ky in range(3):
            block = errors[kx : kx + 2, ky : ky + 2].reshape(128, 256)
            at = kx * 3 + ky
            back = jnp.concatenate([taps_three[26 - at * 3 - kz] for kz in range(3)], axis=1)
            total = total + dot_nn(block, back)
    upwards = join_taps(total, 4, 32, 128) * 0.125
    for row in range(2):
        upward = upwards[2 * row : 2 * row + 2]
        for at_y in range(2):
            wide[pl.ds(0, 32, stride=2), :] = upward[at_y]
            wide[pl.ds(1, 32, stride=2), :] = upward[at_y]
            for dx in range(2):
                for dy in range(2):
                    at = (2 * row + dx, 2 * at_y + dy)
                    err = skip[at].astype(F32) + wide[...]
                    err = (err * slope_two[at].astype(F32)).astype(BF16)
                    err_two[at] = err
                    if dy == at_y:
                        edge = err_first if at_y == 0 else err_last
                        edge[2 * row + dx, 0] = err


def tap_grads(fields, errors):
    spread = spread_errors(errors[...].reshape(16, 64, 128).astype(F32))
    return dot_tn(window_rows(fields, 0, 4, rows=4), spread)


def own_grads_kernel(fields, errors, total):
    total[...] = tap_grads(fields, errors)


def pair_grads_kernel(fields, errors, own_total, three, out, total):
    total[...] = own_total[...] + tap_grads(fields, errors)
    for at in range(9):
        for kz in range(3):
            start = (at * 3 + kz) * 128
            done = 0
            while done < 128:
                piece, row = divmod(start + done, PIECE)
                size = min(PIECE - row, 128 - done)
                rows = slice(at * 128 + done, at * 128 + done + size)
                out[piece, row : row + size] = total[rows, kz * 128 : kz * 128 + 128].astype(BF16)
                done += size
    out[61, 40:PIECE] = jnp.zeros((PIECE - 40, 128), BF16)
    out[62:64, 0:PIECE] = jnp.zeros((2, PIECE, 128), BF16)
    out[:, PIECE : 2 * PIECE] = three[...]


def bottom_grads_kernel(core, own, other, out, total):
    fields, errors = [], []
    for bundle in (own, other):
        for row in range(2):
            columns = []
            for kx in range(3):
                for ky in range(3):
                    at = (row + kx) * 4 + ky
                    columns.append(bundle[at : at + 2].reshape(64, 128))
            fields.append(jnp.concatenate(columns, axis=1))
            for at_y in range(2):
                at = 16 + row * 4 + 2 * at_y
                errors.append(jnp.concatenate([bundle[at], bundle[at + 1]], axis=1).reshape(1, 32, 256))
    errors = jnp.concatenate(errors, axis=0).astype(F32)
    total[...] = dot_tn(spread_errors(errors), jnp.concatenate(fields, axis=0))
    first_core = core[0] == 0
    out[48:64, 48:56] = jnp.zeros((16, 8, 128), BF16)
    for unit in range(27):
        at_x, rows = unit // 7, unit % 7 * 8
        at, kz = unit // 3, unit % 3
        block = total[kz * 256 : kz * 256 + 256, at * 128 : at * 128 + 128]
        block = block.reshape(16, 2, 8, 128)
        block = jnp.where(first_core, block[:, 0], block[:, 1]).astype(BF16)
        out[at_x * 16 : at_x * 16 + 16, rows : rows + 8] = block


def first_errors_kernel(core, own, before, after, left, right, taps_two, slope_one,
                        err_one, err_first, err_last, err_keep, err_send, padded, packed):
    fill_padded(padded, own, before, after, left, right)
    fill_backward(packed, taps_two)
    first_core = core[0] == 0

    def step(at, _):
        product = dot_nt(window_rows(padded, at * 2, 4, rows=2), packed[...])
        back = join_taps(product, 8, 64, 128)
        for half in range(2):
            row = at * 2 + half
            first = back[4 * half : 4 * half + 4] * slope_one[row].astype(F32)
            first, second = first.astype(BF16), own[row]
            err_one[row] = first
            err_first[row] = first[0:1]
            err_last[row] = first[3:4]
            err_keep[row] = jnp.where(first_core, first, second)
            err_send[row] = jnp.where(first_core, second, first)
        return 0

    lax.fori_loop(0, 2, step, 0)


def inner_input_kernel(own, before, after, taps_one, out, padded, packed):
    padded[:, 0:1] = before[...]
    padded[:, 1:5] = own[...]
    padded[:, 5:6] = after[...]
    fill_backward(packed, taps_one)
    product = dot_nt(window_rows(padded, 0, 4, rows=2), packed[...])
    out[...] = join_taps(product, 8, 64, 128).reshape(2, 4, 64, 128).astype(BF16)


def outer_input_kernel(own, before, after, left, right, taps_one, inner, out, padded, packed):
    fill_padded(padded, own, before, after, left, right)
    fill_backward(packed, taps_one)
    out[1:3] = inner[...]
    windows = [window_rows(padded, 0, 4), window_rows(padded, 3, 4)]
    product = dot_nt(jnp.concatenate(windows, axis=0), packed[...])
    rows = join_taps(product, 8, 64, 128).astype(BF16)
    out[0] = rows[0:4]
    out[3] = rows[4:8]


def sum_kernel(pieces, out, three):
    total = pieces[0].astype(F32)
    for at in range(1, 64):
        total = total + pieces[at].astype(F32)
    total = total.astype(BF16)
    three[...] = total[PIECE : 2 * PIECE]
    for at in range(64):
        out[at] = total[0:PIECE]


def place_kernel(chip, pair_0, pair_1, pair_2, pair_3, out, *, scale):
    for distance, pair in enumerate((pair_0, pair_1, pair_2, pair_3)):
        at = lax.rem(chip[0] + 4 - distance, 4)

        def put(rows, pair=pair, at=at):
            both = [pair[c, rows * 8 : rows * 8 + 8].astype(F32) * scale for c in range(2)]
            out[at * 7 + rows] = jnp.concatenate(both, axis=0)

        for rows in range(6):
            put(rows)
        pl.when(at < 3)(functools.partial(put, 6))


def finish_kernel(core, whole, other, grad_one, grad_two, *, scale):
    @pl.when(core[0] == 0)
    def _():
        grad_one[...] = whole[0:3456].astype(F32) * scale
        grad_two[...] = other[0:3456].astype(F32) * scale

    @pl.when(core[0] == 1)
    def _():
        grad_one[...] = other[0:3456].astype(F32) * scale
        grad_two[...] = whole[0:3456].astype(F32) * scale


def in_hbm(array):
    return pltpu.with_memory_space_constraint(array, pltpu.HBM)


def call(kernel, out_shapes, scratch, flops, *operands):
    shapes = [pltpu.HBM(*s[:2]) if s[2:] else jax.ShapeDtypeStruct(*s) for s in out_shapes]
    moved = sum(o.size * o.dtype.itemsize for o in operands)
    return pl.pallas_call(
        kernel,
        out_shape=shapes,
        in_specs=[
            pl.BlockSpec(memory_space=pltpu.SMEM if o.dtype == jnp.int32 else pltpu.VMEM) for o in operands
        ],
        out_specs=[pl.BlockSpec(memory_space=pltpu.VMEM)] * len(shapes),
        scratch_shapes=[pltpu.VMEM(s, d) for s, d in scratch],
        compiler_params=pltpu.CompilerParams(vmem_limit_bytes=18 << 20),
        cost_estimate=pl.CostEstimate(flops=flops // 20, bytes_accessed=moved // 20, transcendentals=0),
        name=kernel.__name__,
    )(*operands)


def on_device(features, skip_grad, bottom_grad, conv_one, conv_two, conv_three):
    core = lax.axis_index("c")
    first, last = call(
        first_edge_kernel, [((5, 2, 64, 128), BF16)] * 2, [], 0, in_hbm(features), in_hbm(bottom_grad)
    )
    first, last, first_core, core_ref, chip = lax.optimization_barrier(
        (first, last, core == 0, core.reshape(1), lax.axis_index("x").reshape(1))
    )
    fine_cells = features.size // 128 * lax.axis_size(GX) * lax.axis_size(GY)
    fine_scale = 1.0 / math.sqrt(fine_cells)
    coarse_scale = 1.0 / math.sqrt(fine_cells // 8)
    taps_one = conv_one.reshape(27, 128, 128)
    taps_two = conv_two.reshape(27, 128, 128)
    half_taps = jnp.swapaxes(conv_three.reshape(27, 128, 16), 1, 2).reshape(27, 2, 8, 128)
    half_taps = jnp.where(first_core, half_taps[:, 0], half_taps[:, 1])
    mine = lax.all_to_all(jnp.broadcast_to(half_taps, (16, 27, 8, 128)), GY, 0, 0)

    f_before, f_after = shifted(last, GY, 1), shifted(first, GY, -1)
    low, high = call(
        first_slab_kernel, [((20, 64, 128), BF16)] * 2, [], 4 * 10**11,
        features, f_before, f_after, bottom_grad,
    )
    f_left, f_right = exchange_x(low, high)

    conv_flops = 2 * 1152 * 128 * 1024 * 3
    field = (6, 6, 64, 128)
    block = (4, 4, 64, 128)
    edge = (4, 1, 64, 128)
    field_keep, field_send, slope_one, slope_two, pooled = call(
        forward_kernel,
        [(field, BF16, True), (field, BF16, True), (block, BF16, True), (block, BF16, True), ((2, 2, 32, 128), BF16, True)],
        [((8, 8, 64, 128), BF16), ((1152, 384), BF16), (field, BF16), ((4, 2, 64, 128), F32)],
        3 * conv_flops, core_ref, features, f_before, f_after, f_left, f_right, taps_one, taps_two,
    )
    field_other = swap_cores(field_send)
    mine, pooled = lax.optimization_barrier((mine, pooled))
    theirs = swap_cores(mine)
    (taps_three,) = call(interleave_kernel, [((27, 256, 128), BF16)], [], 0, core_ref, mine, theirs)
    p_before, p_after = shifted(pooled, GY, 1), shifted(pooled, GY, -1)
    low, high = call(slab_kernel, [((2, 6, 32, 128), BF16)] * 2, [], 0, in_hbm(pooled), p_before, p_after)
    p_pieces = pooled, p_before, p_after, *exchange_x(low, high)
    bottleneck, bundle, err_two, err_first, err_last = call(
        bottom_kernel,
        [((2, 2, 32, 256), BF16, True), ((24, 32, 128), BF16), (block, BF16), (edge, BF16), (edge, BF16)],
        [((6, 6, 32, 128), BF16), ((4, 4, 32, 256), BF16), ((768, 1152), BF16),
         ((4, 4, 32, 256), BF16), ((64, 128), F32)],
        conv_flops, *p_pieces, bottom_grad, f_before, f_after, f_left, f_right,
        taps_three, in_hbm(slope_two), in_hbm(skip_grad),
    )
    e_before, e_after = shifted(err_last, GY, 1), shifted(err_first, GY, -1)
    low, high = call(slab_kernel, [((1, 6, 64, 128), BF16)] * 2, [], 0, err_two, e_before, e_after)
    bundle, low, high = lax.optimization_barrier((bundle, low, high))
    e_left, e_right = exchange_x(low, high)
    (three,) = call(
        bottom_grads_kernel, [((64, PIECE, 128), BF16)], [((768, 1152), F32)],
        conv_flops // 2, core_ref, bundle, swap_cores(bundle),
    )
    three, e_left, e_right = lax.optimization_barrier((three, e_left, e_right))
    err_one, one_first, one_last, err_keep, err_send = call(
        first_errors_kernel,
        [(block, BF16, True), (edge, BF16, True), (edge, BF16, True), (block, BF16), (block, BF16)],
        [(field, BF16), ((384, 1152), BF16)],
        conv_flops, core_ref, err_two, e_before, e_after, e_left, e_right, taps_two, slope_one,
    )
    err_other = swap_cores(err_send)
    (total,) = call(own_grads_kernel, [((1152, 384), F32)], [], conv_flops, field_keep, err_keep)
    (kept,) = call(
        pair_grads_kernel, [((64, 2 * PIECE, 128), BF16, True)], [((1152, 384), F32)],
        conv_flops, field_other, err_other, total, three,
    )
    kept, one_first, one_last = lax.optimization_barrier((kept, one_first, one_last))
    one_before, one_after = shifted(one_last, GY, 1), shifted(one_first, GY, -1)
    part, three_part = call(
        sum_kernel, [((64, PIECE, 128), BF16, True), ((PIECE, 128), BF16)], [], 0,
        lax.all_to_all(kept, FLAT, 0, 0),
    )
    part, one_before, one_after = lax.optimization_barrier((part, one_before, one_after))
    low, high = call(slab_kernel, [((1, 6, 64, 128), BF16)] * 2, [], 0, err_one, one_before, one_after)
    one_left, one_right = exchange_x(low, high)
    whole = lax.all_to_all(part, FLAT, 0, 0).reshape(64 * PIECE, 128)
    both = swap_cores(three_part)
    both = jnp.where(first_core, jnp.stack([three_part, both]), jnp.stack([both, three_part]))
    grad_three = pl.pallas_call(
        functools.partial(place_kernel, scale=coarse_scale),
        out_shape=jax.ShapeDtypeStruct((27, 16, 128), F32),
        in_specs=[pl.BlockSpec(memory_space=pltpu.SMEM)] + [pl.BlockSpec(memory_space=pltpu.VMEM)] * 4,
        out_specs=pl.BlockSpec(memory_space=pltpu.VMEM),
        compiler_params=pltpu.CompilerParams(vmem_limit_bytes=8 << 20),
        name="place_kernel",
    )(chip, *ring_pieces([both] * 4, "x"))
    (inner,) = call(
        inner_input_kernel, [((2, 4, 64, 128), BF16, True)], [((4, 6, 64, 128), BF16), ((384, 1152), BF16)],
        conv_flops // 4, err_one, one_before, one_after, taps_one,
    )
    whole, grad_three, one_left, one_right, inner = lax.optimization_barrier(
        (whole, grad_three, one_left, one_right, inner)
    )
    (input_grad,) = call(
        outer_input_kernel, [(block, BF16, True)], [(field, BF16), ((384, 1152), BF16)],
        conv_flops // 4, in_hbm(err_one), in_hbm(one_before), in_hbm(one_after), one_left, one_right,
        in_hbm(taps_one), in_hbm(inner),
    )
    grad_three = jnp.swapaxes(grad_three, 1, 2).reshape(3, 3, 3, 128, 16)
    grad_one, grad_two = pl.pallas_call(
        functools.partial(finish_kernel, scale=fine_scale),
        out_shape=[jax.ShapeDtypeStruct((3456, 128), F32)] * 2,
        in_specs=[pl.BlockSpec(memory_space=pltpu.SMEM)] + [pl.BlockSpec(memory_space=pltpu.VMEM)] * 2,
        out_specs=[pl.BlockSpec(memory_space=pltpu.VMEM)] * 2,
        compiler_params=pltpu.CompilerParams(vmem_limit_bytes=8 << 20),
        name="finish_kernel",
    )(core_ref, whole, swap_cores(whole))
    grad_one = grad_one.reshape(3, 3, 3, 128, 128)
    grad_two = grad_two.reshape(3, 3, 3, 128, 128)
    return (bottleneck, input_grad, grad_one, grad_two, grad_three)


def solution(mesh):
    fine = Mesh(mesh.devices.reshape(4, 2, 4, 4), ("x", "c", "z", "y"))
    cells = P(GX, GY, None, None)
    outs = P(None, None, None, None, GY)
    return jax.shard_map(
        on_device,
        mesh=fine,
        in_specs=(cells, cells, cells, P(), P(), outs),
        out_specs=(cells, cells, P(), P(), outs),
        check_vma=False,
    )
```

```python
import functools
import math

import jax
import jax.numpy as jnp
from jax import lax
from jax.experimental import pallas as pl
from jax.experimental.pallas import tpu as pltpu
from jax.sharding import Mesh
from jax.sharding import PartitionSpec as P

GX = ("x", "c")
GY = ("z", "y")
FLAT = ("x", "z", "y")
F32 = jnp.float32
BF16 = jnp.bfloat16
PIECE = 56


def shifted(array, axes, step):
    count = lax.axis_size(axes)
    return lax.ppermute(array, axes, [(i, (i + step) % count) for i in range(count)])


def swap_cores(array):
    return lax.ppermute(array, "c", [(0, 1), (1, 0)])


def ring_pieces(pieces, axis):
    sent = [lax.ppermute(pieces[d], axis, [(i, (i + d) % 4) for i in range(4)]) for d in (1, 2, 3)]
    return [pieces[0]] + sent


def slab_kernel(own, before, after, low, high):
    width, size_x = low.shape[0], own.shape[0]
    for slab, start in ((low, 0), (high, size_x - width)):
        rows = slice(start, start + width)
        columns = 0
        for part in (before, own, after):
            slab[:, columns : columns + part.shape[1]] = part[rows]
            columns += part.shape[1]


def first_edge_kernel(own, grads, first, last):
    for edge, start in ((first, 0), (last, 1)):
        edge[0:4] = own[:, 2 * start : 2 * start + 2]
        for half in range(2):
            edge[4, :, half * 32 : half * 32 + 32] = grads[:, start, :, half * 128 : half * 128 + 128]


def first_slab_kernel(own, before, after, grads, low, high):
    for slab, start, row in ((low, 0, 0), (high, 2, 1)):
        for at in range(2):
            slab[at * 8 : at * 8 + 2] = before[start + at]
            slab[at * 8 + 2 : at * 8 + 6] = own[start + at]
            slab[at * 8 + 6 : at * 8 + 8] = after[start + at]
        slab[16] = before[4, row]
        slab[19] = after[4, row]
        for at_y in range(2):
            for half in range(2):
                part = grads[row, at_y, :, half * 128 : half * 128 + 128]
                slab[17 + at_y, half * 32 : half * 32 + 32] = part


def exchange_x(low, high):
    return shifted(high, GX, 1), shifted(low, GX, -1)


def halo_pieces(own, width, first, last):
    before, after = shifted(last, GY, 1), shifted(first, GY, -1)
    size_x, size_y, size_z, chans = own.shape
    slab = (width, size_y + 2 * width, size_z, chans)
    low, high = call(slab_kernel, [(slab, BF16)] * 2, [], 0, own, before, after)
    return own, before, after, *exchange_x(low, high)


def fill_padded(padded, own, before, after, left, right):
    size_x, size_y = own.shape[0], own.shape[1]
    width = left.shape[0]
    padded[0:width] = left[...]
    padded[width + size_x : 2 * width + size_x] = right[...]
    middle = slice(width, width + size_x)
    padded[middle, 0:width] = before[...]
    padded[middle, width : width + size_y] = own[...]
    padded[middle, width + size_y : 2 * width + size_y] = after[...]


def slope_and_silu(values):
    sigma = 1.0 / (1.0 + jnp.exp(-values))
    return values * sigma, sigma * (1.0 + values * (1.0 - sigma))


def window_rows(source, row, count, skip=0, rows=1):
    pieces = []
    for kx in range(3):
        for ky in range(3):
            block = source[pl.ds(row + kx + skip, rows), ky + skip : ky + skip + count]
            pieces.append(block.reshape(rows * block.shape[1] * block.shape[2], block.shape[3]))
    return jnp.concatenate(pieces, axis=1)


def roll_z(values, step):
    return pltpu.roll(values, step % values.shape[1], 1)


def join_taps(product, count, size_z, chans):
    parts = product.reshape(count, size_z, 3 * chans)
    return (
        roll_z(parts[:, :, 0:chans], 1)
        + parts[:, :, chans : 2 * chans]
        + roll_z(parts[:, :, 2 * chans : 3 * chans], -1)
    )


def spread_errors(errors):
    count, size_z, chans = errors.shape
    parts = [roll_z(errors, -1), errors, roll_z(errors, 1)]
    return jnp.concatenate([p.reshape(count * size_z, chans) for p in parts], axis=1).astype(BF16)


def fill_forward(packed, taps):
    for kx in range(3):
        for ky in range(3):
            for kz in range(3):
                at = kx * 3 + ky
                packed[at * 128 : at * 128 + 128, kz * 128 : kz * 128 + 128] = taps[at * 3 + kz]


def fill_backward(packed, taps):
    for kx in range(3):
        for ky in range(3):
            for kz in range(3):
                at = kx * 3 + ky
                packed[kz * 128 : kz * 128 + 128, at * 128 : at * 128 + 128] = taps[26 - at * 3 - kz]


def dot_nn(left, right):
    return lax.dot_general(left, right, (((1,), (0,)), ((), ())), preferred_element_type=F32)


def dot_nt(left, right):
    return lax.dot_general(left, right, (((1,), (1,)), ((), ())), preferred_element_type=F32)


def dot_tn(left, right):
    return lax.dot_general(left, right, (((0,), (0,)), ((), ())), preferred_element_type=F32)


def forward_kernel(core, own, before, after, left, right, taps_one, taps_two,
                   field_keep, field_send, slope_one, slope_two, pooled,
                   padded, packed, act_one, halves):
    for at in range(2):
        padded[at] = left[at * 8 : at * 8 + 8]
        padded[6 + at] = right[at * 8 : at * 8 + 8]
    padded[2:6, 0:2] = before[0:4]
    padded[2:6, 2:6] = own[...]
    padded[2:6, 6:8] = after[0:4]
    fill_forward(packed, taps_one)
    first_core = core[0] == 0

    def first(step, _):
        product = dot_nn(window_rows(padded, step * 2, 6, rows=2), packed[...])
        act, slope = slope_and_silu(join_taps(product, 12, 64, 128))
        act = act.astype(BF16)
        for at in range(2):
            row = step * 2 + at
            part = act[6 * at : 6 * at + 6]
            field = padded[row + 1, 1:7]
            act_one[row] = part
            field_keep[row] = jnp.where(first_core, field, part)
            field_send[row] = jnp.where(first_core, part, field)

            @pl.when((row >= 1) & (row <= 4))
            def _():
                slope_one[row - 1] = slope[6 * at + 1 : 6 * at + 5].astype(BF16)

        return 0

    lax.fori_loop(0, 3, first, 0)
    fill_forward(packed, taps_two)

    def second(step, _):
        product = dot_nn(window_rows(act_one, step * 2, 4, rows=2), packed[...])
        act, slope = slope_and_silu(join_taps(product, 8, 64, 128))
        slope = slope.astype(BF16)
        act = act.astype(BF16).astype(F32)
        for at in range(2):
            row = step * 2 + at
            slope_two[row] = slope[4 * at : 4 * at + 4]
            halves[row] = act[4 * at : 4 * at + 4].reshape(2, 2, 64, 128).sum(axis=1)
        return 0

    lax.fori_loop(0, 2, second, 0)
    for at_x in range(2):
        for at_y in range(2):
            total = 0.0
            for part in range(2):
                for start in range(2):
                    total = total + halves[2 * at_x + part, at_y, pl.ds(start, 32, stride=2), :]
            pooled[at_x, at_y] = (total * 0.125).astype(BF16)


def interleave_kernel(core, mine, theirs, out):
    first_core = core[0] == 0

    def step(tap, _):
        own, other = mine[:, tap].astype(F32), theirs[:, tap].astype(F32)
        parts = [jnp.where(first_core, own, other), jnp.where(first_core, other, own)]
        parts = [p.reshape(16, 1, 8, 128) for p in parts]
        out[tap] = jnp.concatenate(parts, axis=1).reshape(256, 128).astype(BF16)
        return 0

    lax.fori_loop(0, 27, step, 0)


def bottom_kernel(own, before, after, left, right, g_own, f_before, f_after, f_left, f_right,
                  taps_three, slope_two, skip, bottleneck, bundle, err_two, err_first, err_last,
                  padded, grads, packed, errors, wide):
    fill_padded(padded, own, before, after, left, right)
    for half in range(2):
        rows, lanes = slice(half * 32, half * 32 + 32), slice(half * 128, half * 128 + 128)
        grads[0, :, :, lanes] = f_left[16:20, rows]
        grads[3, :, :, lanes] = f_right[16:20, rows]
        for at in range(2):
            grads[1 + at, 0, :, lanes] = f_before[4, at, rows]
            grads[1 + at, 3, :, lanes] = f_after[4, at, rows]
    grads[1:3, 1:3] = g_own[...]
    for at in range(9):
        for kz in range(3):
            packed[kz * 256 : kz * 256 + 256, at * 128 : at * 128 + 128] = taps_three[at * 3 + kz]
    product = dot_nt(window_rows(padded, 0, 4, rows=4), packed[...])
    acts, slopes = slope_and_silu(join_taps(product, 16, 32, 256))
    for row in range(4):
        columns = slice(4 * row, 4 * row + 4)
        if row in (1, 2):
            bottleneck[row - 1] = acts[columns][1:3].astype(BF16)
        errs = (grads[row].astype(F32) * slopes[columns]).astype(BF16)
        errors[row] = errs
        bundle[row * 4 : row * 4 + 4] = padded[row + 1, 1:5]
        if row in (1, 2):
            for at_y in range(2):
                for half in range(2):
                    at = 16 + ((row - 1) * 2 + at_y) * 2 + half
                    bundle[at] = errs[1 + at_y, :, half * 128 : half * 128 + 128]
    total = jnp.zeros((128, 384), F32)
    for kx in range(3):
        for ky in range(3):
            block = errors[kx : kx + 2, ky : ky + 2].reshape(128, 256)
            at = kx * 3 + ky
            back = jnp.concatenate([taps_three[26 - at * 3 - kz] for kz in range(3)], axis=1)
            total = total + dot_nn(block, back)
    upwards = join_taps(total, 4, 32, 128) * 0.125
    for row in range(2):
        upward = upwards[2 * row : 2 * row + 2]
        for at_y in range(2):
            wide[pl.ds(0, 32, stride=2), :] = upward[at_y]
            wide[pl.ds(1, 32, stride=2), :] = upward[at_y]
            for dx in range(2):
                for dy in range(2):
                    at = (2 * row + dx, 2 * at_y + dy)
                    err = skip[at].astype(F32) + wide[...]
                    err = (err * slope_two[at].astype(F32)).astype(BF16)
                    err_two[at] = err
                    if dy == at_y:
                        edge = err_first if at_y == 0 else err_last
                        edge[2 * row + dx, 0] = err


def tap_grads(fields, errors):
    spread = spread_errors(errors[...].reshape(16, 64, 128).astype(F32))
    return dot_tn(window_rows(fields, 0, 4, rows=4), spread)


def own_grads_kernel(fields, errors, total):
    total[...] = tap_grads(fields, errors)


def pair_grads_kernel(fields, errors, own_total, three, out, total):
    total[...] = own_total[...] + tap_grads(fields, errors)
    for at in range(9):
        for kz in range(3):
            start = (at * 3 + kz) * 128
            done = 0
            while done < 128:
                piece, row = divmod(start + done, PIECE)
                size = min(PIECE - row, 128 - done)
                rows = slice(at * 128 + done, at * 128 + done + size)
                out[piece, row : row + size] = total[rows, kz * 128 : kz * 128 + 128].astype(BF16)
                done += size
    out[61, 40:PIECE] = jnp.zeros((PIECE - 40, 128), BF16)
    out[62:64, 0:PIECE] = jnp.zeros((2, PIECE, 128), BF16)
    out[:, PIECE : 2 * PIECE] = three[...]


def bottom_grads_kernel(core, own, other, out, total):
    fields, errors = [], []
    for bundle in (own, other):
        for row in range(2):
            columns = []
            for kx in range(3):
                for ky in range(3):
                    at = (row + kx) * 4 + ky
                    columns.append(bundle[at : at + 2].reshape(64, 128))
            fields.append(jnp.concatenate(columns, axis=1))
            for at_y in range(2):
                at = 16 + row * 4 + 2 * at_y
                errors.append(jnp.concatenate([bundle[at], bundle[at + 1]], axis=1).reshape(1, 32, 256))
    errors = jnp.concatenate(errors, axis=0).astype(F32)
    total[...] = dot_tn(spread_errors(errors), jnp.concatenate(fields, axis=0))
    first_core = core[0] == 0
    out[48:64, 48:56] = jnp.zeros((16, 8, 128), BF16)
    for unit in range(27):
        at_x, rows = unit // 7, unit % 7 * 8
        at, kz = unit // 3, unit % 3
        block = total[kz * 256 : kz * 256 + 256, at * 128 : at * 128 + 128]
        block = block.reshape(16, 2, 8, 128)
        block = jnp.where(first_core, block[:, 0], block[:, 1]).astype(BF16)
        out[at_x * 16 : at_x * 16 + 16, rows : rows + 8] = block


def first_errors_kernel(core, own, before, after, left, right, taps_two, slope_one,
                        err_one, err_first, err_last, err_keep, err_send, padded, packed):
    fill_padded(padded, own, before, after, left, right)
    fill_backward(packed, taps_two)
    first_core = core[0] == 0

    def step(at, _):
        product = dot_nt(window_rows(padded, at * 2, 4, rows=2), packed[...])
        back = join_taps(product, 8, 64, 128)
        for half in range(2):
            row = at * 2 + half
            first = back[4 * half : 4 * half + 4] * slope_one[row].astype(F32)
            first, second = first.astype(BF16), own[row]
            err_one[row] = first
            err_first[row] = first[0:1]
            err_last[row] = first[3:4]
            err_keep[row] = jnp.where(first_core, first, second)
            err_send[row] = jnp.where(first_core, second, first)
        return 0

    lax.fori_loop(0, 2, step, 0)


def inner_input_kernel(own, before, after, taps_one, out, padded, packed):
    padded[:, 0:1] = before[...]
    padded[:, 1:5] = own[...]
    padded[:, 5:6] = after[...]
    fill_backward(packed, taps_one)
    product = dot_nt(window_rows(padded, 0, 4, rows=2), packed[...])
    out[...] = join_taps(product, 8, 64, 128).reshape(2, 4, 64, 128).astype(BF16)


def outer_input_kernel(own, before, after, left, right, taps_one, inner, out, padded, packed):
    fill_padded(padded, own, before, after, left, right)
    fill_backward(packed, taps_one)
    out[1:3] = inner[...]
    windows = [window_rows(padded, 0, 4), window_rows(padded, 3, 4)]
    product = dot_nt(jnp.concatenate(windows, axis=0), packed[...])
    rows = join_taps(product, 8, 64, 128).astype(BF16)
    out[0] = rows[0:4]
    out[3] = rows[4:8]


def sum_kernel(pieces, out, three):
    total = pieces[0].astype(F32)
    for at in range(1, 64):
        total = total + pieces[at].astype(F32)
    total = total.astype(BF16)
    three[...] = total[PIECE : 2 * PIECE]
    for at in range(64):
        out[at] = total[0:PIECE]


def place_kernel(chip, pair_0, pair_1, pair_2, pair_3, out, *, scale):
    for distance, pair in enumerate((pair_0, pair_1, pair_2, pair_3)):
        at = lax.rem(chip[0] + 4 - distance, 4)

        def put(rows, pair=pair, at=at):
            both = [pair[c, rows * 8 : rows * 8 + 8].astype(F32) * scale for c in range(2)]
            out[at * 7 + rows] = jnp.concatenate(both, axis=0)

        for rows in range(6):
            put(rows)
        pl.when(at < 3)(functools.partial(put, 6))


def finish_kernel(core, whole, other, grad_one, grad_two, *, scale):
    @pl.when(core[0] == 0)
    def _():
        grad_one[...] = whole[0:3456].astype(F32) * scale
        grad_two[...] = other[0:3456].astype(F32) * scale

    @pl.when(core[0] == 1)
    def _():
        grad_one[...] = other[0:3456].astype(F32) * scale
        grad_two[...] = whole[0:3456].astype(F32) * scale


def in_hbm(array):
    return pltpu.with_memory_space_constraint(array, pltpu.HBM)


def call(kernel, out_shapes, scratch, flops, *operands):
    shapes = [pltpu.HBM(*s[:2]) if s[2:] else jax.ShapeDtypeStruct(*s) for s in out_shapes]
    moved = sum(o.size * o.dtype.itemsize for o in operands)
    return pl.pallas_call(
        kernel,
        out_shape=shapes,
        in_specs=[
            pl.BlockSpec(memory_space=pltpu.SMEM if o.dtype == jnp.int32 else pltpu.VMEM) for o in operands
        ],
        out_specs=[pl.BlockSpec(memory_space=pltpu.VMEM)] * len(shapes),
        scratch_shapes=[pltpu.VMEM(s, d) for s, d in scratch],
        compiler_params=pltpu.CompilerParams(vmem_limit_bytes=18 << 20),
        cost_estimate=pl.CostEstimate(flops=flops // 20, bytes_accessed=moved // 20, transcendentals=0),
        name=kernel.__name__,
    )(*operands)


def on_device(features, skip_grad, bottom_grad, conv_one, conv_two, conv_three):
    core = lax.axis_index("c")
    first, last = call(
        first_edge_kernel, [((5, 2, 64, 128), BF16)] * 2, [], 0, in_hbm(features), in_hbm(bottom_grad)
    )
    first, last, first_core, core_ref, chip = lax.optimization_barrier(
        (first, last, core == 0, core.reshape(1), lax.axis_index("x").reshape(1))
    )
    fine_cells = features.size // 128 * lax.axis_size(GX) * lax.axis_size(GY)
    fine_scale = 1.0 / math.sqrt(fine_cells)
    coarse_scale = 1.0 / math.sqrt(fine_cells // 8)
    taps_one = conv_one.reshape(27, 128, 128)
    taps_two = conv_two.reshape(27, 128, 128)
    half_taps = jnp.swapaxes(conv_three.reshape(27, 128, 16), 1, 2).reshape(27, 2, 8, 128)
    half_taps = jnp.where(first_core, half_taps[:, 0], half_taps[:, 1])
    mine = lax.all_to_all(jnp.broadcast_to(half_taps, (16, 27, 8, 128)), GY, 0, 0)

    f_before, f_after = shifted(last, GY, 1), shifted(first, GY, -1)
    low, high = call(
        first_slab_kernel, [((20, 64, 128), BF16)] * 2, [], 4 * 10**11,
        features, f_before, f_after, bottom_grad,
    )
    f_left, f_right = exchange_x(low, high)

    conv_flops = 2 * 1152 * 128 * 1024 * 3
    field = (6, 6, 64, 128)
    block = (4, 4, 64, 128)
    edge = (4, 1, 64, 128)
    field_keep, field_send, slope_one, slope_two, pooled = call(
        forward_kernel,
        [(field, BF16, True), (field, BF16, True), (block, BF16, True), (block, BF16, True), ((2, 2, 32, 128), BF16)],
        [((8, 8, 64, 128), BF16), ((1152, 384), BF16), (field, BF16), ((4, 2, 64, 128), F32)],
        3 * conv_flops, core_ref, features, f_before, f_after, f_left, f_right, taps_one, taps_two,
    )
    field_other = swap_cores(field_send)
    mine, pooled = lax.optimization_barrier((mine, pooled))
    theirs = swap_cores(mine)
    (taps_three,) = call(interleave_kernel, [((27, 256, 128), BF16)], [], 0, core_ref, mine, theirs)
    p_pieces = halo_pieces(pooled, 2, pooled, pooled)
    bottleneck, bundle, err_two, err_first, err_last = call(
        bottom_kernel,
        [((2, 2, 32, 256), BF16, True), ((24, 32, 128), BF16), (block, BF16), (edge, BF16), (edge, BF16)],
        [((6, 6, 32, 128), BF16), ((4, 4, 32, 256), BF16), ((768, 1152), BF16),
         ((4, 4, 32, 256), BF16), ((64, 128), F32)],
        conv_flops, *p_pieces, bottom_grad, f_before, f_after, f_left, f_right,
        taps_three, in_hbm(slope_two), in_hbm(skip_grad),
    )
    e_before, e_after = shifted(err_last, GY, 1), shifted(err_first, GY, -1)
    low, high = call(slab_kernel, [((1, 6, 64, 128), BF16)] * 2, [], 0, err_two, e_before, e_after)
    bundle, low, high = lax.optimization_barrier((bundle, low, high))
    e_left, e_right = exchange_x(low, high)
    (three,) = call(
        bottom_grads_kernel, [((64, PIECE, 128), BF16)], [((768, 1152), F32)],
        conv_flops // 2, core_ref, bundle, swap_cores(bundle),
    )
    three, e_left, e_right = lax.optimization_barrier((three, e_left, e_right))
    err_one, one_first, one_last, err_keep, err_send = call(
        first_errors_kernel,
        [(block, BF16, True), (edge, BF16, True), (edge, BF16, True), (block, BF16), (block, BF16)],
        [(field, BF16), ((384, 1152), BF16)],
        conv_flops, core_ref, err_two, e_before, e_after, e_left, e_right, taps_two, slope_one,
    )
    err_other = swap_cores(err_send)
    (total,) = call(own_grads_kernel, [((1152, 384), F32)], [], conv_flops, field_keep, err_keep)
    (kept,) = call(
        pair_grads_kernel, [((64, 2 * PIECE, 128), BF16, True)], [((1152, 384), F32)],
        conv_flops, field_other, err_other, total, three,
    )
    kept, one_first, one_last = lax.optimization_barrier((kept, one_first, one_last))
    one_before, one_after = shifted(one_last, GY, 1), shifted(one_first, GY, -1)
    part, three_part = call(
        sum_kernel, [((64, PIECE, 128), BF16, True), ((PIECE, 128), BF16)], [], 0,
        lax.all_to_all(kept, FLAT, 0, 0),
    )
    part, one_before, one_after = lax.optimization_barrier((part, one_before, one_after))
    low, high = call(slab_kernel, [((1, 6, 64, 128), BF16)] * 2, [], 0, err_one, one_before, one_after)
    one_left, one_right = exchange_x(low, high)
    whole = lax.all_to_all(part, FLAT, 0, 0).reshape(64 * PIECE, 128)
    both = swap_cores(three_part)
    both = jnp.where(first_core, jnp.stack([three_part, both]), jnp.stack([both, three_part]))
    grad_three = pl.pallas_call(
        functools.partial(place_kernel, scale=coarse_scale),
        out_shape=jax.ShapeDtypeStruct((27, 16, 128), F32),
        in_specs=[pl.BlockSpec(memory_space=pltpu.SMEM)] + [pl.BlockSpec(memory_space=pltpu.VMEM)] * 4,
        out_specs=pl.BlockSpec(memory_space=pltpu.VMEM),
        compiler_params=pltpu.CompilerParams(vmem_limit_bytes=8 << 20),
        name="place_kernel",
    )(chip, *ring_pieces([both] * 4, "x"))
    (inner,) = call(
        inner_input_kernel, [((2, 4, 64, 128), BF16, True)], [((4, 6, 64, 128), BF16), ((384, 1152), BF16)],
        conv_flops // 4, err_one, one_before, one_after, taps_one,
    )
    whole, grad_three, one_left, one_right, inner = lax.optimization_barrier(
        (whole, grad_three, one_left, one_right, inner)
    )
    (input_grad,) = call(
        outer_input_kernel, [(block, BF16, True)], [(field, BF16), ((384, 1152), BF16)],
        conv_flops // 4, in_hbm(err_one), in_hbm(one_before), in_hbm(one_after), one_left, one_right,
        in_hbm(taps_one), in_hbm(inner),
    )
    grad_three = jnp.swapaxes(grad_three, 1, 2).reshape(3, 3, 3, 128, 16)
    grad_one, grad_two = pl.pallas_call(
        functools.partial(finish_kernel, scale=fine_scale),
        out_shape=[jax.ShapeDtypeStruct((3456, 128), F32)] * 2,
        in_specs=[pl.BlockSpec(memory_space=pltpu.SMEM)] + [pl.BlockSpec(memory_space=pltpu.VMEM)] * 2,
        out_specs=[pl.BlockSpec(memory_space=pltpu.VMEM)] * 2,
        compiler_params=pltpu.CompilerParams(vmem_limit_bytes=8 << 20),
        name="finish_kernel",
    )(core_ref, whole, swap_cores(whole))
    grad_one = grad_one.reshape(3, 3, 3, 128, 128)
    grad_two = grad_two.reshape(3, 3, 3, 128, 128)
    return (bottleneck, input_grad, grad_one, grad_two, grad_three)


def solution(mesh):
    fine = Mesh(mesh.devices.reshape(4, 2, 4, 4), ("x", "c", "z", "y"))
    cells = P(GX, GY, None, None)
    outs = P(None, None, None, None, GY)
    return jax.shard_map(
        on_device,
        mesh=fine,
        in_specs=(cells, cells, cells, P(), P(), outs),
        out_specs=(cells, cells, P(), P(), outs),
        check_vma=False,
    )
```
